128 devices in a mesh: tm: 16 (over x, y), sector: 8 (over z, core).
Axes of the slice: x: 4, y: 4, z: 4, core: 2. Of those that a mesh axis runs over, the one named last changes fastest.
Arguments:
- propagator: bfloat16 [8, 16, 640, 640], P('sector', 'tm'), may hold values from -6 to 6
- rising_op: bfloat16 [8, 640, 640], P('sector'), may hold values from -0.25 to 0.25
- energies: float32 [8, 640], P('sector'), may hold values from 0.5 to 40
- hyb_particle: float32 [16], P('tm'), may hold values from 0.2 to 1
- hyb_hole: float32 [16], P('tm'), may hold values from 0.2 to 1
- sector_sizes: int32 [8], P('sector'), may hold values from 160 to 640, as said below
Outputs:
- new_prop: bfloat16 [8, 16, 640, 640], P('sector', 'tm')
The draws below stay inside these ranges and needn't reach their ends.
Inputs may be any that keep to these rules, and one draw needn't show every extreme that they name: `sector_sizes`: one sector holds exactly 640 states.
All inputs are finite; a program needn't handle non-finite values.
Results may differ from the reference program's by a relative error of at most 0.0061.
Values may be sent and summed in bfloat16 or wider, within the bound.
No kernel may reach another device: no remote copies, remote signals or barrier semaphores. Data moves between devices by JAX's collectives and lax.ppermute only.
A program may use at most 128 MiB of HBM per device.

```python
import math
import jax
import jax.numpy as jnp
from jax import lax

B = 640
SECT = 8
TIMES = 16


def draw_sector_sizes(key, part):
    first_key = jax.random.fold_in(key, 11)
    second_key = jax.random.fold_in(key, 12)
    counts_drawn = jax.random.randint(first_key, (SECT,), B // 4, B + 1)
    chosen = jax.random.randint(second_key, (), 0, SECT)
    return jnp.where(jnp.arange(SECT) == chosen, B, counts_drawn).astype(jnp.int32)


def levels(key, shape, split, low, high):
    def one(position, parts):
        draws = jax.random.uniform(jax.random.fold_in(jax.random.fold_in(key, 6), position), (parts,), jnp.float32, low / len(split), high / len(split))
        return jnp.repeat(jnp.exp(draws), shape[position] // parts).reshape((-1,) + (1,) * (len(shape) - position - 1))

    level = one(*split[0])
    for cut in split[1:]:
        level = level * one(*cut)
    return level


def centred(stream_key, shape, deviation, reach, shards=(), kind=jnp.bfloat16):
    result = jax.random.normal(stream_key, shape, jnp.float32) * deviation
    if len(shards) > 0:
        result = levels(stream_key, shape, shards, -0.22, 0.18) * result
    return jnp.clip(result, min=-reach, max=reach).astype(kind)


def setup_inputs(seed: int = 0) -> dict:
    splits = jax.random.split(jax.random.key(seed), 7)
    return {
        "propagator": centred(splits[0], (SECT, TIMES, B, B), 1.0, 6.0, ((0, 8), (1, 16))),
        "rising_op": centred(splits[1], (SECT, B, B), B ** -0.5, 0.25, ((0, 8),)),
        "energies": jnp.clip(jnp.exp(math.log(40.0) - 4.3820266 * jax.random.uniform(splits[2], (SECT, B), jnp.float32) ** levels(splits[2], (SECT, B), ((0, 8),), -0.2, 0.2)), 0.5, 40.0),
        "hyb_particle": jnp.clip(jnp.exp(math.log(1.0) - 1.609438 * jax.random.uniform(splits[3], (TIMES,), jnp.float32) ** levels(splits[3], (TIMES,), ((0, 16),), -0.2, 0.2)), 0.2, 1.0),
        "hyb_hole": jnp.clip(jnp.exp(math.log(1.0) - 1.609438 * jax.random.uniform(splits[4], (TIMES,), jnp.float32) ** levels(splits[4], (TIMES,), ((0, 16),), -0.2, 0.2)), 0.2, 1.0),
        "sector_sizes": draw_sector_sizes(jax.random.fold_in(splits[6], 71), 0),
    }


def reference(propagator, rising_op, energies, hyb_particle, hyb_hole, sector_sizes):
    highest = lax.Precision.HIGHEST
    step_size = 1.0 / TIMES
    positions = jnp.arange(B, dtype=jnp.int32)
    live_mask = positions[None, :] < sector_sizes[:, None]
    square = live_mask[:, :, None] & live_mask[:, None, :]
    masked_prop = jnp.where(square[:, None], propagator, jnp.zeros((), propagator.dtype))
    operator_wide = rising_op.astype(jnp.float32)
    raised = jnp.einsum('sik,stkl->stil', operator_wide, masked_prop.astype(jnp.float32), precision=highest).astype(jnp.bfloat16)
    upward = jnp.einsum('stik,sjk->stij', raised.astype(jnp.float32), operator_wide, precision=highest).astype(jnp.bfloat16)
    from_below = jnp.concatenate([jnp.zeros_like(upward[:1]), upward[:-1]], 0)
    from_above = jnp.concatenate([masked_prop[1:], jnp.zeros_like(masked_prop[:1])], 0)
    lowered = jnp.einsum('ski,stkl->stil', operator_wide, from_above.astype(jnp.float32), precision=highest).astype(jnp.bfloat16)
    downward = jnp.einsum('stik,skl->stil', lowered.astype(jnp.float32), operator_wide, precision=highest)
    combined = hyb_particle[None, :, None, None] * from_below.astype(jnp.float32) + hyb_hole[None, :, None, None] * downward
    self_energy = jnp.where(square[:, None], combined, jnp.zeros((), jnp.float32)).astype(jnp.bfloat16)
    identity = positions[:, None] == positions[None, :]

    def one_sector(operands):
        lag_table, history, level_rates, live_row = operands
        lag_wide = lag_table.astype(jnp.float32)
        history_wide = history.astype(jnp.float32)
        running_sum = jnp.zeros((TIMES, B, B), jnp.float32)
        for lag in range(TIMES):
            running_sum = running_sum.at[lag:].add(jnp.einsum('ik,tkl->til', lag_wide[lag], history_wide[:TIMES - lag], precision=highest))
        convolved = step_size * running_sum
        decay = jnp.exp(-step_size * level_rates)

        def advance(running, term):
            running = decay[:, None] * running + term
            return running, running

        _, summed = lax.scan(advance, jnp.zeros((B, B), jnp.float32), convolved)
        moments = jnp.arange(TIMES).astype(jnp.float32)
        free_part = jnp.where(live_row[None, :], jnp.exp(-level_rates[None, :] * (moments[:, None] * step_size)), jnp.zeros((), jnp.float32))
        diagonal = jnp.where(identity[None], free_part[:, :, None], jnp.zeros((), jnp.float32))
        return (diagonal - step_size * summed).astype(jnp.bfloat16)

    return lax.map(one_sector, (self_energy, masked_prop, energies, live_mask))
```

```python
import functools

import jax
import jax.numpy as jnp
import numpy as np
from jax import lax
from jax.experimental import pallas as pl
from jax.experimental.pallas import tpu as pltpu
from jax.sharding import Mesh
from jax.sharding import PartitionSpec as P


def shifted(block, axis, distance):
    devices = range(lax.axis_size(axis))
    route = [(i - distance, i) for i in devices if i - distance in devices]
    return lax.ppermute(block, axis, route)


def ring(block, axis, distance):
    n = lax.axis_size(axis)
    return lax.ppermute(block, axis, [(i, (i + distance) % n) for i in range(n)])


def ring_gather(block, axis):
    half = block.shape[0] // 2
    first, second = block[:half], block[half:]
    below_a = ring(first, axis, 1)
    above_a = ring(second, axis, -1)
    below_b = ring(second, axis, 1)
    above_b = ring(first, axis, -1)
    far_a = ring(below_a, axis, 1)
    far_b = ring(above_a, axis, -1)
    return [
        (-1, 0, below_a),
        (1, 1, above_a),
        (-1, 1, below_b),
        (1, 0, above_b),
        (2, 0, far_a),
        (2, 1, far_b),
    ]


def convolve_kernel(
    plan_e, plan_g, sides, step_size, scalars, rates, *refs
):
    n = sides
    count = 1 + len(plan_e)
    e_parts = refs[:count]
    g_parts = refs[count : 2 * count]
    out, e_all, g_all, total, sems = refs[2 * count :]
    rows = out.shape[1] * n
    here_x, here_y, size = scalars[0], scalars[1], scalars[2]

    copies = []
    for parts, plan, here, target in (
        (e_parts, plan_e, here_y, e_all),
        (g_parts, plan_g, here_x, g_all),
    ):
        copies.append((parts[0], target.at[here]))
        for part, (offset, half, length) in zip(parts[1:], plan):
            source = lax.rem(here + offset + n, n)
            copies.append((part, target.at[source, pl.ds(half * length, length)]))
    started = [
        pltpu.make_async_copy(src, dst, sems.at[i]) for i, (src, dst) in enumerate(copies)
    ]
    for copy in started:
        copy.start()
    total[...] = jnp.zeros_like(total)
    for copy in started:
        copy.wait()

    @pl.loop(0, n)
    def _(source):
        for v in range(n * n):
            lane, first = v % n, v // n

            @pl.when(v - source >= 0)
            def _():
                u = v - source
                left = e_all[source, : n - first].reshape((n - first) * rows, -1)
                right = g_all[u // n, lax.rem(u, n)]
                product = lax.dot_general(
                    left, right, (((1,), (1,)), ((), ())), preferred_element_type=jnp.float32
                )
                total[lane, first * rows :, :] += product

    rate = rates[...]
    decay = jnp.exp(-step_size * rate)
    row = lax.broadcasted_iota(jnp.int32, (rows, rows), 0)
    column = lax.broadcasted_iota(jnp.int32, (rows, rows), 1)
    on_diagonal = (row == column) & (here_x == here_y) & (row + here_x * rows < size)
    running = jnp.zeros((rows, rows), jnp.float32)
    quarter = rows // n
    for t in range(n * n):
        lane, first = t % n, t // n
        running = decay * running + step_size * total[lane, first * rows : (first + 1) * rows, :]
        free = jnp.where(on_diagonal, jnp.exp(-rate * (t * step_size)), 0.0)
        fresh = free - step_size * running
        for b in range(n):
            out[t, :, b * rows : (b + 1) * rows] = fresh[b * quarter : (b + 1) * quarter].astype(
                jnp.bfloat16
            )


def convolve(own_e, rest_e, own_g, rest_g, scalars, rates, n, step_size):
    plan_e = [(o, h, p.shape[0]) for o, h, p in rest_e]
    plan_g = [(o, h, p.shape[0]) for o, h, p in rest_g]
    parts = [own_e] + [p for _, _, p in rest_e] + [own_g] + [p for _, _, p in rest_g]
    _, rows, states = own_e.shape
    anywhere = pl.BlockSpec(memory_space=pl.ANY)
    return pl.pallas_call(
        functools.partial(convolve_kernel, plan_e, plan_g, n, step_size),
        out_shape=jax.ShapeDtypeStruct((n * n, rows // n, states), jnp.bfloat16),
        in_specs=[
            pl.BlockSpec(memory_space=pltpu.SMEM),
            pl.BlockSpec(memory_space=pltpu.VMEM),
        ]
        + [anywhere] * len(parts),
        out_specs=pl.BlockSpec(memory_space=pltpu.VMEM),
        scratch_shapes=[
            pltpu.VMEM((n, n, rows, states), jnp.bfloat16),
            pltpu.VMEM((n, n, rows, states), jnp.bfloat16),
            pltpu.VMEM((n, n * rows, rows), jnp.float32),
            pltpu.SemaphoreType.DMA((len(parts),)),
        ],
        compiler_params=pltpu.CompilerParams(vmem_limit_bytes=40 * 1024 * 1024),
        cost_estimate=pl.CostEstimate(
            flops=2 * 136 * rows * rows * states,
            bytes_accessed=4 * n * n * rows * states,
            transcendentals=0,
        ),
        name="convolve",
    )(scalars, rates, *parts)


def assemble_kernel(n, packets, out):
    quarter, states = packets.shape[1:]
    rows = states // n
    for x in range(n):
        for b in range(n):
            out[x * rows + b * quarter : x * rows + (b + 1) * quarter, :] = jnp.concatenate(
                [packets[x * n + y, :, b * rows : (b + 1) * rows] for y in range(n)], axis=1
            )


def assemble(packets, n):
    states = packets.shape[2]
    return pl.pallas_call(
        functools.partial(assemble_kernel, n),
        out_shape=jax.ShapeDtypeStruct((states, states), jnp.bfloat16),
        in_specs=[pl.BlockSpec(memory_space=pltpu.VMEM)],
        out_specs=pl.BlockSpec(memory_space=pltpu.VMEM),
        name="assemble",
    )(packets)


def per_device(propagator, rising_op, energies, hyb_particle, hyb_hole, sector_sizes):
    states = propagator.shape[2]
    n = lax.axis_size("tx")
    step_size = 1.0 / (n * n)
    rows = states // n
    here_x, here_y = lax.axis_index("tx"), lax.axis_index("ty")
    positions = jnp.arange(states, dtype=jnp.int32)
    live_mask = positions < sector_sizes[0]
    square = live_mask[:, None] & live_mask[None, :]
    zero = jnp.zeros((), jnp.bfloat16)
    masked = jnp.where(square, propagator[0, 0], zero)
    operator = rising_op[0]

    columns = lax.all_to_all(masked.T.reshape(n, rows, states), "ty", 0, 0, tiled=True)

    from_above = shifted(masked, "sector", -1)
    raised = jnp.dot(operator, masked, preferred_element_type=jnp.float32).astype(jnp.bfloat16)
    upward = jnp.einsum("ik,jk->ij", raised, operator, preferred_element_type=jnp.float32).astype(
        jnp.bfloat16
    )
    from_below = shifted(upward, "sector", 1)
    lowered = jnp.einsum(
        "ki,kl->il", operator, from_above, preferred_element_type=jnp.float32
    ).astype(jnp.bfloat16)
    downward = jnp.dot(lowered, operator, preferred_element_type=jnp.float32)
    combined = hyb_particle[0] * from_below.astype(jnp.float32) + hyb_hole[0] * downward
    self_energy = jnp.where(square, combined, 0.0).astype(jnp.bfloat16)

    lines = lax.all_to_all(self_energy.reshape(n, rows, states), "tx", 0, 0, tiled=True)

    rest_g = ring_gather(columns, "tx")
    rest_e = ring_gather(lines, "ty")
    rates = lax.dynamic_slice_in_dim(energies[0], here_x * rows, rows, 0)[:, None]
    scalars = jnp.stack([here_x, here_y, sector_sizes[0]]).astype(jnp.int32)
    packets = convolve(lines, rest_e, columns, rest_g, scalars, rates, n, step_size)
    packets = lax.all_to_all(packets, ("tx", "ty"), 0, 0, tiled=True)
    return assemble(packets, n)[None, None]


def solution(mesh):
    n = math_root(mesh.shape["tm"])
    split = Mesh(
        np.asarray(mesh.devices).reshape(n, n, mesh.shape["sector"]), ("tx", "ty", "sector")
    )
    times = ("tx", "ty")
    placed = (
        P("sector", times, None, None),
        P("sector", None, None),
        P("sector", None),
        P(times),
        P(times),
        P("sector"),
    )
    return jax.shard_map(
        per_device,
        mesh=split,
        in_specs=placed,
        out_specs=P("sector", times, None, None),
        check_vma=False,
    )


def math_root(count):
    return int(round(count**0.5))
```

```python
import functools

import jax
import jax.numpy as jnp
import numpy as np
from jax import lax
from jax.experimental import pallas as pl
from jax.experimental.pallas import tpu as pltpu
from jax.sharding import Mesh
from jax.sharding import PartitionSpec as P

MIB = 1024 * 1024
VMEM = pl.BlockSpec(memory_space=pltpu.VMEM)
SMEM = pl.BlockSpec(memory_space=pltpu.SMEM)
ANY = pl.BlockSpec(memory_space=pl.ANY)
NT = (((1,), (1,)), ((), ()))


def shifted(block, axis, distance):
    devices = range(lax.axis_size(axis))
    route = [(i - distance, i) for i in devices if i - distance in devices]
    return lax.ppermute(block, axis, route)


def ring(block, axis, distance):
    n = lax.axis_size(axis)
    return lax.ppermute(block, axis, [(i, (i + distance) % n) for i in range(n)])


def tied(value, *others):
    return lax.optimization_barrier((value, *others))[0]


def halves_gather(first, second, axis):
    below_a = ring(first, axis, 1)
    above_b = ring(second, axis, -1)
    below_b = ring(second, axis, 1)
    above_a = ring(first, axis, -1)
    far_a = ring(below_a, axis, 1)
    far_b = ring(above_b, axis, -1)
    return [
        (-1, 0, below_a),
        (1, 1, above_b),
        (-1, 1, below_b),
        (1, 0, above_a),
        (2, 0, far_a),
        (2, 1, far_b),
    ]


def live(shape, size, first_row=0):
    row = lax.broadcasted_iota(jnp.int32, shape, 0) + first_row
    column = lax.broadcasted_iota(jnp.int32, shape, 1)
    return (row < size) & (column < size)


def masked_block(value, size, first_row=0):
    wide = value.astype(jnp.float32)
    return jnp.where(live(value.shape, size, first_row), wide, 0.0).astype(jnp.bfloat16)


def dot(a, b):
    return jnp.dot(a, b, preferred_element_type=jnp.float32)


def turn_kernel(scalars, prop, turned):
    turned[...] = masked_block(prop[...], scalars[2]).T


def turn(scalars, prop):
    return pl.pallas_call(
        turn_kernel,
        out_shape=jax.ShapeDtypeStruct(prop.shape, jnp.bfloat16),
        in_specs=[SMEM, VMEM],
        out_specs=VMEM,
        cost_estimate=pl.CostEstimate(flops=0, bytes_accessed=4 * prop.size, transcendentals=0),
        name="turn",
    )(scalars, prop)


def raise_kernel(scalars, prop, operator, upward, flipped):
    inner = masked_block(prop[...], scalars[2])
    r = operator[...]
    raised = dot(r, inner).astype(jnp.bfloat16)
    upward[...] = lax.dot_general(raised, r, NT, preferred_element_type=jnp.float32).astype(
        jnp.bfloat16
    )
    flipped[...] = r.T


def raise_terms(scalars, prop, operator):
    states = prop.shape[0]
    square = jax.ShapeDtypeStruct((states, states), jnp.bfloat16)
    return pl.pallas_call(
        raise_kernel,
        out_shape=(square, square),
        in_specs=[SMEM, VMEM, VMEM],
        out_specs=(VMEM, VMEM),
        cost_estimate=pl.CostEstimate(
            flops=4 * states**3, bytes_accessed=8 * states**2, transcendentals=0
        ),
        name="raise_terms",
    )(scalars, prop, operator)


def energy_kernel(scalars, weights, above, below, operator, flipped, *outs):
    n = len(outs)
    rows = outs[0].shape[0]
    here_x, size, size_above = scalars[0], scalars[2], scalars[3]
    inner = masked_block(above[...], size_above)
    r = operator[...]
    for d in (2, 1, 3, 0):
        first = pl.multiple_of(lax.rem(here_x + d, n) * rows, 32)
        lowered = dot(flipped[pl.ds(first, rows), :], inner).astype(jnp.bfloat16)
        downward = dot(lowered, r)
        raised = below[pl.ds(first, rows), :].astype(jnp.float32)
        both = weights[0] * raised + weights[1] * downward
        outs[d][...] = jnp.where(live(both.shape, size, first), both, 0.0).astype(jnp.bfloat16)


def energy_blocks(scalars, weights, above, below, operator, flipped, n):
    states = above.shape[0]
    block = jax.ShapeDtypeStruct((states // n, states), jnp.bfloat16)
    return pl.pallas_call(
        energy_kernel,
        out_shape=(block,) * n,
        in_specs=[SMEM, SMEM, VMEM, VMEM, VMEM, VMEM],
        out_specs=(VMEM,) * n,
        cost_estimate=pl.CostEstimate(
            flops=4 * states**3, bytes_accessed=10 * states**2, transcendentals=0
        ),
        name="energy_blocks",
    )(scalars, weights, above, below, operator, flipped)


def convolve_kernel(plan, n, step_size, scalars, rates, *refs):
    parts = refs[: len(plan)]
    out, e_all, g_all, total, sems = refs[len(plan) :]
    rows = out.shape[1] * n
    here_x, here_y, size = scalars[0], scalars[1], scalars[2]

    def around(here, offset):
        return lax.rem(here + offset + n, n)

    copies = []
    for part, (kind, dx, dy, half) in zip(parts, plan):
        x, y = around(here_x, dx), around(here_y, dy)
        if kind == "block":
            copies.append((part, e_all.at[x, y]))
        elif kind == "rest":
            tall = part.shape[1]
            for d in range(1, n):
                room = e_all.at[around(here_x, -d), y, pl.ds(half * tall, tall)]
                copies.append((part.at[d - 1], room))
        elif kind == "column":
            copies.append((part, g_all.at[x]))
        else:
            some = part.shape[0]
            copies.append((part, g_all.at[x, pl.ds(half * some, some)]))
    started = [
        pltpu.make_async_copy(src, dst, sems.at[i]) for i, (src, dst) in enumerate(copies)
    ]
    for copy in started:
        copy.start()
    for copy in started:
        copy.wait()

    lags = e_all.reshape(n * n, *e_all.shape[2:])
    for u in range(n * n):
        right = g_all[u // n, u % n]
        for first in range(0, n * n - u, n):
            some = min(n, n * n - u - first)
            left = lags[first : first + some].reshape(some * rows, -1)
            product = lax.dot_general(left, right, NT, preferred_element_type=jnp.float32)
            where = slice((u + first) * rows, (u + first + some) * rows)
            if u == 0:
                total[where] = product
            else:
                total[where] += product

    quarter = rows // n
    scale = step_size * step_size
    for b in range(n):
        row = lax.broadcasted_iota(jnp.int32, (quarter, rows), 0) + b * quarter
        column = lax.broadcasted_iota(jnp.int32, (quarter, rows), 1)
        starts = (row == column) & (here_x == here_y) & (row + here_x * rows < size)
        rate = rates[b * quarter : (b + 1) * quarter]
        decay = jnp.broadcast_to(jnp.exp(-step_size * rate), (quarter, rows))
        for t in range(n * n):
            term = scale * total[t * rows + b * quarter : t * rows + (b + 1) * quarter]
            fresh = (jnp.where(starts, 1.0, 0.0) if t == 0 else decay * fresh) - term
            out[t, :, b * rows : (b + 1) * rows] = fresh.astype(jnp.bfloat16)


def convolve(parts, plan, scalars, rates, n, step_size):
    rows, states = parts[0].shape
    copies = sum(n - 1 if kind == "rest" else 1 for kind, *_ in plan)
    return pl.pallas_call(
        functools.partial(convolve_kernel, plan, n, step_size),
        out_shape=jax.ShapeDtypeStruct((n * n, rows // n, states), jnp.bfloat16),
        in_specs=[SMEM, VMEM] + [ANY] * len(parts),
        out_specs=VMEM,
        scratch_shapes=[
            pltpu.VMEM((n, n, rows, states), jnp.bfloat16),
            pltpu.VMEM((n, n, rows, states), jnp.bfloat16),
            pltpu.VMEM((n * n * rows, rows), jnp.float32),
            pltpu.SemaphoreType.DMA((copies,)),
        ],
        compiler_params=pltpu.CompilerParams(vmem_limit_bytes=32 * MIB),
        cost_estimate=pl.CostEstimate(
            flops=n * n * (n * n + 1) * rows * rows * states,
            bytes_accessed=4 * n * n * rows * states,
            transcendentals=0,
        ),
        name="convolve",
    )(scalars, rates, *parts)


def assemble_kernel(n, packets, out):
    quarter, states = packets.shape[1:]
    rows = states // n
    for x in range(n):
        for b in range(n):
            out[x * rows + b * quarter : x * rows + (b + 1) * quarter, :] = jnp.concatenate(
                [packets[x * n + y, :, b * rows : (b + 1) * rows] for y in range(n)], axis=1
            )


def assemble(packets, n):
    states = packets.shape[2]
    return pl.pallas_call(
        functools.partial(assemble_kernel, n),
        out_shape=jax.ShapeDtypeStruct((states, states), jnp.bfloat16),
        in_specs=[VMEM],
        out_specs=VMEM,
        name="assemble",
    )(packets)


def per_device(propagator, rising_op, energies, hyb_particle, hyb_hole, sector_sizes):
    states = propagator.shape[2]
    n = lax.axis_size("tx")
    step_size = 1.0 / (n * n)
    rows = states // n
    here_x, here_y = lax.axis_index("tx"), lax.axis_index("ty")
    raw, operator = propagator[0, 0], rising_op[0]

    above = shifted(raw, "sector", -1)
    size_above = shifted(sector_sizes, "sector", -1)
    scalars = jnp.stack([here_x, here_y, sector_sizes[0]]).astype(jnp.int32)
    turned = turn(scalars, raw)
    columns = lax.all_to_all(turned.reshape(n, rows, states), "ty", 0, 0, tiled=True)

    upward, flipped = raise_terms(scalars, tied(raw, turned), operator)
    below = shifted(upward, "sector", 1)
    scalars = jnp.stack([here_x, here_y, sector_sizes[0], size_above[0]]).astype(jnp.int32)
    weights = jnp.concatenate([hyb_particle, hyb_hole])
    own, *away = energy_blocks(scalars, weights, above, below, operator, flipped, n)

    crossed = [ring(away[d - 1], "tx", d) for d in (2, 1, 3)]
    crossed = [crossed[1], crossed[0], crossed[2]]
    parts, plan = [own], [("block", 0, 0, 0)]
    spread = [ring(own, "ty", d) for d in (1, -1, 2)]
    *crossed, a, b, c = lax.optimization_barrier((*crossed, *spread))
    for d, piece in zip((1, -1, 2), (a, b, c)):
        parts.append(piece)
        plan.append(("block", 0, -d, 0))
    for d in range(1, n):
        parts.append(crossed[d - 1])
        plan.append(("block", -d, 0, 0))
    half = rows // 2
    first = jnp.stack([block[:half] for block in crossed])
    second = jnp.stack([block[half:] for block in crossed])
    for offset, which, piece in halves_gather(first, second, "ty"):
        parts.append(piece)
        plan.append(("rest", 0, offset, which))

    parts.append(columns)
    plan.append(("column", 0, 0, 0))
    for offset, which, piece in halves_gather(columns[: n // 2], columns[n // 2 :], "tx"):
        parts.append(piece)
        plan.append(("columns", offset, 0, which))

    rates = lax.dynamic_slice_in_dim(energies[0], here_x * rows, rows, 0)[:, None]
    packets = convolve(parts, plan, scalars, rates, n, step_size)
    packets = lax.all_to_all(packets, ("tx", "ty"), 0, 0, tiled=True)
    return assemble(packets, n)[None, None]


def solution(mesh):
    n = round(mesh.shape["tm"] ** 0.5)
    split = Mesh(
        np.asarray(mesh.devices).reshape(n, n, mesh.shape["sector"]), ("tx", "ty", "sector")
    )
    times = ("tx", "ty")
    placed = (
        P("sector", times, None, None),
        P("sector", None, None),
        P("sector", None),
        P(times),
        P(times),
        P("sector"),
    )
    return jax.shard_map(
        per_device,
        mesh=split,
        in_specs=placed,
        out_specs=P("sector", times, None, None),
        check_vma=False,
    )
```

```python
import functools

import jax
import jax.numpy as jnp
import numpy as np
from jax import lax
from jax.experimental import pallas as pl
from jax.experimental.pallas import tpu as pltpu
from jax.sharding import Mesh
from jax.sharding import PartitionSpec as P

MIB = 1024 * 1024
VMEM = pl.BlockSpec(memory_space=pltpu.VMEM)
SMEM = pl.BlockSpec(memory_space=pltpu.SMEM)
ANY = pl.BlockSpec(memory_space=pl.ANY)
NT = (((1,), (1,)), ((), ()))


def shifted(block, axis, distance):
    devices = range(lax.axis_size(axis))
    route = [(i - distance, i) for i in devices if i - distance in devices]
    return lax.ppermute(block, axis, route)


def ring(block, axis, distance):
    n = lax.axis_size(axis)
    return lax.ppermute(block, axis, [(i, (i + distance) % n) for i in range(n)])


def tied(value, *others):
    return lax.optimization_barrier((value, *others))[0]


def spread(block, axis):
    return [(-d, ring(block, axis, d)) for d in (1, -1, 2)]


def halves_gather(first, second, axis):
    below_a = ring(first, axis, 1)
    above_b = ring(second, axis, -1)
    below_b = ring(second, axis, 1)
    above_a = ring(first, axis, -1)
    far_a = ring(below_a, axis, 1)
    far_b = ring(above_b, axis, -1)
    return [
        (-1, 0, below_a),
        (1, 1, above_b),
        (-1, 1, below_b),
        (1, 0, above_a),
        (2, 0, far_a),
        (2, 1, far_b),
    ]


def stacked_halves(blocks):
    half = blocks[0].shape[0] // 2
    return jnp.stack([b[:half] for b in blocks]), jnp.stack([b[half:] for b in blocks])


def live(shape, size, first_row=0):
    row = lax.broadcasted_iota(jnp.int32, shape, 0) + first_row
    column = lax.broadcasted_iota(jnp.int32, shape, 1)
    return (row < size) & (column < size)


def dot(a, b):
    return jnp.dot(a, b, preferred_element_type=jnp.float32)


def turn_kernel(masked, *outs):
    n = len(outs)
    rows = outs[0].shape[0]
    here_y = lax.axis_index("ty")
    for k in range(n):
        block = masked[:, k * rows : (k + 1) * rows].T
        for d in range(n):

            @pl.when(lax.rem(here_y + d, n) == k)
            def _():
                outs[d][...] = block


def turn_blocks(masked, n):
    states = masked.shape[0]
    block = jax.ShapeDtypeStruct((states // n, states), jnp.bfloat16)
    return pl.pallas_call(
        turn_kernel,
        out_shape=(block,) * n,
        in_specs=[VMEM],
        out_specs=(VMEM,) * n,
        cost_estimate=pl.CostEstimate(flops=0, bytes_accessed=4 * states**2, transcendentals=0),
        name="turn_blocks",
    )(masked)


def raise_kernel(masked, operator, upward, flipped):
    r = operator[...]
    raised = dot(r, masked[...]).astype(jnp.bfloat16)
    upward[...] = lax.dot_general(raised, r, NT, preferred_element_type=jnp.float32).astype(
        jnp.bfloat16
    )
    flipped[...] = r.T


def raise_terms(masked, operator):
    states = masked.shape[0]
    square = jax.ShapeDtypeStruct((states, states), jnp.bfloat16)
    return pl.pallas_call(
        raise_kernel,
        out_shape=(square, square),
        in_specs=[VMEM, VMEM],
        out_specs=(VMEM, VMEM),
        cost_estimate=pl.CostEstimate(
            flops=4 * states**3, bytes_accessed=8 * states**2, transcendentals=0
        ),
        name="raise_terms",
    )(masked, operator)


def energy_kernel(sizes, particle, hole, above, below, operator, flipped, *outs):
    n = len(outs)
    rows = outs[0].shape[0]
    here_x = lax.axis_index("tx")
    inner = above[...]
    r = operator[...]
    for d in (2, 1, 3, 0):
        first = pl.multiple_of(lax.rem(here_x + d, n) * rows, 32)
        lowered = dot(flipped[pl.ds(first, rows), :], inner).astype(jnp.bfloat16)
        downward = dot(lowered, r)
        raised = below[pl.ds(first, rows), :].astype(jnp.float32)
        both = particle[0] * raised + hole[0] * downward
        kept = live(both.shape, sizes[0], first)
        outs[d][...] = jnp.where(kept, both, 0.0).astype(jnp.bfloat16)


def energy_blocks(sizes, particle, hole, above, below, operator, flipped, n):
    states = above.shape[0]
    block = jax.ShapeDtypeStruct((states // n, states), jnp.bfloat16)
    return pl.pallas_call(
        energy_kernel,
        out_shape=(block,) * n,
        in_specs=[SMEM] * 3 + [VMEM] * 4,
        out_specs=(VMEM,) * n,
        cost_estimate=pl.CostEstimate(
            flops=4 * states**3, bytes_accessed=10 * states**2, transcendentals=0
        ),
        name="energy_blocks",
    )(sizes, particle, hole, above, below, operator, flipped)


def convolve_kernel(plan, n, step_size, sizes, rates, *refs):
    parts = refs[: len(plan)]
    out, e_all, g_all, total, sems = refs[len(plan) :]
    rows = out.shape[1] * n
    here_x, here_y, size = lax.axis_index("tx"), lax.axis_index("ty"), sizes[0]

    def around(here, offset):
        return lax.rem(here + offset + n, n)

    copies = []
    for part, (kind, far, near, half) in zip(parts, plan):
        room = e_all if kind == "e" else g_all

        def place(cross, ring_step):
            if kind == "e":
                return around(here_x, cross), around(here_y, ring_step)
            return around(here_x, ring_step), around(here_y, cross)

        if half is None:
            copies.append((part, room.at[place(far, near)]))
        else:
            tall = part.shape[1]
            for d in range(1, n):
                copies.append(
                    (part.at[d - 1], room.at[(*place(-d, near), pl.ds(half * tall, tall))])
                )
    started = [
        pltpu.make_async_copy(src, dst, sems.at[i]) for i, (src, dst) in enumerate(copies)
    ]
    for copy in started:
        copy.start()
    for copy in started:
        copy.wait()

    lags = e_all.reshape(n * n, *e_all.shape[2:])
    for u in range(n * n):
        right = g_all[u // n, u % n]
        for first in range(0, n * n - u, n):
            some = min(n, n * n - u - first)
            left = lags[first : first + some].reshape(some * rows, -1)
            product = lax.dot_general(left, right, NT, preferred_element_type=jnp.float32)
            where = slice((u + first) * rows, (u + first + some) * rows)
            if u == 0:
                total[where] = product
            else:
                total[where] += product

    quarter = rows // n
    scale = step_size * step_size
    for b in range(n):
        row = lax.broadcasted_iota(jnp.int32, (quarter, rows), 0) + b * quarter
        column = lax.broadcasted_iota(jnp.int32, (quarter, rows), 1)
        starts = (row == column) & (here_x == here_y) & (row + here_x * rows < size)
        rate = rates[b * quarter : (b + 1) * quarter]
        decay = jnp.broadcast_to(jnp.exp(-step_size * rate), (quarter, rows))
        for t in range(n * n):
            term = scale * total[t * rows + b * quarter : t * rows + (b + 1) * quarter]
            fresh = (jnp.where(starts, 1.0, 0.0) if t == 0 else decay * fresh) - term
            out[t, :, b * rows : (b + 1) * rows] = fresh.astype(jnp.bfloat16)


def convolve(parts, plan, sizes, rates, n, step_size):
    rows, states = parts[0].shape
    copies = sum(1 if half is None else n - 1 for *_, half in plan)
    return pl.pallas_call(
        functools.partial(convolve_kernel, plan, n, step_size),
        out_shape=jax.ShapeDtypeStruct((n * n, rows // n, states), jnp.bfloat16),
        in_specs=[SMEM, VMEM] + [ANY] * len(parts),
        out_specs=VMEM,
        scratch_shapes=[
            pltpu.VMEM((n, n, rows, states), jnp.bfloat16),
            pltpu.VMEM((n, n, rows, states), jnp.bfloat16),
            pltpu.VMEM((n * n * rows, rows), jnp.float32),
            pltpu.SemaphoreType.DMA((copies,)),
        ],
        compiler_params=pltpu.CompilerParams(vmem_limit_bytes=50 * MIB),
        cost_estimate=pl.CostEstimate(
            flops=n * n * (n * n + 1) * rows * rows * states,
            bytes_accessed=4 * n * n * rows * states,
            transcendentals=0,
        ),
        name="convolve",
    )(sizes, rates, *parts)


def assemble_kernel(n, packets, out):
    quarter, states = packets.shape[1:]
    rows = states // n
    for x in range(n):
        for b in range(n):
            out[x * rows + b * quarter : x * rows + (b + 1) * quarter, :] = jnp.concatenate(
                [packets[x * n + y, :, b * rows : (b + 1) * rows] for y in range(n)], axis=1
            )


def assemble(packets, n):
    states = packets.shape[2]
    return pl.pallas_call(
        functools.partial(assemble_kernel, n),
        out_shape=jax.ShapeDtypeStruct((states, states), jnp.bfloat16),
        in_specs=[VMEM],
        out_specs=VMEM,
        name="assemble",
    )(packets)


def per_device(propagator, rising_op, energies, hyb_particle, hyb_hole, sector_sizes):
    states = propagator.shape[2]
    n = lax.axis_size("tx")
    step_size = 1.0 / (n * n)
    rows = states // n
    here_x = lax.axis_index("tx")
    operator = rising_op[0]
    live_mask = jnp.arange(states, dtype=jnp.int32) < sector_sizes[0]
    square = live_mask[:, None] & live_mask[None, :]
    masked = jnp.where(square, propagator[0, 0], jnp.zeros((), jnp.bfloat16))

    above = shifted(masked, "sector", -1)
    upward, flipped = raise_terms(masked, operator)
    below = shifted(upward, "sector", 1)

    own_g, *away_g = turn_blocks(tied(masked, upward), n)
    crossed_g = {d: ring(away_g[d - 1], "ty", d) for d in (2, 1, 3)}
    spread_g = spread(own_g, "tx")

    operator_late = tied(operator, own_g)
    own_e, *away_e = energy_blocks(
        sector_sizes, hyb_particle, hyb_hole, above, below, operator_late, flipped, n
    )
    crossed_e = {d: ring(away_e[d - 1], "tx", d) for d in (2, 1, 3)}
    spread_e = spread(own_e, "ty")

    parts, plan = [], []

    def add(kind, far, near, half, piece):
        parts.append(piece)
        plan.append((kind, far, near, half))

    crossed_e = [crossed_e[d] for d in range(1, n)]
    crossed_g = [crossed_g[d] for d in range(1, n)]
    arrived = lax.optimization_barrier((crossed_e, crossed_g, [p for _, p in spread_e]))
    crossed_e, crossed_g, pieces_e = arrived
    for kind, own, crossed, near in (
        ("e", own_e, crossed_e, list(zip([o for o, _ in spread_e], pieces_e))),
        ("g", own_g, crossed_g, spread_g),
    ):
        add(kind, 0, 0, None, own)
        for d in range(1, n):
            add(kind, -d, 0, None, crossed[d - 1])
        for offset, piece in near:
            add(kind, 0, offset, None, piece)
        axis = "ty" if kind == "e" else "tx"
        for offset, half, piece in halves_gather(*stacked_halves(crossed), axis):
            add(kind, 0, offset, half, piece)

    rates = lax.dynamic_slice_in_dim(energies[0], here_x * rows, rows, 0)[:, None]
    packets = convolve(parts, plan, sector_sizes, rates, n, step_size)
    packets = lax.all_to_all(packets, ("tx", "ty"), 0, 0, tiled=True)
    return assemble(packets, n)[None, None]


def solution(mesh):
    n = round(mesh.shape["tm"] ** 0.5)
    split = Mesh(
        np.asarray(mesh.devices).reshape(n, n, mesh.shape["sector"]), ("tx", "ty", "sector")
    )
    times = ("tx", "ty")
    placed = (
        P("sector", times, None, None),
        P("sector", None, None),
        P("sector", None),
        P(times),
        P(times),
        P("sector"),
    )
    return jax.shard_map(
        per_device,
        mesh=split,
        in_specs=placed,
        out_specs=P("sector", times, None, None),
        check_vma=False,
    )
```

```python
import functools

import jax
import jax.numpy as jnp
import numpy as np
from jax import lax
from jax.experimental import pallas as pl
from jax.experimental.pallas import tpu as pltpu
from jax.sharding import Mesh
from jax.sharding import PartitionSpec as P

MIB = 1024 * 1024
VMEM = pl.BlockSpec(memory_space=pltpu.VMEM)
SMEM = pl.BlockSpec(memory_space=pltpu.SMEM)
HBM = pl.BlockSpec(memory_space=pltpu.HBM)
NT = (((1,), (1,)), ((), ()))


def shifted(block, axis, distance):
    devices = range(lax.axis_size(axis))
    route = [(i - distance, i) for i in devices if i - distance in devices]
    return lax.ppermute(block, axis, route)


def ring(block, axis, distance):
    n = lax.axis_size(axis)
    return lax.ppermute(block, axis, [(i, (i + distance) % n) for i in range(n)])


def tied(value, *others):
    return lax.optimization_barrier((value, *others))[0]


def spread(block, axis):
    return [(-d, ring(block, axis, d)) for d in (1, -1, 2)]


def relay_gather(block, axis):
    half = block.shape[0] // 2
    below, above = ring(block, axis, 1), ring(block, axis, -1)
    return below, above, ring(below[:half], axis, 1), ring(above[half:], axis, -1)


def live(shape, size, first_row=0):
    row = lax.broadcasted_iota(jnp.int32, shape, 0) + first_row
    column = lax.broadcasted_iota(jnp.int32, shape, 1)
    return (row < size) & (column < size)


def dot(a, b):
    return jnp.dot(a, b, preferred_element_type=jnp.float32)


def raise_kernel(sizes, prop, operator, masked, upward):
    inner = prop[...].astype(jnp.float32)
    inner = jnp.where(live(inner.shape, sizes[0]), inner, 0.0).astype(jnp.bfloat16)
    masked[...] = inner
    r = operator[...]
    raised = dot(r, inner).astype(jnp.bfloat16)
    upward[...] = lax.dot_general(raised, r, NT, preferred_element_type=jnp.float32).astype(
        jnp.bfloat16
    )


def raise_terms(sizes, prop, operator):
    states = prop.shape[0]
    square = jax.ShapeDtypeStruct((states, states), jnp.bfloat16)
    return pl.pallas_call(
        raise_kernel,
        out_shape=(square, square),
        in_specs=[SMEM, VMEM, VMEM],
        out_specs=(VMEM, VMEM),
        cost_estimate=pl.CostEstimate(
            flops=4 * states**3, bytes_accessed=8 * states**2, transcendentals=0
        ),
        name="raise_terms",
    )(sizes, prop, operator)


def turn_kernel(masked, operator, turned, flipped):
    turned[...] = masked[...].T
    flipped[...] = operator[...].T


def turn(masked, operator):
    states = masked.shape[0]
    square = jax.ShapeDtypeStruct((states, states), jnp.bfloat16)
    return pl.pallas_call(
        turn_kernel,
        out_shape=(square, square),
        in_specs=[VMEM, VMEM],
        out_specs=(VMEM, VMEM),
        cost_estimate=pl.CostEstimate(flops=0, bytes_accessed=8 * states**2, transcendentals=0),
        name="turn",
    )(masked, operator)


def energy_kernel(sizes, particle, hole, *refs):
    sources, (*outs,), copies, sems = refs[:4], refs[4:-5], refs[-5:-1], refs[-1]
    moves = [
        pltpu.make_async_copy(src, dst, sems.at[i])
        for i, (src, dst) in enumerate(zip(sources, copies))
    ]
    for move in moves:
        move.start()
    n = len(outs)
    rows = outs[0].shape[0]
    here_x = lax.axis_index("tx")
    for move in moves:
        move.wait()
    flipped, above, operator, below = copies
    inner = above[...]
    r = operator[...]
    for d in (2, 1, 3, 0):
        first = pl.multiple_of(lax.rem(here_x + d, n) * rows, 32)
        lowered = dot(flipped[pl.ds(first, rows), :], inner).astype(jnp.bfloat16)
        downward = dot(lowered, r)
        raised = below[pl.ds(first, rows), :].astype(jnp.float32)
        both = particle[0] * raised + hole[0] * downward
        kept = live(both.shape, sizes[0], first)
        outs[d][...] = jnp.where(kept, both, 0.0).astype(jnp.bfloat16)


def energy_blocks(sizes, particle, hole, above, below, operator, flipped, n):
    states = above.shape[0]
    block = jax.ShapeDtypeStruct((states // n, states), jnp.bfloat16)
    return pl.pallas_call(
        energy_kernel,
        out_shape=(block,) * n,
        in_specs=[SMEM] * 3 + [HBM] * 4,
        out_specs=(VMEM,) * n,
        scratch_shapes=[pltpu.VMEM((states, states), jnp.bfloat16)] * 4
        + [pltpu.SemaphoreType.DMA((4,))],
        cost_estimate=pl.CostEstimate(
            flops=4 * states**3, bytes_accessed=10 * states**2, transcendentals=0
        ),
        name="energy_blocks",
    )(sizes, particle, hole, flipped, above, operator, below)


def around(here, offset, n):
    return lax.rem(here + offset + n, n)


def placed(parts, plan, n, e_all, g_all, pad, sems):
    here_x = lax.axis_index("tx")
    copies = []
    for part, (kind, offset, slot) in zip(parts, plan):
        if kind == "e":
            copies.append((part, e_all.at[slot, around(here_x, offset, n)]))
        elif kind == "rest":
            for d in range(1, n):
                copies.append((part.at[d - 1], e_all.at[slot, around(here_x, -d, n)]))
        else:
            some = part.shape[0]
            start = pad + around(here_x, offset, n) * n + slot * some
            copies.append((part, g_all.at[pl.ds(start, some)]))
    moves = [
        pltpu.make_async_copy(src, dst, sems.at[i]) for i, (src, dst) in enumerate(copies)
    ]
    for move in moves:
        move.start()
    return moves


def near_kernel(plan, n, *refs):
    parts = refs[: len(plan)]
    total, e_all, g_all, sems = refs[len(plan) :]
    rows = total.shape[2]
    moves = placed(parts, plan, n, e_all, g_all, n - 1, sems)
    g_all[: n - 1] = jnp.zeros((n - 1, *g_all.shape[1:]), jnp.bfloat16)
    here_y = lax.axis_index("ty")
    for move in moves:
        move.wait()

    for slot in range(n - 1):
        source = lax.rem(here_y + slot + slot // 2, n)
        for v in range(n * n):
            lane, first = v % n, v // n
            left = e_all[slot, : n - first].reshape((n - first) * rows, -1)
            right = g_all[v - source + n - 1]
            product = lax.dot_general(left, right, NT, preferred_element_type=jnp.float32)
            if slot == 0 and first == 0:
                total[lane] = product
            else:
                total[lane, first * rows :, :] += product


def far_kernel(plan, n, step_size, sizes, rates, near, *refs):
    parts = refs[: len(plan)]
    out, e_all, g_all, total, sems = refs[len(plan) :]
    rows = total.shape[2]
    moves = placed(parts, plan, n, e_all, g_all, n - 1, sems)
    g_all[: n - 1] = jnp.zeros((n - 1, *g_all.shape[1:]), jnp.bfloat16)
    here_x, here_y, size = lax.axis_index("tx"), lax.axis_index("ty"), sizes[0]
    source = lax.rem(here_y + n // 2, n)
    for move in moves:
        move.wait()
    for v in range(n * n):
        lane, first = v % n, v // n
        left = e_all[0, : n - first].reshape((n - first) * rows, -1)
        right = g_all[v - source + n - 1]
        product = lax.dot_general(left, right, NT, preferred_element_type=jnp.float32)
        if first == 0:
            total[lane] = near[lane] + product
        else:
            total[lane, first * rows :, :] += product

    quarter = rows // n
    scale = step_size * step_size
    for b in range(n):
        row = lax.broadcasted_iota(jnp.int32, (quarter, rows), 0) + b * quarter
        column = lax.broadcasted_iota(jnp.int32, (quarter, rows), 1)
        starts = (row == column) & (here_x == here_y) & (row + here_x * rows < size)
        rate = rates[b * quarter : (b + 1) * quarter]
        decay = jnp.broadcast_to(jnp.exp(-step_size * rate), (quarter, rows))
        for t in range(n * n):
            top = t // n * rows + b * quarter
            term = scale * total[t % n, top : top + quarter]
            fresh = (jnp.where(starts, 1.0, 0.0) if t == 0 else decay * fresh) - term
            out[t, :, b * rows : (b + 1) * rows] = fresh.astype(jnp.bfloat16)


def copies_of(plan, n):
    return sum(n - 1 if kind == "rest" else 1 for kind, *_ in plan)


def convolve_near(entries, n):
    plan, parts = [e[:3] for e in entries], [e[3] for e in entries]
    rows, states = parts[0].shape
    return pl.pallas_call(
        functools.partial(near_kernel, plan, n),
        out_shape=jax.ShapeDtypeStruct((n, n * rows, rows), jnp.float32),
        in_specs=[HBM] * len(parts),
        out_specs=VMEM,
        scratch_shapes=[
            pltpu.VMEM((n - 1, n, rows, states), jnp.bfloat16),
            pltpu.VMEM((n * n + n - 1, rows, states), jnp.bfloat16),
            pltpu.SemaphoreType.DMA((copies_of(plan, n),)),
        ],
        compiler_params=pltpu.CompilerParams(vmem_limit_bytes=52 * MIB),
        cost_estimate=pl.CostEstimate(
            flops=200 * rows * rows * states,
            bytes_accessed=56 * rows * states,
            transcendentals=0,
        ),
        name="convolve_near",
    )(*parts)


def convolve_far(entries, near, sizes, rates, n, step_size):
    plan, parts = [e[:3] for e in entries], [e[3] for e in entries]
    rows, states = parts[0].shape
    return pl.pallas_call(
        functools.partial(far_kernel, plan, n, step_size),
        out_shape=jax.ShapeDtypeStruct((n * n, rows // n, states), jnp.bfloat16),
        in_specs=[SMEM, VMEM, VMEM] + [HBM] * len(parts),
        out_specs=VMEM,
        scratch_shapes=[
            pltpu.VMEM((1, n, rows, states), jnp.bfloat16),
            pltpu.VMEM((n * n + n - 1, rows, states), jnp.bfloat16),
            pltpu.VMEM((n, n * rows, rows), jnp.float32),
            pltpu.SemaphoreType.DMA((copies_of(plan, n),)),
        ],
        compiler_params=pltpu.CompilerParams(vmem_limit_bytes=52 * MIB),
        cost_estimate=pl.CostEstimate(
            flops=72 * rows * rows * states,
            bytes_accessed=60 * rows * states,
            transcendentals=0,
        ),
        name="convolve_far",
    )(sizes, rates, near, *parts)


def assemble_kernel(n, packets, out):
    quarter, states = packets.shape[1:]
    rows = states // n
    for x in range(n):
        for b in range(n):
            out[x * rows + b * quarter : x * rows + (b + 1) * quarter, :] = jnp.concatenate(
                [packets[x * n + y, :, b * rows : (b + 1) * rows] for y in range(n)], axis=1
            )


def assemble(packets, n):
    states = packets.shape[2]
    return pl.pallas_call(
        functools.partial(assemble_kernel, n),
        out_shape=jax.ShapeDtypeStruct((states, states), jnp.bfloat16),
        in_specs=[VMEM],
        out_specs=VMEM,
        name="assemble",
    )(packets)


def per_device(propagator, rising_op, energies, hyb_particle, hyb_hole, sector_sizes):
    states = propagator.shape[2]
    n = lax.axis_size("tx")
    step_size = 1.0 / (n * n)
    rows = states // n
    here_x = lax.axis_index("tx")
    operator = rising_op[0]

    masked, upward = raise_terms(sector_sizes, propagator[0, 0], operator)
    below = shifted(upward, "sector", 1)
    above = shifted(masked, "sector", -1)

    turned, flipped = turn(masked, operator)
    columns = lax.all_to_all(turned.reshape(n, rows, states), "ty", 0, 0, tiled=True)

    own, *away = energy_blocks(
        sector_sizes, hyb_particle, hyb_hole, above, below, operator, flipped, n
    )
    crossed = {d: ring(away[d - 1], "tx", d) for d in (2, 1, 3)}
    crossed = [crossed[d] for d in range(1, n)]
    down, up, across = (ring(own, "ty", d) for d in (1, -1, 2))
    crossed, down, up, across = lax.optimization_barrier((crossed, down, up, across))

    previous_g, next_g, far_first, far_second = relay_gather(columns, "tx")

    rest = jnp.stack(crossed)
    rest_down, rest_up = ring(rest, "ty", 1), ring(rest, "ty", -1)
    rest_late = tied(rest, rest_down, rest_up)
    rest_across = ring(rest_late, "ty", 2)

    entries_g = [
        ("g", 0, 0, columns),
        ("g", -1, 0, previous_g),
        ("g", 1, 0, next_g),
        ("g", 2, 0, far_first),
        ("g", 2, 1, far_second),
    ]
    entries_near = (
        [("e", 0, 0, own)]
        + [("e", -d, 0, crossed[d - 1]) for d in range(1, n)]
        + [("e", 0, 2, down), ("rest", None, 2, rest_down)]
        + [("e", 0, 1, up), ("rest", None, 1, rest_up)]
        + entries_g
    )
    entries_far = [("e", 0, 0, across), ("rest", None, 0, rest_across)] + entries_g
    rates = lax.dynamic_slice_in_dim(energies[0], here_x * rows, rows, 0)[:, None]
    near = convolve_near(entries_near, n)
    packets = convolve_far(entries_far, near, sector_sizes, rates, n, step_size)
    packets = lax.all_to_all(packets, ("tx", "ty"), 0, 0, tiled=True)
    return assemble(packets, n)[None, None]


def solution(mesh):
    n = round(mesh.shape["tm"] ** 0.5)
    split = Mesh(
        np.asarray(mesh.devices).reshape(n, n, mesh.shape["sector"]), ("tx", "ty", "sector")
    )
    times = ("tx", "ty")
    placed = (
        P("sector", times, None, None),
        P("sector", None, None),
        P("sector", None),
        P(times),
        P(times),
        P("sector"),
    )
    return jax.shard_map(
        per_device,
        mesh=split,
        in_specs=placed,
        out_specs=P("sector", times, None, None),
        check_vma=False,
    )
```

```python
import functools

import jax
import jax.numpy as jnp
import numpy as np
from jax import lax
from jax.experimental import pallas as pl
from jax.experimental.pallas import tpu as pltpu
from jax.sharding import Mesh
from jax.sharding import PartitionSpec as P

MIB = 1024 * 1024
VMEM = pl.BlockSpec(memory_space=pltpu.VMEM)
SMEM = pl.BlockSpec(memory_space=pltpu.SMEM)
HBM = pl.BlockSpec(memory_space=pltpu.HBM)
NT = (((1,), (1,)), ((), ()))


def shifted(block, axis, distance):
    devices = range(lax.axis_size(axis))
    route = [(i - distance, i) for i in devices if i - distance in devices]
    return lax.ppermute(block, axis, route)


def ring(block, axis, distance):
    n = lax.axis_size(axis)
    return lax.ppermute(block, axis, [(i, (i + distance) % n) for i in range(n)])


def tied(value, *others):
    return lax.optimization_barrier((value, *others))[0]


def spread(block, axis):
    return [(-d, ring(block, axis, d)) for d in (1, -1, 2)]


def relay_gather(block, axis):
    half = block.shape[0] // 2
    below, above = ring(block, axis, 1), ring(block, axis, -1)
    return below, above, ring(below[:half], axis, 1), ring(above[half:], axis, -1)


def live(shape, size, first_row=0):
    row = lax.broadcasted_iota(jnp.int32, shape, 0) + first_row
    column = lax.broadcasted_iota(jnp.int32, shape, 1)
    return (row < size) & (column < size)


def dot(a, b):
    return jnp.dot(a, b, preferred_element_type=jnp.float32)


def prepare_kernel(sizes, prop, operator, masked, upward, turned, flipped):
    inner = prop[...].astype(jnp.float32)
    inner = jnp.where(live(inner.shape, sizes[0]), inner, 0.0).astype(jnp.bfloat16)
    masked[...] = inner
    r = operator[...]
    raised = dot(r, inner).astype(jnp.bfloat16)
    upward[...] = lax.dot_general(raised, r, NT, preferred_element_type=jnp.float32).astype(
        jnp.bfloat16
    )
    turned[...] = inner.T
    flipped[...] = r.T


def prepare(sizes, prop, operator):
    states = prop.shape[0]
    square = jax.ShapeDtypeStruct((states, states), jnp.bfloat16)
    return pl.pallas_call(
        prepare_kernel,
        out_shape=(square,) * 4,
        in_specs=[SMEM, VMEM, VMEM],
        out_specs=(VMEM,) * 4,
        cost_estimate=pl.CostEstimate(
            flops=4 * states**3, bytes_accessed=12 * states**2, transcendentals=0
        ),
        name="prepare",
    )(sizes, prop, operator)


def energy_kernel(sizes, particle, hole, *refs):
    sources, (*outs,), copies, sems = refs[:4], refs[4:-5], refs[-5:-1], refs[-1]
    moves = [
        pltpu.make_async_copy(src, dst, sems.at[i])
        for i, (src, dst) in enumerate(zip(sources, copies))
    ]
    for move in moves:
        move.start()
    n = len(outs)
    rows = outs[0].shape[0]
    here_x = lax.axis_index("tx")
    for move in moves:
        move.wait()
    flipped, above, operator, below = copies
    inner = above[...]
    r = operator[...]
    for d in (2, 1, 3, 0):
        first = pl.multiple_of(lax.rem(here_x + d, n) * rows, 32)
        lowered = dot(flipped[pl.ds(first, rows), :], inner).astype(jnp.bfloat16)
        downward = dot(lowered, r)
        raised = below[pl.ds(first, rows), :].astype(jnp.float32)
        both = particle[0] * raised + hole[0] * downward
        kept = live(both.shape, sizes[0], first)
        outs[d][...] = jnp.where(kept, both, 0.0).astype(jnp.bfloat16)


def energy_blocks(sizes, particle, hole, above, below, operator, flipped, n):
    states = above.shape[0]
    block = jax.ShapeDtypeStruct((states // n, states), jnp.bfloat16)
    return pl.pallas_call(
        energy_kernel,
        out_shape=(block,) * n,
        in_specs=[SMEM] * 3 + [HBM] * 4,
        out_specs=(VMEM,) * n,
        scratch_shapes=[pltpu.VMEM((states, states), jnp.bfloat16)] * 4
        + [pltpu.SemaphoreType.DMA((4,))],
        cost_estimate=pl.CostEstimate(
            flops=4 * states**3, bytes_accessed=10 * states**2, transcendentals=0
        ),
        name="energy_blocks",
    )(sizes, particle, hole, flipped, above, operator, below)


def around(here, offset, n):
    return lax.rem(here + offset + n, n)


def placed(parts, plan, n, e_all, g_all, pad, sems):
    here_x = lax.axis_index("tx")
    copies = []
    for part, (kind, offset, slot) in zip(parts, plan):
        if kind == "e":
            copies.append((part, e_all.at[slot, around(here_x, offset, n)]))
        elif kind == "rest":
            tall = part.shape[1]
            room = e_all.at[slot, :, pl.ds(offset * tall, tall)]
            for d in range(1, n):
                copies.append((part.at[d - 1], room.at[around(here_x, -d, n)]))
        else:
            some = part.shape[0]
            start = pad + around(here_x, offset, n) * n + slot * some
            copies.append((part, g_all.at[pl.ds(start, some)]))
    moves = [
        pltpu.make_async_copy(src, dst, sems.at[i]) for i, (src, dst) in enumerate(copies)
    ]
    for move in moves:
        move.start()
    return moves


def products(e_all, g_all, slot, source, n, rows):
    for v in range(n * n):
        lane, first = v % n, v // n
        left = e_all[slot, : n - first].reshape((n - first) * rows, -1)
        right = g_all[v - source + n - 1]
        yield lane, first, lax.dot_general(left, right, NT, preferred_element_type=jnp.float32)


def source_of(slot, n):
    return lax.rem(lax.axis_index("ty") + slot + slot // 2, n)


def near_kernel(plan, n, *refs):
    parts = refs[: len(plan)]
    total, e_all, g_all, sems = refs[len(plan) :]
    rows = total.shape[2]
    moves = placed(parts, plan, n, e_all, g_all, n - 1, sems)
    g_all[: n - 1] = jnp.zeros((n - 1, *g_all.shape[1:]), jnp.bfloat16)
    far = n - 1 + n * around(lax.axis_index("tx"), n // 2, n)
    g_all[pl.ds(far, n)] = jnp.zeros((n, *g_all.shape[1:]), jnp.bfloat16)
    for move in moves:
        move.wait()
    for slot in range(n - 1):
        for lane, first, product in products(e_all, g_all, slot, source_of(slot, n), n, rows):
            if slot == 0 and first == 0:
                total[lane] = product
            else:
                total[lane, first * rows :, :] += product


def far_kernel(plan, late, n, step_size, sizes, rates, near, *refs):
    parts = refs[: len(plan)]
    out, e_all, g_all, total, sems = refs[len(plan) :]
    rows = total.shape[2]
    moves = placed(parts, plan, n, e_all, g_all, n - 1, sems)
    g_all[: n - 1] = jnp.zeros((n - 1, *g_all.shape[1:]), jnp.bfloat16)
    here_x, here_y, size = lax.axis_index("tx"), lax.axis_index("ty"), sizes[0]
    for move in moves[:-late]:
        move.wait()
    for lane, first, product in products(
        e_all, g_all, n - 1, lax.rem(here_y + n // 2, n), n, rows
    ):
        if first == 0:
            total[lane, : n * rows] = near[lane] + product
        else:
            total[lane, first * rows : n * rows] += product
    for move in moves[-late:]:
        move.wait()
    far = around(here_x, n // 2, n)
    for slot in range(n - 1):
        left = e_all[slot].reshape(n * rows, -1)
        for k in range(n):
            v = source_of(slot, n) + k
            right = g_all[n - 1 + n * far + k]
            top = pl.multiple_of((far + v // n) * rows, 32)
            total[lax.rem(v, n), pl.ds(top, n * rows)] += lax.dot_general(
                left, right, NT, preferred_element_type=jnp.float32
            )

    quarter = rows // n
    scale = step_size * step_size
    for b in range(n):
        row = lax.broadcasted_iota(jnp.int32, (quarter, rows), 0) + b * quarter
        column = lax.broadcasted_iota(jnp.int32, (quarter, rows), 1)
        starts = (row == column) & (here_x == here_y) & (row + here_x * rows < size)
        rate = rates[b * quarter : (b + 1) * quarter]
        decay = jnp.broadcast_to(jnp.exp(-step_size * rate), (quarter, rows))
        for t in range(n * n):
            top = t // n * rows + b * quarter
            term = scale * total[t % n, top : top + quarter]
            fresh = (jnp.where(starts, 1.0, 0.0) if t == 0 else decay * fresh) - term
            out[t, :, b * rows : (b + 1) * rows] = fresh.astype(jnp.bfloat16)


def copies_of(plan, n):
    return sum(n - 1 if kind == "rest" else 1 for kind, *_ in plan)


def convolve_near(entries, n):
    plan, parts = [e[:3] for e in entries], [e[3] for e in entries]
    rows, states = parts[0].shape
    return pl.pallas_call(
        functools.partial(near_kernel, plan, n),
        out_shape=jax.ShapeDtypeStruct((n, n * rows, rows), jnp.float32),
        in_specs=[HBM] * len(parts),
        out_specs=VMEM,
        scratch_shapes=[
            pltpu.VMEM((n - 1, n, rows, states), jnp.bfloat16),
            pltpu.VMEM((n * n + n - 1, rows, states), jnp.bfloat16),
            pltpu.SemaphoreType.DMA((copies_of(plan, n),)),
        ],
        compiler_params=pltpu.CompilerParams(vmem_limit_bytes=52 * MIB),
        cost_estimate=pl.CostEstimate(
            flops=200 * rows * rows * states,
            bytes_accessed=56 * rows * states,
            transcendentals=0,
        ),
        name="convolve_near",
    )(*parts)


def convolve_far(entries, late_entries, near, sizes, rates, n, step_size):
    plan = [e[:3] for e in entries + late_entries]
    parts = [e[3] for e in entries + late_entries]
    late = copies_of([e[:3] for e in late_entries], n)
    rows, states = parts[0].shape
    return pl.pallas_call(
        functools.partial(far_kernel, plan, late, n, step_size),
        out_shape=jax.ShapeDtypeStruct((n * n, rows // n, states), jnp.bfloat16),
        in_specs=[SMEM, VMEM, VMEM] + [HBM] * len(parts),
        out_specs=VMEM,
        scratch_shapes=[
            pltpu.VMEM((n, n, rows, states), jnp.bfloat16),
            pltpu.VMEM((n * n + n - 1, rows, states), jnp.bfloat16),
            pltpu.VMEM((n, 2 * n * rows, rows), jnp.float32),
            pltpu.SemaphoreType.DMA((copies_of(plan, n),)),
        ],
        compiler_params=pltpu.CompilerParams(vmem_limit_bytes=52 * MIB),
        cost_estimate=pl.CostEstimate(
            flops=130 * rows * rows * states,
            bytes_accessed=80 * rows * states,
            transcendentals=0,
        ),
        name="convolve_far",
    )(sizes, rates, near, *parts)


def assemble_kernel(n, packets, out):
    quarter, states = packets.shape[1:]
    rows = states // n
    for x in range(n):
        for b in range(n):
            out[x * rows + b * quarter : x * rows + (b + 1) * quarter, :] = jnp.concatenate(
                [packets[x * n + y, :, b * rows : (b + 1) * rows] for y in range(n)], axis=1
            )


def assemble(packets, n):
    states = packets.shape[2]
    return pl.pallas_call(
        functools.partial(assemble_kernel, n),
        out_shape=jax.ShapeDtypeStruct((states, states), jnp.bfloat16),
        in_specs=[VMEM],
        out_specs=VMEM,
        name="assemble",
    )(packets)


def per_device(propagator, rising_op, energies, hyb_particle, hyb_hole, sector_sizes):
    states = propagator.shape[2]
    n = lax.axis_size("tx")
    step_size = 1.0 / (n * n)
    rows = states // n
    here_x = lax.axis_index("tx")
    operator = rising_op[0]

    masked, upward, turned, flipped = prepare(sector_sizes, propagator[0, 0], operator)
    below = shifted(upward, "sector", 1)
    above = shifted(masked, "sector", -1)
    columns = lax.all_to_all(turned.reshape(n, rows, states), "ty", 0, 0, tiled=True)

    own, *away = energy_blocks(
        sector_sizes, hyb_particle, hyb_hole, above, below, operator, flipped, n
    )
    crossed = {d: ring(away[d - 1], "tx", d) for d in (2, 1, 3)}
    crossed = [crossed[d] for d in range(1, n)]
    down, up, across = (ring(own, "ty", d) for d in (1, -1, 2))

    previous_g, next_g, far_first, far_second = relay_gather(columns, "tx")

    rest = jnp.stack(crossed)
    half = rows // 2
    rest_down, rest_up = ring(rest, "ty", 1), ring(rest, "ty", -1)
    across_first = ring(rest_down[:, :half], "ty", 1)
    across_second = ring(rest_up[:, half:], "ty", -1)

    near_g = [("g", 0, 0, columns), ("g", -1, 0, previous_g), ("g", 1, 0, next_g)]
    far_g = [("g", 2, 0, far_first), ("g", 2, 1, far_second)]
    near_e = (
        [("e", 0, 0, own)]
        + [("e", -d, 0, crossed[d - 1]) for d in range(1, n)]
        + [("e", 0, 2, down), ("rest", 0, 2, rest_down)]
        + [("e", 0, 1, up), ("rest", 0, 1, rest_up)]
    )
    far_e = [
        ("e", 0, 3, across),
        ("rest", 0, 3, across_first),
        ("rest", 1, 3, across_second),
    ]
    rates = lax.dynamic_slice_in_dim(energies[0], here_x * rows, rows, 0)[:, None]
    near = convolve_near(near_e + near_g, n)
    packets = convolve_far(
        far_e + near_g + far_g, near_e, near, sector_sizes, rates, n, step_size
    )
    packets = lax.all_to_all(packets, ("tx", "ty"), 0, 0, tiled=True)
    return assemble(packets, n)[None, None]


def solution(mesh):
    n = round(mesh.shape["tm"] ** 0.5)
    split = Mesh(
        np.asarray(mesh.devices).reshape(n, n, mesh.shape["sector"]), ("tx", "ty", "sector")
    )
    times = ("tx", "ty")
    placed = (
        P("sector", times, None, None),
        P("sector", None, None),
        P("sector", None),
        P(times),
        P(times),
        P("sector"),
    )
    return jax.shard_map(
        per_device,
        mesh=split,
        in_specs=placed,
        out_specs=P("sector", times, None, None),
        check_vma=False,
    )
```

```python
import functools

import jax
import jax.numpy as jnp
import numpy as np
from jax import lax
from jax.experimental import pallas as pl
from jax.experimental.pallas import tpu as pltpu
from jax.sharding import Mesh
from jax.sharding import PartitionSpec as P

MIB = 1024 * 1024
VMEM = pl.BlockSpec(memory_space=pltpu.VMEM)
SMEM = pl.BlockSpec(memory_space=pltpu.SMEM)
HBM = pl.BlockSpec(memory_space=pltpu.HBM)
NT = (((1,), (1,)), ((), ()))


def shifted(block, axis, distance):
    devices = range(lax.axis_size(axis))
    route = [(i - distance, i) for i in devices if i - distance in devices]
    return lax.ppermute(block, axis, route)


def ring(block, axis, distance):
    n = lax.axis_size(axis)
    return lax.ppermute(block, axis, [(i, (i + distance) % n) for i in range(n)])


def tied(value, *others):
    return lax.optimization_barrier((value, *others))[0]


def spread(block, axis):
    return [(-d, ring(block, axis, d)) for d in (1, -1, 2)]


def live(shape, size, first_row=0):
    row = lax.broadcasted_iota(jnp.int32, shape, 0) + first_row
    column = lax.broadcasted_iota(jnp.int32, shape, 1)
    return (row < size) & (column < size)


def dot(a, b):
    return jnp.dot(a, b, preferred_element_type=jnp.float32)


def prepare_kernel(sizes, prop, operator, masked, upward, turned, flipped):
    inner = prop[...].astype(jnp.float32)
    inner = jnp.where(live(inner.shape, sizes[0]), inner, 0.0).astype(jnp.bfloat16)
    masked[...] = inner
    r = operator[...]
    raised = dot(r, inner).astype(jnp.bfloat16)
    upward[...] = lax.dot_general(raised, r, NT, preferred_element_type=jnp.float32).astype(
        jnp.bfloat16
    )
    turned[...] = inner.T
    flipped[...] = r.T


def prepare(sizes, prop, operator):
    states = prop.shape[0]
    square = jax.ShapeDtypeStruct((states, states), jnp.bfloat16)
    return pl.pallas_call(
        prepare_kernel,
        out_shape=(square,) * 4,
        in_specs=[SMEM, VMEM, VMEM],
        out_specs=(VMEM,) * 4,
        cost_estimate=pl.CostEstimate(
            flops=4 * states**3, bytes_accessed=12 * states**2, transcendentals=0
        ),
        name="prepare",
    )(sizes, prop, operator)


def energy_kernel(sizes, particle, hole, *refs):
    sources, (*outs,), copies, sems = refs[:4], refs[4:-5], refs[-5:-1], refs[-1]
    moves = [
        pltpu.make_async_copy(src, dst, sems.at[i])
        for i, (src, dst) in enumerate(zip(sources, copies))
    ]
    for move in moves:
        move.start()
    n = len(outs)
    rows = outs[0].shape[0]
    here_x = lax.axis_index("tx")
    for move in moves:
        move.wait()
    flipped, above, operator, below = copies
    inner = above[...]
    r = operator[...]
    for d in (2, 1, 3, 0):
        first = pl.multiple_of(lax.rem(here_x + d, n) * rows, 32)
        lowered = dot(flipped[pl.ds(first, rows), :], inner).astype(jnp.bfloat16)
        downward = dot(lowered, r)
        raised = below[pl.ds(first, rows), :].astype(jnp.float32)
        both = particle[0] * raised + hole[0] * downward
        kept = live(both.shape, sizes[0], first)
        outs[d][...] = jnp.where(kept, both, 0.0).astype(jnp.bfloat16)


def energy_blocks(sizes, particle, hole, above, below, operator, flipped, n):
    states = above.shape[0]
    block = jax.ShapeDtypeStruct((states // n, states), jnp.bfloat16)
    return pl.pallas_call(
        energy_kernel,
        out_shape=(block,) * n,
        in_specs=[SMEM] * 3 + [HBM] * 4,
        out_specs=(VMEM,) * n,
        scratch_shapes=[pltpu.VMEM((states, states), jnp.bfloat16)] * 4
        + [pltpu.SemaphoreType.DMA((4,))],
        cost_estimate=pl.CostEstimate(
            flops=4 * states**3, bytes_accessed=10 * states**2, transcendentals=0
        ),
        name="energy_blocks",
    )(sizes, particle, hole, flipped, above, operator, below)


def around(here, offset, n):
    return lax.rem(here + offset + n, n)


def convolve_kernel(plan, n, step_size, sizes, rates, *refs):
    parts = refs[: len(plan)]
    out, e_all, g_all, total, sems = refs[len(plan) :]
    rows, states = g_all.shape[1], e_all.shape[1] // (n * n + 1)
    here_x, here_y, size = lax.axis_index("tx"), lax.axis_index("ty"), sizes[0]
    copies_e, copies_g = [], []

    def lag_room(x, y, top, tall):
        slot = n * n - 1 - (n * around(here_x, x, n) + around(here_y, y, n))
        left = pl.multiple_of(slot * states, 128)
        return e_all.at[pl.ds(top, tall), pl.ds(left, states)]

    for part, (kind, across, step) in zip(parts, plan):
        if kind == "e":
            copies_e.append((part, lag_room(across, step, 0, rows)))
        elif kind == "all":
            tall = part.shape[1]
            for d in range(n):
                copies_e.append((part.at[d], lag_room(-d, step, across * tall, tall)))
        else:
            first = around(here_x, step, n) * (n // 2)
            for k in range(2):
                room = g_all.at[pl.ds(first, n // 2), :, pl.ds(k * states, states)]
                copies_g.append((part.at[:, k], room))
    moves = [
        pltpu.make_async_copy(src, dst, sems.at[i])
        for i, (src, dst) in enumerate(copies_e + copies_g)
    ]
    for move in moves:
        move.start()
    e_all[:, n * n * states :] = jnp.zeros((rows, states), jnp.bfloat16)
    for move in moves:
        move.wait()

    for u in range(0, n * n, 2):
        right = g_all[u // 2]
        for first in range(0, n * n - u, n):
            lags = range(first, min(first + n, n * n - u))
            left = jnp.concatenate(
                [
                    e_all[:, (n * n - 1 - lag) * states : (n * n + 1 - lag) * states]
                    for lag in lags
                ],
                axis=0,
            )
            product = lax.dot_general(left, right, NT, preferred_element_type=jnp.float32)
            where = slice((u + lags[0]) * rows, (u + lags[-1] + 1) * rows)
            if u == 0:
                total[where] = product
            else:
                total[where] += product

    quarter = rows // n
    scale = step_size * step_size
    for b in range(n):
        row = lax.broadcasted_iota(jnp.int32, (quarter, rows), 0) + b * quarter
        column = lax.broadcasted_iota(jnp.int32, (quarter, rows), 1)
        starts = (row == column) & (here_x == here_y) & (row + here_x * rows < size)
        rate = rates[b * quarter : (b + 1) * quarter]
        decay = jnp.broadcast_to(jnp.exp(-step_size * rate), (quarter, rows))
        for t in range(n * n):
            term = scale * total[t * rows + b * quarter : t * rows + (b + 1) * quarter]
            fresh = (jnp.where(starts, 1.0, 0.0) if t == 0 else decay * fresh) - term
            out[t, :, b * rows : (b + 1) * rows] = fresh.astype(jnp.bfloat16)


def convolve(entries, sizes, rates, n, step_size):
    plan, parts = [e[:3] for e in entries], [e[3] for e in entries]
    rows, states = parts[0].shape
    copies = sum({"e": 1, "all": n, "g": 2}[kind] for kind, *_ in plan)
    return pl.pallas_call(
        functools.partial(convolve_kernel, plan, n, step_size),
        out_shape=jax.ShapeDtypeStruct((n * n, rows // n, states), jnp.bfloat16),
        in_specs=[SMEM, VMEM] + [HBM] * len(parts),
        out_specs=VMEM,
        scratch_shapes=[
            pltpu.VMEM((rows, (n * n + 1) * states), jnp.bfloat16),
            pltpu.VMEM((n * n // 2, rows, 2 * states), jnp.bfloat16),
            pltpu.VMEM((n * n * rows, rows), jnp.float32),
            pltpu.SemaphoreType.DMA((copies,)),
        ],
        compiler_params=pltpu.CompilerParams(vmem_limit_bytes=52 * MIB),
        cost_estimate=pl.CostEstimate(
            flops=n * n * (n * n + 1) * rows * rows * states,
            bytes_accessed=4 * n * n * rows * states,
            transcendentals=0,
        ),
        name="convolve",
    )(sizes, rates, *parts)


def assemble_kernel(n, packets, out):
    quarter, states = packets.shape[1:]
    rows = states // n
    for x in range(n):
        for b in range(n):
            out[x * rows + b * quarter : x * rows + (b + 1) * quarter, :] = jnp.concatenate(
                [packets[x * n + y, :, b * rows : (b + 1) * rows] for y in range(n)], axis=1
            )


def assemble(packets, n):
    states = packets.shape[2]
    return pl.pallas_call(
        functools.partial(assemble_kernel, n),
        out_shape=jax.ShapeDtypeStruct((states, states), jnp.bfloat16),
        in_specs=[VMEM],
        out_specs=VMEM,
        name="assemble",
    )(packets)


def per_device(propagator, rising_op, energies, hyb_particle, hyb_hole, sector_sizes):
    states = propagator.shape[2]
    n = lax.axis_size("tx")
    step_size = 1.0 / (n * n)
    rows = states // n
    here_x = lax.axis_index("tx")
    operator = rising_op[0]

    masked, upward, turned, flipped = prepare(sector_sizes, propagator[0, 0], operator)
    below = shifted(upward, "sector", 1)
    above = shifted(masked, "sector", -1)
    columns = lax.all_to_all(turned.reshape(n, rows, states), "ty", 0, 0, tiled=True)

    own, *away = energy_blocks(
        sector_sizes, hyb_particle, hyb_hole, above, below, operator, flipped, n
    )
    away, columns = lax.optimization_barrier((away, columns))
    crossed = {d: ring(away[d - 1], "tx", d) for d in (2, 1, 3)}
    crossed = [crossed[d] for d in range(1, n)]
    gathered = [(0, columns)] + [(-d, ring(columns, "tx", d)) for d in (1, -1, 2)]

    lines = jnp.stack([own] + crossed)
    half = rows // 2
    down, up = ring(lines, "ty", 1), ring(lines, "ty", -1)
    down, up, *nearest = lax.optimization_barrier((down, up, gathered[1][1], gathered[2][1]))
    gathered[1:3] = [(gathered[1][0], nearest[0]), (gathered[2][0], nearest[1])]
    across_first = ring(down[:, :half], "ty", 1)
    across_second = ring(up[:, half:], "ty", -1)

    entries = (
        [("e", 0, 0, own)]
        + [("e", -d, 0, crossed[d - 1]) for d in range(1, n)]
        + [("all", 0, -1, down), ("all", 0, 1, up)]
        + [("all", 0, 2, across_first), ("all", 1, 2, across_second)]
        + [("g", 0, step, g.reshape(n // 2, 2, rows, states)) for step, g in gathered]
    )
    rates = lax.dynamic_slice_in_dim(energies[0], here_x * rows, rows, 0)[:, None]
    packets = convolve(entries, sector_sizes, rates, n, step_size)
    packets = lax.all_to_all(packets, ("tx", "ty"), 0, 0, tiled=True)
    return assemble(packets, n)[None, None]


def solution(mesh):
    n = round(mesh.shape["tm"] ** 0.5)
    split = Mesh(
        np.asarray(mesh.devices).reshape(n, n, mesh.shape["sector"]), ("tx", "ty", "sector")
    )
    times = ("tx", "ty")
    placed = (
        P("sector", times, None, None),
        P("sector", None, None),
        P("sector", None),
        P(times),
        P(times),
        P("sector"),
    )
    return jax.shard_map(
        per_device,
        mesh=split,
        in_specs=placed,
        out_specs=P("sector", times, None, None),
        check_vma=False,
    )
```

```python
import functools

import jax
import jax.numpy as jnp
import numpy as np
from jax import lax
from jax.experimental import pallas as pl
from jax.experimental.pallas import tpu as pltpu
from jax.sharding import Mesh
from jax.sharding import PartitionSpec as P

MIB = 1024 * 1024
VMEM = pl.BlockSpec(memory_space=pltpu.VMEM)
SMEM = pl.BlockSpec(memory_space=pltpu.SMEM)
HBM = pl.BlockSpec(memory_space=pltpu.HBM)
NT = (((1,), (1,)), ((), ()))


def shifted(block, axis, distance):
    devices = range(lax.axis_size(axis))
    route = [(i - distance, i) for i in devices if i - distance in devices]
    return lax.ppermute(block, axis, route)


def ring(block, axis, distance):
    n = lax.axis_size(axis)
    return lax.ppermute(block, axis, [(i, (i + distance) % n) for i in range(n)])


def turn_sign():
    return 1 - 2 * lax.rem(lax.axis_index("sector"), 2)


def turned_ring(block, axis, distance):
    n, sectors = lax.axis_size(axis), lax.axis_size("sector")
    route = []
    for i in range(n):
        for s in range(sectors):
            step = distance if s % 2 == 0 else -distance
            route.append((i * sectors + s, (i + step) % n * sectors + s))
    return lax.ppermute(block, (axis, "sector"), route)


def ring_gather(block, axis):
    before = turned_ring(block, axis, 1)
    after = turned_ring(block, axis, -1)
    return [(0, block), (-1, before), (1, after), (2, turned_ring(before, axis, 1))]


def live(shape, size, first_row=0):
    row = lax.broadcasted_iota(jnp.int32, shape, 0) + first_row
    column = lax.broadcasted_iota(jnp.int32, shape, 1)
    return (row < size) & (column < size)


def dot(a, b):
    return jnp.dot(a, b, preferred_element_type=jnp.float32)


def prepare_kernel(sizes, prop, operator, masked, upward, flipped, *refs):
    *turned, staged = refs
    n = len(turned)
    rows = turned[0].shape[0]
    inner = prop[...].astype(jnp.float32)
    inner = jnp.where(live(inner.shape, sizes[0]), inner, 0.0).astype(jnp.bfloat16)
    masked[...] = inner
    r = operator[...]
    raised = dot(r, inner).astype(jnp.bfloat16)
    upward[...] = lax.dot_general(raised, r, NT, preferred_element_type=jnp.float32).astype(
        jnp.bfloat16
    )
    staged[...] = inner.T
    here_y = lax.axis_index("ty")
    for d in range(n):
        first = pl.multiple_of(lax.rem(here_y + d, n) * rows, 32)
        turned[d][...] = staged[pl.ds(first, rows), :]
    flipped[...] = r.T


def prepare(sizes, prop, operator, n):
    states = prop.shape[0]
    square = jax.ShapeDtypeStruct((states, states), jnp.bfloat16)
    block = jax.ShapeDtypeStruct((states // n, states), jnp.bfloat16)
    return pl.pallas_call(
        prepare_kernel,
        out_shape=(square,) * 3 + (block,) * n,
        in_specs=[SMEM, VMEM, VMEM],
        out_specs=(VMEM,) * (3 + n),
        scratch_shapes=[pltpu.VMEM((states, states), jnp.bfloat16)],
        cost_estimate=pl.CostEstimate(
            flops=4 * states**3, bytes_accessed=12 * states**2, transcendentals=0
        ),
        name="prepare",
    )(sizes, prop, operator)


def energy_kernel(sizes, particle, hole, *refs):
    sources, (*outs,), copies, sems = refs[:4], refs[4:-5], refs[-5:-1], refs[-1]
    moves = [
        pltpu.make_async_copy(src, dst, sems.at[i])
        for i, (src, dst) in enumerate(zip(sources, copies))
    ]
    for move in moves:
        move.start()
    n = len(outs)
    rows = outs[0].shape[0]
    here_x = lax.axis_index("tx")
    for move in moves:
        move.wait()
    flipped, above, operator, below = copies
    inner = above[...]
    r = operator[...]
    for d in (2, 1, 3, 0):
        first = pl.multiple_of(lax.rem(here_x + d, n) * rows, 32)
        lowered = dot(flipped[pl.ds(first, rows), :], inner).astype(jnp.bfloat16)
        downward = dot(lowered, r)
        raised = below[pl.ds(first, rows), :].astype(jnp.float32)
        both = particle[0] * raised + hole[0] * downward
        kept = live(both.shape, sizes[0], first)
        outs[d][...] = jnp.where(kept, both, 0.0).astype(jnp.bfloat16)


def energy_blocks(sizes, particle, hole, above, below, operator, flipped, n):
    states = above.shape[0]
    block = jax.ShapeDtypeStruct((states // n, states), jnp.bfloat16)
    return pl.pallas_call(
        energy_kernel,
        out_shape=(block,) * n,
        in_specs=[SMEM] * 3 + [HBM] * 4,
        out_specs=(VMEM,) * n,
        scratch_shapes=[pltpu.VMEM((states, states), jnp.bfloat16)] * 4
        + [pltpu.SemaphoreType.DMA((4,))],
        cost_estimate=pl.CostEstimate(
            flops=4 * states**3, bytes_accessed=10 * states**2, transcendentals=0
        ),
        name="energy_blocks",
    )(sizes, particle, hole, flipped, above, operator, below)


def around(here, offset, n):
    return lax.rem(here + offset + n, n)


def convolve_kernel(plan, n, step_size, sizes, rates, *refs):
    parts = refs[: len(plan)]
    out, e_all, g_all, total, sems = refs[len(plan) :]
    rows, states = g_all.shape[1], e_all.shape[1] // (n * n + 1)
    here_x, here_y, size = lax.axis_index("tx"), lax.axis_index("ty"), sizes[0]
    sign = turn_sign()
    copies_e, copies_g = [], []
    for part, (kind, step) in zip(parts, plan):
        for d in range(n):
            if kind == "e":
                lag = n * around(here_x, -d, n) + around(here_y, sign * step, n)
                left = pl.multiple_of((n * n - 1 - lag) * states, 128)
                copies_e.append((part.at[d], e_all.at[:, pl.ds(left, states)]))
            else:
                u = n * around(here_x, sign * step, n) + around(here_y, -d, n)
                left = pl.multiple_of(lax.rem(u, 2) * states, 128)
                copies_g.append((part.at[d], g_all.at[u // 2, :, pl.ds(left, states)]))
    moves = [
        pltpu.make_async_copy(src, dst, sems.at[i])
        for i, (src, dst) in enumerate(copies_e + copies_g)
    ]
    for move in moves:
        move.start()
    e_all[:, n * n * states :] = jnp.zeros((rows, states), jnp.bfloat16)
    for move in moves:
        move.wait()

    for u in range(0, n * n, 2):
        right = g_all[u // 2]
        for first in range(0, n * n - u, n):
            lags = range(first, min(first + n, n * n - u))
            left = jnp.concatenate(
                [
                    e_all[:, (n * n - 1 - lag) * states : (n * n + 1 - lag) * states]
                    for lag in lags
                ],
                axis=0,
            )
            product = lax.dot_general(left, right, NT, preferred_element_type=jnp.float32)
            where = slice((u + lags[0]) * rows, (u + lags[-1] + 1) * rows)
            if u == 0:
                total[where] = product
            else:
                total[where] += product

    quarter = rows // n
    scale = step_size * step_size
    for b in range(n):
        row = lax.broadcasted_iota(jnp.int32, (quarter, rows), 0) + b * quarter
        column = lax.broadcasted_iota(jnp.int32, (quarter, rows), 1)
        starts = (row == column) & (here_x == here_y) & (row + here_x * rows < size)
        rate = rates[b * quarter : (b + 1) * quarter]
        decay = jnp.broadcast_to(jnp.exp(-step_size * rate), (quarter, rows))
        for t in range(n * n):
            term = scale * total[t * rows + b * quarter : t * rows + (b + 1) * quarter]
            fresh = (jnp.where(starts, 1.0, 0.0) if t == 0 else decay * fresh) - term
            out[t, :, b * rows : (b + 1) * rows] = fresh.astype(jnp.bfloat16)


def convolve(entries, sizes, rates, n, step_size):
    plan, parts = [e[:2] for e in entries], [e[2] for e in entries]
    _, rows, states = parts[0].shape
    copies = n * len(parts)
    return pl.pallas_call(
        functools.partial(convolve_kernel, plan, n, step_size),
        out_shape=jax.ShapeDtypeStruct((n * n, rows // n, states), jnp.bfloat16),
        in_specs=[SMEM, VMEM] + [HBM] * len(parts),
        out_specs=VMEM,
        scratch_shapes=[
            pltpu.VMEM((rows, (n * n + 1) * states), jnp.bfloat16),
            pltpu.VMEM((n * n // 2, rows, 2 * states), jnp.bfloat16),
            pltpu.VMEM((n * n * rows, rows), jnp.float32),
            pltpu.SemaphoreType.DMA((copies,)),
        ],
        compiler_params=pltpu.CompilerParams(vmem_limit_bytes=52 * MIB),
        cost_estimate=pl.CostEstimate(
            flops=n * n * (n * n + 1) * rows * rows * states,
            bytes_accessed=4 * n * n * rows * states,
            transcendentals=0,
        ),
        name="convolve",
    )(sizes, rates, *parts)


def assemble_kernel(n, packets, out):
    quarter, states = packets.shape[1:]
    rows = states // n
    for x in range(n):
        for b in range(n):
            out[x * rows + b * quarter : x * rows + (b + 1) * quarter, :] = jnp.concatenate(
                [packets[x * n + y, :, b * rows : (b + 1) * rows] for y in range(n)], axis=1
            )


def assemble(packets, n):
    states = packets.shape[2]
    return pl.pallas_call(
        functools.partial(assemble_kernel, n),
        out_shape=jax.ShapeDtypeStruct((states, states), jnp.bfloat16),
        in_specs=[VMEM],
        out_specs=VMEM,
        name="assemble",
    )(packets)


def per_device(propagator, rising_op, energies, hyb_particle, hyb_hole, sector_sizes):
    states = propagator.shape[2]
    n = lax.axis_size("tx")
    step_size = 1.0 / (n * n)
    rows = states // n
    here_x = lax.axis_index("tx")
    operator = rising_op[0]

    masked, upward, flipped, own_g, *away_g = prepare(
        sector_sizes, propagator[0, 0], operator, n
    )
    below = shifted(upward, "sector", 1)
    above = shifted(masked, "sector", -1)
    crossed_g = {d: ring(away_g[d - 1], "ty", d) for d in (2, 1, 3)}
    columns = jnp.stack([own_g] + [crossed_g[d] for d in range(1, n)])

    own_e, *away_e = energy_blocks(
        sector_sizes, hyb_particle, hyb_hole, above, below, operator, flipped, n
    )
    crossed_e = {d: ring(away_e[d - 1], "tx", d) for d in (2, 1, 3)}
    lines = jnp.stack([own_e] + [crossed_e[d] for d in range(1, n)])

    entries = [("g", step, part) for step, part in ring_gather(columns, "tx")]
    entries = [("e", step, part) for step, part in ring_gather(lines, "ty")] + entries
    rates = lax.dynamic_slice_in_dim(energies[0], here_x * rows, rows, 0)[:, None]
    packets = convolve(entries, sector_sizes, rates, n, step_size)
    packets = lax.all_to_all(packets, ("tx", "ty"), 0, 0, tiled=True)
    return assemble(packets, n)[None, None]


def solution(mesh):
    n = round(mesh.shape["tm"] ** 0.5)
    split = Mesh(
        np.asarray(mesh.devices).reshape(n, n, mesh.shape["sector"]), ("tx", "ty", "sector")
    )
    times = ("tx", "ty")
    placed = (
        P("sector", times, None, None),
        P("sector", None, None),
        P("sector", None),
        P(times),
        P(times),
        P("sector"),
    )
    return jax.shard_map(
        per_device,
        mesh=split,
        in_specs=placed,
        out_specs=P("sector", times, None, None),
        check_vma=False,
    )
```

```python
import functools

import jax
import jax.numpy as jnp
import numpy as np
from jax import lax
from jax.experimental import pallas as pl
from jax.experimental.pallas import tpu as pltpu
from jax.sharding import Mesh
from jax.sharding import PartitionSpec as P

MIB = 1024 * 1024
VMEM = pl.BlockSpec(memory_space=pltpu.VMEM)
SMEM = pl.BlockSpec(memory_space=pltpu.SMEM)
HBM = pl.BlockSpec(memory_space=pltpu.HBM)
NT = (((1,), (1,)), ((), ()))


def shifted(block, axis, distance):
    devices = range(lax.axis_size(axis))
    route = [(i - distance, i) for i in devices if i - distance in devices]
    return lax.ppermute(block, axis, route)


def ring(block, axis, distance):
    n = lax.axis_size(axis)
    return lax.ppermute(block, axis, [(i, (i + distance) % n) for i in range(n)])


def tied(value, *others):
    return lax.optimization_barrier((value, *others))[0]


def turn_sign():
    return 1 - 2 * lax.rem(lax.axis_index("sector"), 2)


def turned_ring(block, axis, distance):
    n, sectors = lax.axis_size(axis), lax.axis_size("sector")
    route = []
    for i in range(n):
        for s in range(sectors):
            step = distance if s % 2 == 0 else -distance
            route.append((i * sectors + s, (i + step) % n * sectors + s))
    return lax.ppermute(block, (axis, "sector"), route)


def live(shape, size, first_row=0):
    row = lax.broadcasted_iota(jnp.int32, shape, 0) + first_row
    column = lax.broadcasted_iota(jnp.int32, shape, 1)
    return (row < size) & (column < size)


def dot(a, b):
    return jnp.dot(a, b, preferred_element_type=jnp.float32)


def prepare_kernel(sizes, prop, operator, masked, upward, flipped, *refs):
    *turned, staged = refs
    n = len(turned)
    rows = turned[0].shape[0]
    inner = prop[...].astype(jnp.float32)
    inner = jnp.where(live(inner.shape, sizes[0]), inner, 0.0).astype(jnp.bfloat16)
    masked[...] = inner
    r = operator[...]
    raised = dot(r, inner).astype(jnp.bfloat16)
    upward[...] = lax.dot_general(raised, r, NT, preferred_element_type=jnp.float32).astype(
        jnp.bfloat16
    )
    staged[...] = inner.T
    here_y = lax.axis_index("ty")
    for d in range(n):
        first = pl.multiple_of(lax.rem(here_y + d, n) * rows, 32)
        turned[d][...] = staged[pl.ds(first, rows), :]
    flipped[...] = r.T


def prepare(sizes, prop, operator, n):
    states = prop.shape[0]
    square = jax.ShapeDtypeStruct((states, states), jnp.bfloat16)
    block = jax.ShapeDtypeStruct((states // n, states), jnp.bfloat16)
    return pl.pallas_call(
        prepare_kernel,
        out_shape=(square,) * 3 + (block,) * n,
        in_specs=[SMEM, VMEM, VMEM],
        out_specs=(VMEM,) * (3 + n),
        scratch_shapes=[pltpu.VMEM((states, states), jnp.bfloat16)],
        cost_estimate=pl.CostEstimate(
            flops=4 * states**3, bytes_accessed=12 * states**2, transcendentals=0
        ),
        name="prepare",
    )(sizes, prop, operator)


def energy_kernel(sizes, particle, hole, *refs):
    sources, (*outs,), copies, sems = refs[:4], refs[4:-5], refs[-5:-1], refs[-1]
    moves = [
        pltpu.make_async_copy(src, dst, sems.at[i])
        for i, (src, dst) in enumerate(zip(sources, copies))
    ]
    for move in moves:
        move.start()
    n = len(outs)
    rows = outs[0].shape[0]
    here_x = lax.axis_index("tx")
    for move in moves:
        move.wait()
    flipped, above, operator, below = copies
    inner = above[...]
    r = operator[...]
    for d in (2, 1, 3, 0):
        first = pl.multiple_of(lax.rem(here_x + d, n) * rows, 32)
        lowered = dot(flipped[pl.ds(first, rows), :], inner).astype(jnp.bfloat16)
        downward = dot(lowered, r)
        raised = below[pl.ds(first, rows), :].astype(jnp.float32)
        both = particle[0] * raised + hole[0] * downward
        kept = live(both.shape, sizes[0], first)
        outs[d][...] = jnp.where(kept, both, 0.0).astype(jnp.bfloat16)


def energy_blocks(sizes, particle, hole, above, below, operator, flipped, n):
    states = above.shape[0]
    block = jax.ShapeDtypeStruct((states // n, states), jnp.bfloat16)
    return pl.pallas_call(
        energy_kernel,
        out_shape=(block,) * n,
        in_specs=[SMEM] * 3 + [HBM] * 4,
        out_specs=(VMEM,) * n,
        scratch_shapes=[pltpu.VMEM((states, states), jnp.bfloat16)] * 4
        + [pltpu.SemaphoreType.DMA((4,))],
        cost_estimate=pl.CostEstimate(
            flops=4 * states**3, bytes_accessed=10 * states**2, transcendentals=0
        ),
        compiler_params=pltpu.CompilerParams(vmem_limit_bytes=56 * MIB),
        name="energy_blocks",
    )(sizes, particle, hole, flipped, above, operator, below)


def around(here, offset, n):
    return lax.rem(here + offset + n, n)


def convolve_kernel(plan, n, step_size, sizes, rates, *refs):
    parts = refs[: len(plan)]
    out, e_all, g_all, total, sems = refs[len(plan) :]
    rows, states = g_all.shape[1], e_all.shape[1] // (n * n + 1)
    here_x, here_y, size = lax.axis_index("tx"), lax.axis_index("ty"), sizes[0]
    sign = turn_sign()
    copies_e, copies_g = [], []
    for part, (kind, step) in zip(parts, plan):
        for d in range(n):
            if kind == "e":
                lag = n * around(here_x, -d, n) + around(here_y, sign * step, n)
                left = pl.multiple_of((n * n - 1 - lag) * states, 128)
                copies_e.append((part.at[d], e_all.at[:, pl.ds(left, states)]))
            else:
                u = n * around(here_x, sign * step, n) + around(here_y, -d, n)
                left = pl.multiple_of(lax.rem(u, 2) * states, 128)
                copies_g.append((part.at[d], g_all.at[u // 2, :, pl.ds(left, states)]))
    moves = [
        pltpu.make_async_copy(src, dst, sems.at[i])
        for i, (src, dst) in enumerate(copies_e + copies_g)
    ]
    for move in moves:
        move.start()
    e_all[:, n * n * states :] = jnp.zeros((rows, states), jnp.bfloat16)
    for move in moves:
        move.wait()

    for u in range(0, n * n, 2):
        right = g_all[u // 2]
        for first in range(0, n * n - u, n):
            lags = range(first, min(first + n, n * n - u))
            left = jnp.concatenate(
                [
                    e_all[:, (n * n - 1 - lag) * states : (n * n + 1 - lag) * states]
                    for lag in lags
                ],
                axis=0,
            )
            product = lax.dot_general(left, right, NT, preferred_element_type=jnp.float32)
            where = slice((u + lags[0]) * rows, (u + lags[-1] + 1) * rows)
            if u == 0:
                total[where] = product
            else:
                total[where] += product

    quarter = rows // n
    scale = step_size * step_size
    for b in range(n):
        row = lax.broadcasted_iota(jnp.int32, (quarter, rows), 0) + b * quarter
        column = lax.broadcasted_iota(jnp.int32, (quarter, rows), 1)
        starts = (row == column) & (here_x == here_y) & (row + here_x * rows < size)
        rate = rates[b * quarter : (b + 1) * quarter]
        decay = jnp.broadcast_to(jnp.exp(-step_size * rate), (quarter, rows))
        for t in range(n * n):
            term = scale * total[t * rows + b * quarter : t * rows + (b + 1) * quarter]
            fresh = (jnp.where(starts, 1.0, 0.0) if t == 0 else decay * fresh) - term
            out[t, :, b * rows : (b + 1) * rows] = fresh.astype(jnp.bfloat16)


def convolve(entries, sizes, rates, n, step_size):
    plan, parts = [e[:2] for e in entries], [e[2] for e in entries]
    _, rows, states = parts[0].shape
    copies = n * len(parts)
    return pl.pallas_call(
        functools.partial(convolve_kernel, plan, n, step_size),
        out_shape=jax.ShapeDtypeStruct((n * n, rows // n, states), jnp.bfloat16),
        in_specs=[SMEM, VMEM] + [HBM] * len(parts),
        out_specs=VMEM,
        scratch_shapes=[
            pltpu.VMEM((rows, (n * n + 1) * states), jnp.bfloat16),
            pltpu.VMEM((n * n // 2, rows, 2 * states), jnp.bfloat16),
            pltpu.VMEM((n * n * rows, rows), jnp.float32),
            pltpu.SemaphoreType.DMA((copies,)),
        ],
        compiler_params=pltpu.CompilerParams(vmem_limit_bytes=52 * MIB),
        cost_estimate=pl.CostEstimate(
            flops=n * n * (n * n + 1) * rows * rows * states,
            bytes_accessed=4 * n * n * rows * states,
            transcendentals=0,
        ),
        name="convolve",
    )(sizes, rates, *parts)


def assemble_kernel(n, packets, out):
    quarter, states = packets.shape[1:]
    rows = states // n
    for b in range(n):
        out[b * quarter : (b + 1) * quarter, :] = jnp.concatenate(
            [packets[y, :, b * rows : (b + 1) * rows] for y in range(n)], axis=1
        )


def assemble(packets, n):
    quarter, states = packets.shape[1:]
    return pl.pallas_call(
        functools.partial(assemble_kernel, n),
        out_shape=jax.ShapeDtypeStruct((states, states), jnp.bfloat16),
        grid=(n,),
        in_specs=[pl.BlockSpec((n, quarter, states), lambda x: (x, 0, 0))],
        out_specs=pl.BlockSpec((states // n, states), lambda x: (x, 0)),
        name="assemble",
    )(packets)


def per_device(propagator, rising_op, energies, hyb_particle, hyb_hole, sector_sizes):
    states = propagator.shape[2]
    n = lax.axis_size("tx")
    step_size = 1.0 / (n * n)
    rows = states // n
    here_x = lax.axis_index("tx")
    operator = rising_op[0]

    masked, upward, flipped, own_g, *away_g = prepare(
        sector_sizes, propagator[0, 0], operator, n
    )
    below = shifted(upward, "sector", 1)
    above = shifted(masked, "sector", -1)
    crossed_g = {d: ring(away_g[d - 1], "ty", d) for d in (2, 1, 3)}
    columns = jnp.stack([own_g] + [crossed_g[d] for d in range(1, n)])

    own_e, *away_e = energy_blocks(
        sector_sizes, hyb_particle, hyb_hole, above, below, operator, flipped, n
    )
    crossed_e = {d: ring(away_e[d - 1], "tx", d) for d in (2, 1, 3)}
    lines = jnp.stack([own_e] + [crossed_e[d] for d in range(1, n)])

    before_g = turned_ring(columns, "tx", 1)
    before_e = turned_ring(lines, "ty", 1)
    after_g = turned_ring(tied(columns, lines), "tx", -1)
    after_e = turned_ring(tied(lines, before_g), "ty", -1)
    far_g = turned_ring(before_g, "tx", 1)
    far_e = turned_ring(before_e, "ty", 1)
    entries = [
        (kind, step, part)
        for kind, parts in (
            ("e", (lines, before_e, after_e, far_e)),
            ("g", (columns, before_g, after_g, far_g)),
        )
        for step, part in zip((0, -1, 1, 2), parts)
    ]
    rates = lax.dynamic_slice_in_dim(energies[0], here_x * rows, rows, 0)[:, None]
    packets = convolve(entries, sector_sizes, rates, n, step_size)
    packets = lax.all_to_all(packets, ("tx", "ty"), 0, 0, tiled=True)
    return assemble(packets, n)[None, None]


def solution(mesh):
    n = round(mesh.shape["tm"] ** 0.5)
    split = Mesh(
        np.asarray(mesh.devices).reshape(n, n, mesh.shape["sector"]), ("tx", "ty", "sector")
    )
    times = ("tx", "ty")
    placed = (
        P("sector", times, None, None),
        P("sector", None, None),
        P("sector", None),
        P(times),
        P(times),
        P("sector"),
    )
    return jax.shard_map(
        per_device,
        mesh=split,
        in_specs=placed,
        out_specs=P("sector", times, None, None),
        check_vma=False,
    )
```

```python
import functools

import jax
import jax.numpy as jnp
import numpy as np
from jax import lax
from jax.experimental import pallas as pl
from jax.experimental.pallas import tpu as pltpu
from jax.sharding import Mesh
from jax.sharding import PartitionSpec as P

MIB = 1024 * 1024
VMEM = pl.BlockSpec(memory_space=pltpu.VMEM)
SMEM = pl.BlockSpec(memory_space=pltpu.SMEM)
HBM = pl.BlockSpec(memory_space=pltpu.HBM)
NT = (((1,), (1,)), ((), ()))


def shifted(block, axis, distance):
    devices = range(lax.axis_size(axis))
    route = [(i - distance, i) for i in devices if i - distance in devices]
    return lax.ppermute(block, axis, route)


def ring(block, axis, distance):
    n = lax.axis_size(axis)
    return lax.ppermute(block, axis, [(i, (i + distance) % n) for i in range(n)])


def tied(value, *others):
    return lax.optimization_barrier((value, *others))[0]


def turn_sign():
    return 1 - 2 * lax.rem(lax.axis_index("sector"), 2)


def turned_ring(block, axis, distance):
    n, sectors = lax.axis_size(axis), lax.axis_size("sector")
    route = []
    for i in range(n):
        for s in range(sectors):
            step = distance if s % 2 == 0 else -distance
            route.append((i * sectors + s, (i + step) % n * sectors + s))
    return lax.ppermute(block, (axis, "sector"), route)


def live(shape, size, first_row=0):
    row = lax.broadcasted_iota(jnp.int32, shape, 0) + first_row
    column = lax.broadcasted_iota(jnp.int32, shape, 1)
    return (row < size) & (column < size)


def dot(a, b):
    return jnp.dot(a, b, preferred_element_type=jnp.float32)


def prepare_kernel(sizes, prop, operator, masked, upward, flipped, *refs):
    *turned, staged = refs
    n = len(turned)
    rows = turned[0].shape[0]
    inner = prop[...].astype(jnp.float32)
    inner = jnp.where(live(inner.shape, sizes[0]), inner, 0.0).astype(jnp.bfloat16)
    masked[...] = inner
    r = operator[...]
    raised = dot(r, inner).astype(jnp.bfloat16)
    upward[...] = lax.dot_general(raised, r, NT, preferred_element_type=jnp.float32).astype(
        jnp.bfloat16
    )
    staged[...] = inner.T
    here_y = lax.axis_index("ty")
    for d in range(n):
        first = pl.multiple_of(lax.rem(here_y + d, n) * rows, 32)
        turned[d][...] = staged[pl.ds(first, rows), :]
    flipped[...] = r.T


def prepare(sizes, prop, operator, n):
    states = prop.shape[0]
    square = jax.ShapeDtypeStruct((states, states), jnp.bfloat16)
    block = jax.ShapeDtypeStruct((states // n, states), jnp.bfloat16)
    return pl.pallas_call(
        prepare_kernel,
        out_shape=(square,) * 3 + (block,) * n,
        in_specs=[SMEM, VMEM, VMEM],
        out_specs=(VMEM,) * (3 + n),
        scratch_shapes=[pltpu.VMEM((states, states), jnp.bfloat16)],
        cost_estimate=pl.CostEstimate(
            flops=4 * states**3, bytes_accessed=12 * states**2, transcendentals=0
        ),
        name="prepare",
    )(sizes, prop, operator)


def energy_kernel(sizes, particle, hole, *refs):
    sources, (*outs,), copies, sems = refs[:4], refs[4:-5], refs[-5:-1], refs[-1]
    moves = [
        pltpu.make_async_copy(src, dst, sems.at[i])
        for i, (src, dst) in enumerate(zip(sources, copies))
    ]
    for move in moves:
        move.start()
    n = len(outs)
    rows = outs[0].shape[0]
    here_x = lax.axis_index("tx")
    for move in moves:
        move.wait()
    flipped, above, operator, below = copies
    inner = above[...]
    r = operator[...]
    for d in (2, 1, 3, 0):
        first = pl.multiple_of(lax.rem(here_x + d, n) * rows, 32)
        lowered = dot(flipped[pl.ds(first, rows), :], inner).astype(jnp.bfloat16)
        downward = dot(lowered, r)
        raised = below[pl.ds(first, rows), :].astype(jnp.float32)
        both = particle[0] * raised + hole[0] * downward
        kept = live(both.shape, sizes[0], first)
        outs[d][...] = jnp.where(kept, both, 0.0).astype(jnp.bfloat16)


def energy_blocks(sizes, particle, hole, above, below, operator, flipped, n):
    states = above.shape[0]
    block = jax.ShapeDtypeStruct((states // n, states), jnp.bfloat16)
    return pl.pallas_call(
        energy_kernel,
        out_shape=(block,) * n,
        in_specs=[SMEM] * 3 + [HBM] * 4,
        out_specs=(VMEM,) * n,
        scratch_shapes=[pltpu.VMEM((states, states), jnp.bfloat16)] * 4
        + [pltpu.SemaphoreType.DMA((4,))],
        cost_estimate=pl.CostEstimate(
            flops=4 * states**3, bytes_accessed=10 * states**2, transcendentals=0
        ),
        compiler_params=pltpu.CompilerParams(vmem_limit_bytes=56 * MIB),
        name="energy_blocks",
    )(sizes, particle, hole, flipped, above, operator, below)


def around(here, offset, n):
    return lax.rem(here + offset + n, n)


def convolve_kernel(plan, n, step_size, sizes, rates, *refs):
    parts = refs[: len(plan)]
    out, e_all, g_all, total, sems = refs[len(plan) :]
    rows, states = g_all.shape[1], e_all.shape[1] // (n * n + 1)
    here_x, here_y, size = lax.axis_index("tx"), lax.axis_index("ty"), sizes[0]
    sign = turn_sign()
    copies_e, copies_g = [], []
    for part, (kind, step) in zip(parts, plan):
        skipped = 1 if part.shape[0] == n - 1 else 0
        for d in range(skipped, skipped + part.shape[0]):
            if kind == "e":
                lag = n * around(here_x, -d, n) + around(here_y, sign * step, n)
                left = pl.multiple_of((n * n - 1 - lag) * states, 128)
                copies_e.append((part.at[d - skipped], e_all.at[:, pl.ds(left, states)]))
            else:
                u = n * around(here_x, sign * step, n) + around(here_y, -d, n)
                left = pl.multiple_of(lax.rem(u, 2) * states, 128)
                copies_g.append((part.at[d - skipped], g_all.at[u // 2, :, pl.ds(left, states)]))
    moves = [
        pltpu.make_async_copy(src, dst, sems.at[i])
        for i, (src, dst) in enumerate(copies_e + copies_g)
    ]
    for move in moves:
        move.start()
    e_all[:, n * n * states :] = jnp.zeros((rows, states), jnp.bfloat16)
    for move in moves:
        move.wait()

    for u in range(0, n * n, 2):
        right = g_all[u // 2]
        for first in range(0, n * n - u, n):
            lags = range(first, min(first + n, n * n - u))
            left = jnp.concatenate(
                [
                    e_all[:, (n * n - 1 - lag) * states : (n * n + 1 - lag) * states]
                    for lag in lags
                ],
                axis=0,
            )
            product = lax.dot_general(left, right, NT, preferred_element_type=jnp.float32)
            where = slice((u + lags[0]) * rows, (u + lags[-1] + 1) * rows)
            if u == 0:
                total[where] = product
            else:
                total[where] += product

    quarter = rows // n
    scale = step_size * step_size
    for b in range(n):
        row = lax.broadcasted_iota(jnp.int32, (quarter, rows), 0) + b * quarter
        column = lax.broadcasted_iota(jnp.int32, (quarter, rows), 1)
        starts = (row == column) & (here_x == here_y) & (row + here_x * rows < size)
        rate = rates[b * quarter : (b + 1) * quarter]
        decay = jnp.broadcast_to(jnp.exp(-step_size * rate), (quarter, rows))
        for t in range(n * n):
            term = scale * total[t * rows + b * quarter : t * rows + (b + 1) * quarter]
            fresh = (jnp.where(starts, 1.0, 0.0) if t == 0 else decay * fresh) - term
            out[t, :, b * rows : (b + 1) * rows] = fresh.astype(jnp.bfloat16)


def convolve(entries, sizes, rates, n, step_size):
    plan, parts = [e[:2] for e in entries], [e[2] for e in entries]
    _, rows, states = parts[0].shape
    copies = sum(part.shape[0] for part in parts)
    return pl.pallas_call(
        functools.partial(convolve_kernel, plan, n, step_size),
        out_shape=jax.ShapeDtypeStruct((n * n, rows // n, states), jnp.bfloat16),
        in_specs=[SMEM, VMEM] + [HBM] * len(parts),
        out_specs=VMEM,
        scratch_shapes=[
            pltpu.VMEM((rows, (n * n + 1) * states), jnp.bfloat16),
            pltpu.VMEM((n * n // 2, rows, 2 * states), jnp.bfloat16),
            pltpu.VMEM((n * n * rows, rows), jnp.float32),
            pltpu.SemaphoreType.DMA((copies,)),
        ],
        compiler_params=pltpu.CompilerParams(vmem_limit_bytes=52 * MIB),
        cost_estimate=pl.CostEstimate(
            flops=n * n * (n * n + 1) * rows * rows * states,
            bytes_accessed=4 * n * n * rows * states,
            transcendentals=0,
        ),
        name="convolve",
    )(sizes, rates, *parts)


def assemble_kernel(n, packets, out):
    quarter, states = packets.shape[1:]
    rows = states // n
    for x in range(n):
        for b in range(n):
            out[x * rows + b * quarter : x * rows + (b + 1) * quarter, :] = jnp.concatenate(
                [packets[x * n + y, :, b * rows : (b + 1) * rows] for y in range(n)], axis=1
            )


def assemble(packets, n):
    states = packets.shape[2]
    return pl.pallas_call(
        functools.partial(assemble_kernel, n),
        out_shape=jax.ShapeDtypeStruct((states, states), jnp.bfloat16),
        in_specs=[VMEM],
        out_specs=VMEM,
        name="assemble",
    )(packets)


def per_device(propagator, rising_op, energies, hyb_particle, hyb_hole, sector_sizes):
    states = propagator.shape[2]
    n = lax.axis_size("tx")
    step_size = 1.0 / (n * n)
    rows = states // n
    here_x = lax.axis_index("tx")
    operator = rising_op[0]

    masked, upward, flipped, own_g, *away_g = prepare(
        sector_sizes, propagator[0, 0], operator, n
    )
    below = shifted(upward, "sector", 1)
    above = shifted(masked, "sector", -1)
    crossed_g = {d: ring(away_g[d - 1], "ty", d) for d in (2, 1, 3)}
    columns = jnp.stack([own_g] + [crossed_g[d] for d in range(1, n)])

    own_e, *away_e = energy_blocks(
        sector_sizes, hyb_particle, hyb_hole, above, below, operator, flipped, n
    )
    crossed_e = {d: ring(away_e[d - 1], "tx", d) for d in (2, 1, 3)}
    crossed_e = [crossed_e[d] for d in range(1, n)]
    own_before, own_after = turned_ring(own_e, "ty", 1), turned_ring(own_e, "ty", -1)
    columns, crossed_e, own_before, own_after = lax.optimization_barrier(
        (columns, crossed_e, own_before, own_after)
    )
    before_g = turned_ring(columns, "tx", 1)
    lines = jnp.stack(crossed_e)
    before_e = turned_ring(lines, "ty", 1)
    after_g = turned_ring(columns, "tx", -1)
    after_e = turned_ring(lines, "ty", -1)
    own_far = turned_ring(own_before, "ty", 1)
    far_g = turned_ring(before_g, "tx", 1)
    far_e = turned_ring(before_e, "ty", 1)
    entries = [
        (kind, step, part)
        for kind, parts in (
            ("e", (own_e[None], own_before[None], own_after[None], own_far[None])),
            ("e", (lines, before_e, after_e, far_e)),
            ("g", (columns, before_g, after_g, far_g)),
        )
        for step, part in zip((0, -1, 1, 2), parts)
    ]
    rates = lax.dynamic_slice_in_dim(energies[0], here_x * rows, rows, 0)[:, None]
    packets = convolve(entries, sector_sizes, rates, n, step_size)
    packets = lax.all_to_all(packets, ("tx", "ty"), 0, 0, tiled=True)
    return assemble(packets, n)[None, None]


def solution(mesh):
    n = round(mesh.shape["tm"] ** 0.5)
    split = Mesh(
        np.asarray(mesh.devices).reshape(n, n, mesh.shape["sector"]), ("tx", "ty", "sector")
    )
    times = ("tx", "ty")
    placed = (
        P("sector", times, None, None),
        P("sector", None, None),
        P("sector", None),
        P(times),
        P(times),
        P("sector"),
    )
    return jax.shard_map(
        per_device,
        mesh=split,
        in_specs=placed,
        out_specs=P("sector", times, None, None),
        check_vma=False,
    )
```

```python
import functools

import jax
import jax.numpy as jnp
import numpy as np
from jax import lax
from jax.experimental import pallas as pl
from jax.experimental.pallas import tpu as pltpu
from jax.sharding import Mesh
from jax.sharding import PartitionSpec as P

MIB = 1024 * 1024
VMEM = pl.BlockSpec(memory_space=pltpu.VMEM)
SMEM = pl.BlockSpec(memory_space=pltpu.SMEM)
HBM = pl.BlockSpec(memory_space=pltpu.HBM)
NT = (((1,), (1,)), ((), ()))


def shifted(block, axis, distance):
    devices = range(lax.axis_size(axis))
    route = [(i - distance, i) for i in devices if i - distance in devices]
    return lax.ppermute(block, axis, route)


def ring(block, axis, distance):
    n = lax.axis_size(axis)
    return lax.ppermute(block, axis, [(i, (i + distance) % n) for i in range(n)])


def tied(value, *others):
    return lax.optimization_barrier((value, *others))[0]


def turn_sign():
    return 1 - 2 * lax.rem(lax.axis_index("sector"), 2)


def turned_ring(block, axis, distance):
    n, sectors = lax.axis_size(axis), lax.axis_size("sector")
    route = []
    for i in range(n):
        for s in range(sectors):
            step = distance if s % 2 == 0 else -distance
            route.append((i * sectors + s, (i + step) % n * sectors + s))
    return lax.ppermute(block, (axis, "sector"), route)


def live(shape, size, first_row=0):
    row = lax.broadcasted_iota(jnp.int32, shape, 0) + first_row
    column = lax.broadcasted_iota(jnp.int32, shape, 1)
    return (row < size) & (column < size)


def dot(a, b):
    return jnp.dot(a, b, preferred_element_type=jnp.float32)


def prepare_kernel(sizes, prop, operator, masked, upward, flipped, *refs):
    *turned, staged = refs
    n = len(turned)
    rows = turned[0].shape[0]
    inner = prop[...].astype(jnp.float32)
    inner = jnp.where(live(inner.shape, sizes[0]), inner, 0.0).astype(jnp.bfloat16)
    masked[...] = inner
    r = operator[...]
    raised = dot(r, inner).astype(jnp.bfloat16)
    upward[...] = lax.dot_general(raised, r, NT, preferred_element_type=jnp.float32).astype(
        jnp.bfloat16
    )
    staged[...] = inner.T
    here_y = lax.axis_index("ty")
    for d in range(n):
        first = pl.multiple_of(lax.rem(here_y + d, n) * rows, 32)
        turned[d][...] = staged[pl.ds(first, rows), :]
    flipped[...] = r.T


def prepare(sizes, prop, operator, n):
    states = prop.shape[0]
    square = jax.ShapeDtypeStruct((states, states), jnp.bfloat16)
    block = jax.ShapeDtypeStruct((states // n, states), jnp.bfloat16)
    return pl.pallas_call(
        prepare_kernel,
        out_shape=(square,) * 3 + (block,) * n,
        in_specs=[SMEM, VMEM, VMEM],
        out_specs=(VMEM,) * (3 + n),
        scratch_shapes=[pltpu.VMEM((states, states), jnp.bfloat16)],
        cost_estimate=pl.CostEstimate(
            flops=4 * states**3, bytes_accessed=12 * states**2, transcendentals=0
        ),
        name="prepare",
    )(sizes, prop, operator)


def energy_kernel(sizes, particle, hole, *refs):
    sources, (*outs,), copies, sems = refs[:4], refs[4:-5], refs[-5:-1], refs[-1]
    moves = [
        pltpu.make_async_copy(src, dst, sems.at[i])
        for i, (src, dst) in enumerate(zip(sources, copies))
    ]
    for move in moves:
        move.start()
    n = len(outs)
    rows = outs[0].shape[0]
    here_x = lax.axis_index("tx")
    flipped, above, operator, below = copies
    moves[0].wait()
    moves[1].wait()
    for d in (2, 1, 3, 0):
        first = pl.multiple_of(lax.rem(here_x + d, n) * rows, 32)
        lowered = dot(flipped[pl.ds(first, rows), :], above[...]).astype(jnp.bfloat16)
        if d == 2:
            moves[2].wait()
        downward = dot(lowered, operator[...])
        if d == 2:
            moves[3].wait()
        raised = below[pl.ds(first, rows), :].astype(jnp.float32)
        both = particle[0] * raised + hole[0] * downward
        kept = live(both.shape, sizes[0], first)
        outs[d][...] = jnp.where(kept, both, 0.0).astype(jnp.bfloat16)


def energy_blocks(sizes, particle, hole, above, below, operator, flipped, n):
    states = above.shape[0]
    block = jax.ShapeDtypeStruct((states // n, states), jnp.bfloat16)
    return pl.pallas_call(
        energy_kernel,
        out_shape=(block,) * n,
        in_specs=[SMEM] * 3 + [HBM] * 4,
        out_specs=(VMEM,) * n,
        scratch_shapes=[pltpu.VMEM((states, states), jnp.bfloat16)] * 4
        + [pltpu.SemaphoreType.DMA((4,))],
        cost_estimate=pl.CostEstimate(
            flops=4 * states**3, bytes_accessed=10 * states**2, transcendentals=0
        ),
        name="energy_blocks",
    )(sizes, particle, hole, flipped, above, operator, below)


def around(here, offset, n):
    return lax.rem(here + offset + n, n)


def convolve_kernel(plan, n, step_size, sizes, rates, *refs):
    parts = refs[: len(plan)]
    out, e_all, g_all, total, sems = refs[len(plan) :]
    rows, states = g_all.shape[1], e_all.shape[1] // (n * n + 1)
    here_x, here_y, size = lax.axis_index("tx"), lax.axis_index("ty"), sizes[0]
    sign = turn_sign()
    copies_e, copies_g = [], []
    for part, (kind, step) in zip(parts, plan):
        for d in range(n):
            if kind == "e":
                lag = n * around(here_x, -d, n) + around(here_y, sign * step, n)
                left = pl.multiple_of((n * n - 1 - lag) * states, 128)
                copies_e.append((part.at[d], e_all.at[:, pl.ds(left, states)]))
            else:
                u = n * around(here_x, sign * step, n) + around(here_y, -d, n)
                left = pl.multiple_of(lax.rem(u, 2) * states, 128)
                copies_g.append((part.at[d], g_all.at[u // 2, :, pl.ds(left, states)]))
    moves = [
        pltpu.make_async_copy(src, dst, sems.at[i])
        for i, (src, dst) in enumerate(copies_e + copies_g)
    ]
    for move in moves:
        move.start()
    e_all[:, n * n * states :] = jnp.zeros((rows, states), jnp.bfloat16)
    for move in moves:
        move.wait()

    for u in range(0, n * n, 2):
        right = g_all[u // 2]
        for first in range(0, n * n - u, n):
            lags = range(first, min(first + n, n * n - u))
            left = jnp.concatenate(
                [
                    e_all[:, (n * n - 1 - lag) * states : (n * n + 1 - lag) * states]
                    for lag in lags
                ],
                axis=0,
            )
            product = lax.dot_general(left, right, NT, preferred_element_type=jnp.float32)
            where = slice((u + lags[0]) * rows, (u + lags[-1] + 1) * rows)
            if u == 0:
                total[where] = product
            else:
                total[where] += product

    quarter = rows // n
    scale = step_size * step_size
    for b in range(n):
        row = lax.broadcasted_iota(jnp.int32, (quarter, rows), 0) + b * quarter
        column = lax.broadcasted_iota(jnp.int32, (quarter, rows), 1)
        starts = (row == column) & (here_x == here_y) & (row + here_x * rows < size)
        rate = rates[b * quarter : (b + 1) * quarter]
        decay = jnp.broadcast_to(jnp.exp(-step_size * rate), (quarter, rows))
        for t in range(n * n):
            term = scale * total[t * rows + b * quarter : t * rows + (b + 1) * quarter]
            fresh = (jnp.where(starts, 1.0, 0.0) if t == 0 else decay * fresh) - term
            out[t, :, b * rows : (b + 1) * rows] = fresh.astype(jnp.bfloat16)


def convolve(entries, sizes, rates, n, step_size):
    plan, parts = [e[:2] for e in entries], [e[2] for e in entries]
    _, rows, states = parts[0].shape
    copies = n * len(parts)
    return pl.pallas_call(
        functools.partial(convolve_kernel, plan, n, step_size),
        out_shape=jax.ShapeDtypeStruct((n * n, rows // n, states), jnp.bfloat16),
        in_specs=[SMEM, VMEM] + [HBM] * len(parts),
        out_specs=VMEM,
        scratch_shapes=[
            pltpu.VMEM((rows, (n * n + 1) * states), jnp.bfloat16),
            pltpu.VMEM((n * n // 2, rows, 2 * states), jnp.bfloat16),
            pltpu.VMEM((n * n * rows, rows), jnp.float32),
            pltpu.SemaphoreType.DMA((copies,)),
        ],
        compiler_params=pltpu.CompilerParams(vmem_limit_bytes=52 * MIB),
        cost_estimate=pl.CostEstimate(
            flops=n * n * (n * n + 1) * rows * rows * states,
            bytes_accessed=4 * n * n * rows * states,
            transcendentals=0,
        ),
        name="convolve",
    )(sizes, rates, *parts)


def assemble_kernel(n, packets, out):
    quarter, states = packets.shape[1:]
    rows = states // n
    for x in range(n):
        for b in range(n):
            out[x * rows + b * quarter : x * rows + (b + 1) * quarter, :] = jnp.concatenate(
                [packets[x * n + y, :, b * rows : (b + 1) * rows] for y in range(n)], axis=1
            )


def assemble(packets, n):
    states = packets.shape[2]
    return pl.pallas_call(
        functools.partial(assemble_kernel, n),
        out_shape=jax.ShapeDtypeStruct((states, states), jnp.bfloat16),
        in_specs=[VMEM],
        out_specs=VMEM,
        name="assemble",
    )(packets)


def per_device(propagator, rising_op, energies, hyb_particle, hyb_hole, sector_sizes):
    states = propagator.shape[2]
    n = lax.axis_size("tx")
    step_size = 1.0 / (n * n)
    rows = states // n
    here_x = lax.axis_index("tx")
    operator = rising_op[0]

    masked, upward, flipped, own_g, *away_g = prepare(
        sector_sizes, propagator[0, 0], operator, n
    )
    below = shifted(upward, "sector", 1)
    above = shifted(masked, "sector", -1)
    crossed_g = {d: ring(away_g[d - 1], "ty", d) for d in (2, 1, 3)}
    columns = jnp.stack([own_g] + [crossed_g[d] for d in range(1, n)])

    own_e, *away_e = energy_blocks(
        sector_sizes, hyb_particle, hyb_hole, above, below, operator, flipped, n
    )
    crossed_e = {d: ring(away_e[d - 1], "tx", d) for d in (2, 1, 3)}
    lines = jnp.stack([own_e] + [crossed_e[d] for d in range(1, n)])

    before_g = turned_ring(columns, "tx", 1)
    after_g = turned_ring(columns, "tx", -1)
    before_e = turned_ring(lines, "ty", 1)
    after_e = turned_ring(tied(lines, before_g), "ty", -1)
    far_g = turned_ring(before_g, "tx", 1)
    far_e = turned_ring(before_e, "ty", 1)
    entries = [
        (kind, step, part)
        for kind, parts in (
            ("e", (lines, before_e, after_e, far_e)),
            ("g", (columns, before_g, after_g, far_g)),
        )
        for step, part in zip((0, -1, 1, 2), parts)
    ]
    rates = lax.dynamic_slice_in_dim(energies[0], here_x * rows, rows, 0)[:, None]
    packets = convolve(entries, sector_sizes, rates, n, step_size)
    packets = lax.all_to_all(packets, ("tx", "ty"), 0, 0, tiled=True)
    return assemble(packets, n)[None, None]


def solution(mesh):
    n = round(mesh.shape["tm"] ** 0.5)
    split = Mesh(
        np.asarray(mesh.devices).reshape(n, n, mesh.shape["sector"]), ("tx", "ty", "sector")
    )
    times = ("tx", "ty")
    placed = (
        P("sector", times, None, None),
        P("sector", None, None),
        P("sector", None),
        P(times),
        P(times),
        P("sector"),
    )
    return jax.shard_map(
        per_device,
        mesh=split,
        in_specs=placed,
        out_specs=P("sector", times, None, None),
        check_vma=False,
    )
```

```python
import functools

import jax
import jax.numpy as jnp
import numpy as np
from jax import lax
from jax.experimental import pallas as pl
from jax.experimental.pallas import tpu as pltpu
from jax.sharding import Mesh
from jax.sharding import PartitionSpec as P

MIB = 1024 * 1024
VMEM = pl.BlockSpec(memory_space=pltpu.VMEM)
SMEM = pl.BlockSpec(memory_space=pltpu.SMEM)
ANY = pl.BlockSpec(memory_space=pl.ANY)
HBM = pl.BlockSpec(memory_space=pltpu.HBM)
NT = (((1,), (1,)), ((), ()))


def shifted(block, axis, distance):
    devices = range(lax.axis_size(axis))
    route = [(i - distance, i) for i in devices if i - distance in devices]
    return lax.ppermute(block, axis, route)


def ring(block, axis, distance):
    n = lax.axis_size(axis)
    return lax.ppermute(block, axis, [(i, (i + distance) % n) for i in range(n)])


def turn_sign():
    return 1 - 2 * lax.rem(lax.axis_index("sector"), 2)


def turned_ring(block, axis, distance):
    n, sectors = lax.axis_size(axis), lax.axis_size("sector")
    route = []
    for i in range(n):
        for s in range(sectors):
            step = distance if s % 2 == 0 else -distance
            route.append((i * sectors + s, (i + step) % n * sectors + s))
    return lax.ppermute(block, (axis, "sector"), route)


def ring_gather(block, axis):
    before = turned_ring(block, axis, 1)
    after = turned_ring(block, axis, -1)
    return [(0, block), (-1, before), (1, after), (2, turned_ring(before, axis, 1))]


def live(shape, size, first_row=0):
    row = lax.broadcasted_iota(jnp.int32, shape, 0) + first_row
    column = lax.broadcasted_iota(jnp.int32, shape, 1)
    return (row < size) & (column < size)


def dot(a, b):
    return jnp.dot(a, b, preferred_element_type=jnp.float32)


def prepare_kernel(sizes, prop, operator, masked, upward, flipped, *refs):
    *turned, staged = refs
    n = len(turned)
    rows = turned[0].shape[0]
    inner = prop[...].astype(jnp.float32)
    inner = jnp.where(live(inner.shape, sizes[0]), inner, 0.0).astype(jnp.bfloat16)
    masked[...] = inner
    r = operator[...]
    raised = dot(r, inner).astype(jnp.bfloat16)
    upward[...] = lax.dot_general(raised, r, NT, preferred_element_type=jnp.float32).astype(
        jnp.bfloat16
    )
    staged[...] = inner.T
    here_y = lax.axis_index("ty")
    for d in range(n):
        first = pl.multiple_of(lax.rem(here_y + d, n) * rows, 32)
        turned[d][...] = staged[pl.ds(first, rows), :]
    flipped[...] = r.T


def prepare(sizes, prop, operator, n):
    states = prop.shape[0]
    square = jax.ShapeDtypeStruct((states, states), jnp.bfloat16)
    block = jax.ShapeDtypeStruct((states // n, states), jnp.bfloat16)
    return pl.pallas_call(
        prepare_kernel,
        out_shape=(square,) * 3 + (block,) * n,
        in_specs=[SMEM, VMEM, VMEM],
        out_specs=(VMEM,) * (3 + n),
        scratch_shapes=[pltpu.VMEM((states, states), jnp.bfloat16)],
        cost_estimate=pl.CostEstimate(
            flops=4 * states**3, bytes_accessed=12 * states**2, transcendentals=0
        ),
        name="prepare",
    )(sizes, prop, operator)


def energy_kernel(sizes, particle, hole, *refs):
    sources, (*outs,), copies, sems = refs[:4], refs[4:-5], refs[-5:-1], refs[-1]
    moves = [
        pltpu.make_async_copy(src, dst, sems.at[i])
        for i, (src, dst) in enumerate(zip(sources, copies))
    ]
    for move in moves:
        move.start()
    n = len(outs)
    rows = outs[0].shape[0]
    here_x = lax.axis_index("tx")
    for move in moves:
        move.wait()
    flipped, above, operator, below = copies
    inner = above[...]
    r = operator[...]
    for d in (2, 1, 3, 0):
        first = pl.multiple_of(lax.rem(here_x + d, n) * rows, 32)
        lowered = dot(flipped[pl.ds(first, rows), :], inner).astype(jnp.bfloat16)
        downward = dot(lowered, r)
        raised = below[pl.ds(first, rows), :].astype(jnp.float32)
        both = particle[0] * raised + hole[0] * downward
        kept = live(both.shape, sizes[0], first)
        outs[d][...] = jnp.where(kept, both, 0.0).astype(jnp.bfloat16)


def energy_blocks(sizes, particle, hole, above, below, operator, flipped, n):
    states = above.shape[0]
    block = jax.ShapeDtypeStruct((states // n, states), jnp.bfloat16)
    return pl.pallas_call(
        energy_kernel,
        out_shape=(block,) * n,
        in_specs=[SMEM] * 3 + [ANY] * 4,
        out_specs=(VMEM,) * n,
        scratch_shapes=[pltpu.VMEM((states, states), jnp.bfloat16)] * 4
        + [pltpu.SemaphoreType.DMA((4,))],
        cost_estimate=pl.CostEstimate(
            flops=4 * states**3, bytes_accessed=10 * states**2, transcendentals=0
        ),
        compiler_params=pltpu.CompilerParams(vmem_limit_bytes=16 * MIB),
        name="energy_blocks",
    )(sizes, particle, hole, flipped, above, operator, below)


def around(here, offset, n):
    return lax.rem(here + offset + n, n)


def convolve_kernel(plan, n, step_size, sizes, rates, *refs):
    parts = refs[: len(plan)]
    out, e_all, g_all, total, sems = refs[len(plan) :]
    rows, states = g_all.shape[1], e_all.shape[1] // (n * n + 1)
    here_x, here_y, size = lax.axis_index("tx"), lax.axis_index("ty"), sizes[0]
    sign = turn_sign()
    copies_e, copies_g = [], []
    for part, (kind, step) in zip(parts, plan):
        for d in range(n):
            if kind == "e":
                lag = n * around(here_x, -d, n) + around(here_y, sign * step, n)
                left = pl.multiple_of((n * n - 1 - lag) * states, 128)
                copies_e.append((part.at[d], e_all.at[:, pl.ds(left, states)]))
            else:
                u = n * around(here_x, sign * step, n) + around(here_y, -d, n)
                left = pl.multiple_of(lax.rem(u, 2) * states, 128)
                copies_g.append((part.at[d], g_all.at[u // 2, :, pl.ds(left, states)]))
    moves = [
        pltpu.make_async_copy(src, dst, sems.at[i])
        for i, (src, dst) in enumerate(copies_e + copies_g)
    ]
    for move in moves:
        move.start()
    e_all[:, n * n * states :] = jnp.zeros((rows, states), jnp.bfloat16)
    for move in moves:
        move.wait()

    for u in range(0, n * n, 2):
        right = g_all[u // 2]
        for first in range(0, n * n - u, n):
            lags = range(first, min(first + n, n * n - u))
            left = jnp.concatenate(
                [
                    e_all[:, (n * n - 1 - lag) * states : (n * n + 1 - lag) * states]
                    for lag in lags
                ],
                axis=0,
            )
            product = lax.dot_general(left, right, NT, preferred_element_type=jnp.float32)
            where = slice((u + lags[0]) * rows, (u + lags[-1] + 1) * rows)
            if u == 0:
                total[where] = product
            else:
                total[where] += product

    quarter = rows // n
    scale = step_size * step_size
    for b in range(n):
        row = lax.broadcasted_iota(jnp.int32, (quarter, rows), 0) + b * quarter
        column = lax.broadcasted_iota(jnp.int32, (quarter, rows), 1)
        starts = (row == column) & (here_x == here_y) & (row + here_x * rows < size)
        rate = rates[b * quarter : (b + 1) * quarter]
        decay = jnp.broadcast_to(jnp.exp(-step_size * rate), (quarter, rows))
        for t in range(n * n):
            term = scale * total[t * rows + b * quarter : t * rows + (b + 1) * quarter]
            fresh = (jnp.where(starts, 1.0, 0.0) if t == 0 else decay * fresh) - term
            out[t, :, b * rows : (b + 1) * rows] = fresh.astype(jnp.bfloat16)


def convolve(entries, sizes, rates, n, step_size):
    plan, parts = [e[:2] for e in entries], [e[2] for e in entries]
    _, rows, states = parts[0].shape
    copies = n * len(parts)
    return pl.pallas_call(
        functools.partial(convolve_kernel, plan, n, step_size),
        out_shape=jax.ShapeDtypeStruct((n * n, rows // n, states), jnp.bfloat16),
        in_specs=[SMEM, VMEM] + [ANY] * len(parts),
        out_specs=VMEM,
        scratch_shapes=[
            pltpu.VMEM((rows, (n * n + 1) * states), jnp.bfloat16),
            pltpu.VMEM((n * n // 2, rows, 2 * states), jnp.bfloat16),
            pltpu.VMEM((n * n * rows, rows), jnp.float32),
            pltpu.SemaphoreType.DMA((copies,)),
        ],
        compiler_params=pltpu.CompilerParams(vmem_limit_bytes=20 * MIB),
        cost_estimate=pl.CostEstimate(
            flops=n * n * (n * n + 1) * rows * rows * states,
            bytes_accessed=4 * n * n * rows * states,
            transcendentals=0,
        ),
        name="convolve",
    )(sizes, rates, *parts)


def assemble_kernel(n, packets, out):
    quarter, states = packets.shape[1:]
    rows = states // n
    for x in range(n):
        for b in range(n):
            out[x * rows + b * quarter : x * rows + (b + 1) * quarter, :] = jnp.concatenate(
                [packets[x * n + y, :, b * rows : (b + 1) * rows] for y in range(n)], axis=1
            )


def assemble(packets, n):
    states = packets.shape[2]
    return pl.pallas_call(
        functools.partial(assemble_kernel, n),
        out_shape=jax.ShapeDtypeStruct((states, states), jnp.bfloat16),
        in_specs=[VMEM],
        out_specs=VMEM,
        name="assemble",
    )(packets)


def per_device(propagator, rising_op, energies, hyb_particle, hyb_hole, sector_sizes):
    states = propagator.shape[2]
    n = lax.axis_size("tx")
    step_size = 1.0 / (n * n)
    rows = states // n
    here_x = lax.axis_index("tx")
    operator = rising_op[0]

    masked, upward, flipped, own_g, *away_g = prepare(
        sector_sizes, propagator[0, 0], operator, n
    )
    below = shifted(upward, "sector", 1)
    above = shifted(masked, "sector", -1)
    crossed_g = {d: ring(away_g[d - 1], "ty", d) for d in (2, 1, 3)}
    columns = jnp.stack([own_g] + [crossed_g[d] for d in range(1, n)])

    own_e, *away_e = energy_blocks(
        sector_sizes, hyb_particle, hyb_hole, above, below, operator, flipped, n
    )
    crossed_e = {d: ring(away_e[d - 1], "tx", d) for d in (2, 1, 3)}
    lines = jnp.stack([own_e] + [crossed_e[d] for d in range(1, n)])

    entries = [("g", step, part) for step, part in ring_gather(columns, "tx")]
    entries = [("e", step, part) for step, part in ring_gather(lines, "ty")] + entries
    rates = lax.dynamic_slice_in_dim(energies[0], here_x * rows, rows, 0)[:, None]
    packets = convolve(entries, sector_sizes, rates, n, step_size)
    packets = lax.all_to_all(packets, ("tx", "ty"), 0, 0, tiled=True)
    return assemble(packets, n)[None, None]


def solution(mesh):
    n = round(mesh.shape["tm"] ** 0.5)
    split = Mesh(
        np.asarray(mesh.devices).reshape(n, n, mesh.shape["sector"]), ("tx", "ty", "sector")
    )
    times = ("tx", "ty")
    placed = (
        P("sector", times, None, None),
        P("sector", None, None),
        P("sector", None),
        P(times),
        P(times),
        P("sector"),
    )
    return jax.shard_map(
        per_device,
        mesh=split,
        in_specs=placed,
        out_specs=P("sector", times, None, None),
        check_vma=False,
    )
```

```python
import functools

import jax
import jax.numpy as jnp
import numpy as np
from jax import lax
from jax.experimental import pallas as pl
from jax.experimental.pallas import tpu as pltpu
from jax.sharding import Mesh
from jax.sharding import PartitionSpec as P

MIB = 1024 * 1024
VMEM = pl.BlockSpec(memory_space=pltpu.VMEM)
SMEM = pl.BlockSpec(memory_space=pltpu.SMEM)
ANY = pl.BlockSpec(memory_space=pl.ANY)
NT = (((1,), (1,)), ((), ()))


def shifted(block, axis, distance):
    devices = range(lax.axis_size(axis))
    route = [(i - distance, i) for i in devices if i - distance in devices]
    return lax.ppermute(block, axis, route)


def ring(block, axis, distance):
    n = lax.axis_size(axis)
    return lax.ppermute(block, axis, [(i, (i + distance) % n) for i in range(n)])


def turn_sign():
    return 1 - 2 * lax.rem(lax.axis_index("sector"), 2)


def turned_ring(block, axis, distance):
    n, sectors = lax.axis_size(axis), lax.axis_size("sector")
    route = []
    for i in range(n):
        for s in range(sectors):
            step = distance if s % 2 == 0 else -distance
            route.append((i * sectors + s, (i + step) % n * sectors + s))
    return lax.ppermute(block, (axis, "sector"), route)


def ring_gather(block, axis):
    before = turned_ring(block, axis, 1)
    after = turned_ring(block, axis, -1)
    return [(0, block), (-1, before), (1, after), (2, turned_ring(before, axis, 1))]


def live(shape, size, first_row=0):
    row = lax.broadcasted_iota(jnp.int32, shape, 0) + first_row
    column = lax.broadcasted_iota(jnp.int32, shape, 1)
    return (row < size) & (column < size)


def dot(a, b):
    return jnp.dot(a, b, preferred_element_type=jnp.float32)


def prepare_kernel(sizes, prop, operator, masked, upward, *refs):
    *turned, staged = refs
    n = len(turned)
    rows = turned[0].shape[0]
    inner = prop[...].astype(jnp.float32)
    inner = jnp.where(live(inner.shape, sizes[0]), inner, 0.0).astype(jnp.bfloat16)
    masked[...] = inner
    r = operator[...]
    raised = dot(r, inner).astype(jnp.bfloat16)
    upward[...] = lax.dot_general(raised, r, NT, preferred_element_type=jnp.float32).astype(
        jnp.bfloat16
    )
    staged[...] = inner.T
    here_y = lax.axis_index("ty")
    for d in range(n):
        first = pl.multiple_of(lax.rem(here_y + d, n) * rows, 32)
        turned[d][...] = staged[pl.ds(first, rows), :]


def prepare(sizes, prop, operator, n):
    states = prop.shape[0]
    square = jax.ShapeDtypeStruct((states, states), jnp.bfloat16)
    block = jax.ShapeDtypeStruct((states // n, states), jnp.bfloat16)
    return pl.pallas_call(
        prepare_kernel,
        out_shape=(square,) * 2 + (block,) * n,
        in_specs=[SMEM, VMEM, VMEM],
        out_specs=(VMEM,) * (2 + n),
        scratch_shapes=[pltpu.VMEM((states, states), jnp.bfloat16)],
        cost_estimate=pl.CostEstimate(
            flops=4 * states**3, bytes_accessed=12 * states**2, transcendentals=0
        ),
        name="prepare",
    )(sizes, prop, operator)


def energy_kernel(sizes, particle, hole, *refs):
    sources, (*outs,), copies, lowered, sems = refs[:3], refs[3:-5], refs[-5:-2], refs[-2], refs[-1]
    moves = [
        pltpu.make_async_copy(src, dst, sems.at[i])
        for i, (src, dst) in enumerate(zip(sources, copies))
    ]
    for move in moves:
        move.start()
    n = len(outs)
    rows = outs[0].shape[0]
    here_x = lax.axis_index("tx")
    for move in moves:
        move.wait()
    above, operator, below = copies
    r = operator[...]
    lowered[...] = lax.dot_general(
        r, above[...], (((0,), (0,)), ((), ())), preferred_element_type=jnp.float32
    ).astype(jnp.bfloat16)
    for d in (2, 1, 3, 0):
        first = pl.multiple_of(lax.rem(here_x + d, n) * rows, 32)
        downward = dot(lowered[pl.ds(first, rows), :], r)
        raised = below[pl.ds(first, rows), :].astype(jnp.float32)
        both = particle[0] * raised + hole[0] * downward
        kept = live(both.shape, sizes[0], first)
        outs[d][...] = jnp.where(kept, both, 0.0).astype(jnp.bfloat16)


def energy_blocks(sizes, particle, hole, above, below, operator, n):
    states = above.shape[0]
    block = jax.ShapeDtypeStruct((states // n, states), jnp.bfloat16)
    return pl.pallas_call(
        energy_kernel,
        out_shape=(block,) * n,
        in_specs=[SMEM] * 3 + [ANY] * 3,
        out_specs=(VMEM,) * n,
        scratch_shapes=[pltpu.VMEM((states, states), jnp.bfloat16)] * 4
        + [pltpu.SemaphoreType.DMA((3,))],
        cost_estimate=pl.CostEstimate(
            flops=4 * states**3, bytes_accessed=8 * states**2, transcendentals=0
        ),
        compiler_params=pltpu.CompilerParams(vmem_limit_bytes=16 * MIB),
        name="energy_blocks",
    )(sizes, particle, hole, above, operator, below)


def around(here, offset, n):
    return lax.rem(here + offset + n, n)


def convolve_kernel(plan, n, step_size, sizes, rates, *refs):
    parts = refs[: len(plan)]
    out, e_all, g_all, total, sems = refs[len(plan) :]
    rows, states = g_all.shape[1], e_all.shape[1] // (n * n + 1)
    here_x, here_y, size = lax.axis_index("tx"), lax.axis_index("ty"), sizes[0]
    sign = turn_sign()
    copies_e, copies_g = [], []
    for part, (kind, step) in zip(parts, plan):
        for d in range(n):
            if kind == "e":
                lag = n * around(here_x, -d, n) + around(here_y, sign * step, n)
                left = pl.multiple_of((n * n - 1 - lag) * states, 128)
                copies_e.append((part.at[d], e_all.at[:, pl.ds(left, states)]))
            else:
                u = n * around(here_x, sign * step, n) + around(here_y, -d, n)
                left = pl.multiple_of(lax.rem(u, 2) * states, 128)
                copies_g.append((part.at[d], g_all.at[u // 2, :, pl.ds(left, states)]))
    moves = [
        pltpu.make_async_copy(src, dst, sems.at[i])
        for i, (src, dst) in enumerate(copies_e + copies_g)
    ]
    for move in moves:
        move.start()
    e_all[:, n * n * states :] = jnp.zeros((rows, states), jnp.bfloat16)
    for move in moves:
        move.wait()

    for u in range(0, n * n, 2):
        right = g_all[u // 2]
        for first in range(0, n * n - u, n):
            lags = range(first, min(first + n, n * n - u))
            left = jnp.concatenate(
                [
                    e_all[:, (n * n - 1 - lag) * states : (n * n + 1 - lag) * states]
                    for lag in lags
                ],
                axis=0,
            )
            product = lax.dot_general(left, right, NT, preferred_element_type=jnp.float32)
            where = slice((u + lags[0]) * rows, (u + lags[-1] + 1) * rows)
            if u == 0:
                total[where] = product
            else:
                total[where] += product

    quarter = rows // n
    scale = step_size * step_size
    for b in range(n):
        row = lax.broadcasted_iota(jnp.int32, (quarter, rows), 0) + b * quarter
        column = lax.broadcasted_iota(jnp.int32, (quarter, rows), 1)
        starts = (row == column) & (here_x == here_y) & (row + here_x * rows < size)
        rate = rates[b * quarter : (b + 1) * quarter]
        decay = jnp.broadcast_to(jnp.exp(-step_size * rate), (quarter, rows))
        for t in range(n * n):
            term = scale * total[t * rows + b * quarter : t * rows + (b + 1) * quarter]
            fresh = (jnp.where(starts, 1.0, 0.0) if t == 0 else decay * fresh) - term
            out[t, :, b * rows : (b + 1) * rows] = fresh.astype(jnp.bfloat16)


def convolve(entries, sizes, rates, n, step_size):
    plan, parts = [e[:2] for e in entries], [e[2] for e in entries]
    _, rows, states = parts[0].shape
    copies = n * len(parts)
    return pl.pallas_call(
        functools.partial(convolve_kernel, plan, n, step_size),
        out_shape=jax.ShapeDtypeStruct((n * n, rows // n, states), jnp.bfloat16),
        in_specs=[SMEM, VMEM] + [ANY] * len(parts),
        out_specs=VMEM,
        scratch_shapes=[
            pltpu.VMEM((rows, (n * n + 1) * states), jnp.bfloat16),
            pltpu.VMEM((n * n // 2, rows, 2 * states), jnp.bfloat16),
            pltpu.VMEM((n * n * rows, rows), jnp.float32),
            pltpu.SemaphoreType.DMA((copies,)),
        ],
        compiler_params=pltpu.CompilerParams(vmem_limit_bytes=20 * MIB),
        cost_estimate=pl.CostEstimate(
            flops=n * n * (n * n + 1) * rows * rows * states,
            bytes_accessed=4 * n * n * rows * states,
            transcendentals=0,
        ),
        name="convolve",
    )(sizes, rates, *parts)


def assemble_kernel(n, packets, out):
    quarter, states = packets.shape[1:]
    rows = states // n
    for x in range(n):
        for b in range(n):
            out[x * rows + b * quarter : x * rows + (b + 1) * quarter, :] = jnp.concatenate(
                [packets[x * n + y, :, b * rows : (b + 1) * rows] for y in range(n)], axis=1
            )


def assemble(packets, n):
    states = packets.shape[2]
    return pl.pallas_call(
        functools.partial(assemble_kernel, n),
        out_shape=jax.ShapeDtypeStruct((states, states), jnp.bfloat16),
        in_specs=[VMEM],
        out_specs=VMEM,
        name="assemble",
    )(packets)


def per_device(propagator, rising_op, energies, hyb_particle, hyb_hole, sector_sizes):
    states = propagator.shape[2]
    n = lax.axis_size("tx")
    step_size = 1.0 / (n * n)
    rows = states // n
    here_x = lax.axis_index("tx")
    operator = rising_op[0]

    masked, upward, own_g, *away_g = prepare(
        sector_sizes, propagator[0, 0], operator, n
    )
    below = shifted(upward, "sector", 1)
    above = shifted(masked, "sector", -1)
    crossed_g = {d: ring(away_g[d - 1], "ty", d) for d in (2, 1, 3)}
    columns = jnp.stack([own_g] + [crossed_g[d] for d in range(1, n)])

    own_e, *away_e = energy_blocks(
        sector_sizes, hyb_particle, hyb_hole, above, below, operator, n
    )
    crossed_e = {d: ring(away_e[d - 1], "tx", d) for d in (2, 1, 3)}
    lines = jnp.stack([own_e] + [crossed_e[d] for d in range(1, n)])

    entries = [("g", step, part) for step, part in ring_gather(columns, "tx")]
    entries = [("e", step, part) for step, part in ring_gather(lines, "ty")] + entries
    rates = lax.dynamic_slice_in_dim(energies[0], here_x * rows, rows, 0)[:, None]
    packets = convolve(entries, sector_sizes, rates, n, step_size)
    packets = lax.all_to_all(packets, ("tx", "ty"), 0, 0, tiled=True)
    return assemble(packets, n)[None, None]


def solution(mesh):
    n = round(mesh.shape["tm"] ** 0.5)
    split = Mesh(
        np.asarray(mesh.devices).reshape(n, n, mesh.shape["sector"]), ("tx", "ty", "sector")
    )
    times = ("tx", "ty")
    placed = (
        P("sector", times, None, None),
        P("sector", None, None),
        P("sector", None),
        P(times),
        P(times),
        P("sector"),
    )
    return jax.shard_map(
        per_device,
        mesh=split,
        in_specs=placed,
        out_specs=P("sector", times, None, None),
        check_vma=False,
    )
```

```python
import functools

import jax
import jax.numpy as jnp
import numpy as np
from jax import lax
from jax.experimental import pallas as pl
from jax.experimental.pallas import tpu as pltpu
from jax.sharding import Mesh
from jax.sharding import PartitionSpec as P

MIB = 1024 * 1024
VMEM = pl.BlockSpec(memory_space=pltpu.VMEM)
SMEM = pl.BlockSpec(memory_space=pltpu.SMEM)
ANY = pl.BlockSpec(memory_space=pl.ANY)
NT = (((1,), (1,)), ((), ()))


def shifted(block, axis, distance):
    devices = range(lax.axis_size(axis))
    route = [(i - distance, i) for i in devices if i - distance in devices]
    return lax.ppermute(block, axis, route)


def ring(block, axis, distance):
    n = lax.axis_size(axis)
    return lax.ppermute(block, axis, [(i, (i + distance) % n) for i in range(n)])


def turn_sign():
    return 1 - 2 * lax.rem(lax.axis_index("sector"), 2)


def turned_ring(block, axis, distance):
    n, sectors = lax.axis_size(axis), lax.axis_size("sector")
    route = []
    for i in range(n):
        for s in range(sectors):
            step = distance if s % 2 == 0 else -distance
            route.append((i * sectors + s, (i + step) % n * sectors + s))
    return lax.ppermute(block, (axis, "sector"), route)


def live(shape, size, first_row=0):
    row = lax.broadcasted_iota(jnp.int32, shape, 0) + first_row
    column = lax.broadcasted_iota(jnp.int32, shape, 1)
    return (row < size) & (column < size)


def dot(a, b):
    return jnp.dot(a, b, preferred_element_type=jnp.float32)


def prepare_kernel(sizes, prop, operator, masked, upward, *refs):
    *turned, staged = refs
    n = len(turned)
    rows = turned[0].shape[0]
    inner = prop[...].astype(jnp.float32)
    inner = jnp.where(live(inner.shape, sizes[0]), inner, 0.0).astype(jnp.bfloat16)
    masked[...] = inner
    r = operator[...]
    raised = dot(r, inner).astype(jnp.bfloat16)
    upward[...] = lax.dot_general(raised, r, NT, preferred_element_type=jnp.float32).astype(
        jnp.bfloat16
    )
    staged[...] = inner.T
    here_y = lax.axis_index("ty")
    for d in range(n):
        first = pl.multiple_of(lax.rem(here_y + d, n) * rows, 32)
        turned[d][...] = staged[pl.ds(first, rows), :]


def prepare(sizes, prop, operator, n):
    states = prop.shape[0]
    square = jax.ShapeDtypeStruct((states, states), jnp.bfloat16)
    block = jax.ShapeDtypeStruct((states // n, states), jnp.bfloat16)
    return pl.pallas_call(
        prepare_kernel,
        out_shape=(square,) * 2 + (block,) * n,
        in_specs=[SMEM, VMEM, VMEM],
        out_specs=(VMEM,) * (2 + n),
        scratch_shapes=[pltpu.VMEM((states, states), jnp.bfloat16)],
        cost_estimate=pl.CostEstimate(
            flops=4 * states**3, bytes_accessed=12 * states**2, transcendentals=0
        ),
        name="prepare",
    )(sizes, prop, operator)


def energy_kernel(sizes, particle, hole, *refs):
    sources, (*outs,), copies, lowered, sems = refs[:3], refs[3:-5], refs[-5:-2], refs[-2], refs[-1]
    moves = [
        pltpu.make_async_copy(src, dst, sems.at[i])
        for i, (src, dst) in enumerate(zip(sources, copies))
    ]
    for move in moves:
        move.start()
    n = len(outs)
    rows = outs[0].shape[0]
    here_x = lax.axis_index("tx")
    for move in moves:
        move.wait()
    above, operator, below = copies
    r = operator[...]
    lowered[...] = lax.dot_general(
        r, above[...], (((0,), (0,)), ((), ())), preferred_element_type=jnp.float32
    ).astype(jnp.bfloat16)
    for d in (2, 1, 3, 0):
        first = pl.multiple_of(lax.rem(here_x + d, n) * rows, 32)
        downward = dot(lowered[pl.ds(first, rows), :], r)
        raised = below[pl.ds(first, rows), :].astype(jnp.float32)
        both = particle[0] * raised + hole[0] * downward
        kept = live(both.shape, sizes[0], first)
        outs[d][...] = jnp.where(kept, both, 0.0).astype(jnp.bfloat16)


def energy_blocks(sizes, particle, hole, above, below, operator, n):
    states = above.shape[0]
    block = jax.ShapeDtypeStruct((states // n, states), jnp.bfloat16)
    return pl.pallas_call(
        energy_kernel,
        out_shape=(block,) * n,
        in_specs=[SMEM] * 3 + [ANY] * 3,
        out_specs=(VMEM,) * n,
        scratch_shapes=[pltpu.VMEM((states, states), jnp.bfloat16)] * 4
        + [pltpu.SemaphoreType.DMA((3,))],
        cost_estimate=pl.CostEstimate(
            flops=4 * states**3, bytes_accessed=8 * states**2, transcendentals=0
        ),
        compiler_params=pltpu.CompilerParams(vmem_limit_bytes=16 * MIB),
        name="energy_blocks",
    )(sizes, particle, hole, above, operator, below)


def around(here, offset, n):
    return lax.rem(here + offset + n, n)


def convolve_kernel(plan, n, step_size, sizes, rates, *refs):
    parts = refs[: len(plan)]
    out, e_all, g_all, total, sems = refs[len(plan) :]
    rows, states = g_all.shape[1], e_all.shape[1] // (n * n + 1)
    here_x, here_y, size = lax.axis_index("tx"), lax.axis_index("ty"), sizes[0]
    sign = turn_sign()
    copies_e, copies_g = [], []
    for part, (kind, step, crossed) in zip(parts, plan):
        for k in range(part.shape[0]):
            d = crossed + k
            if kind == "e":
                lag = n * around(here_x, -d, n) + around(here_y, sign * step, n)
                left = pl.multiple_of((n * n - 1 - lag) * states, 128)
                copies_e.append((part.at[k], e_all.at[:, pl.ds(left, states)]))
            else:
                u = n * around(here_x, sign * step, n) + around(here_y, -d, n)
                left = pl.multiple_of(lax.rem(u, 2) * states, 128)
                copies_g.append((part.at[k], g_all.at[u // 2, :, pl.ds(left, states)]))
    moves = [
        pltpu.make_async_copy(src, dst, sems.at[i])
        for i, (src, dst) in enumerate(copies_e + copies_g)
    ]
    for move in moves:
        move.start()
    e_all[:, n * n * states :] = jnp.zeros((rows, states), jnp.bfloat16)
    for move in moves:
        move.wait()

    for u in range(0, n * n, 2):
        right = g_all[u // 2]
        for first in range(0, n * n - u, n):
            lags = range(first, min(first + n, n * n - u))
            left = jnp.concatenate(
                [
                    e_all[:, (n * n - 1 - lag) * states : (n * n + 1 - lag) * states]
                    for lag in lags
                ],
                axis=0,
            )
            product = lax.dot_general(left, right, NT, preferred_element_type=jnp.float32)
            where = slice((u + lags[0]) * rows, (u + lags[-1] + 1) * rows)
            if u == 0:
                total[where] = product
            else:
                total[where] += product

    quarter = rows // n
    scale = step_size * step_size
    for b in range(n):
        row = lax.broadcasted_iota(jnp.int32, (quarter, rows), 0) + b * quarter
        column = lax.broadcasted_iota(jnp.int32, (quarter, rows), 1)
        starts = (row == column) & (here_x == here_y) & (row + here_x * rows < size)
        rate = rates[b * quarter : (b + 1) * quarter]
        decay = jnp.broadcast_to(jnp.exp(-step_size * rate), (quarter, rows))
        for t in range(n * n):
            term = scale * total[t * rows + b * quarter : t * rows + (b + 1) * quarter]
            fresh = (jnp.where(starts, 1.0, 0.0) if t == 0 else decay * fresh) - term
            out[t, :, b * rows : (b + 1) * rows] = fresh.astype(jnp.bfloat16)


def convolve(entries, sizes, rates, n, step_size):
    plan, parts = [e[:3] for e in entries], [e[3] for e in entries]
    _, rows, states = parts[0].shape
    copies = sum(part.shape[0] for part in parts)
    return pl.pallas_call(
        functools.partial(convolve_kernel, plan, n, step_size),
        out_shape=jax.ShapeDtypeStruct((n * n, rows // n, states), jnp.bfloat16),
        in_specs=[SMEM, VMEM] + [ANY] * len(parts),
        out_specs=VMEM,
        scratch_shapes=[
            pltpu.VMEM((rows, (n * n + 1) * states), jnp.bfloat16),
            pltpu.VMEM((n * n // 2, rows, 2 * states), jnp.bfloat16),
            pltpu.VMEM((n * n * rows, rows), jnp.float32),
            pltpu.SemaphoreType.DMA((copies,)),
        ],
        compiler_params=pltpu.CompilerParams(vmem_limit_bytes=20 * MIB),
        cost_estimate=pl.CostEstimate(
            flops=n * n * (n * n + 1) * rows * rows * states,
            bytes_accessed=4 * n * n * rows * states,
            transcendentals=0,
        ),
        name="convolve",
    )(sizes, rates, *parts)


def assemble_kernel(n, packets, out):
    quarter, states = packets.shape[1:]
    rows = states // n
    for x in range(n):
        for b in range(n):
            out[x * rows + b * quarter : x * rows + (b + 1) * quarter, :] = jnp.concatenate(
                [packets[x * n + y, :, b * rows : (b + 1) * rows] for y in range(n)], axis=1
            )


def assemble(packets, n):
    states = packets.shape[2]
    return pl.pallas_call(
        functools.partial(assemble_kernel, n),
        out_shape=jax.ShapeDtypeStruct((states, states), jnp.bfloat16),
        in_specs=[VMEM],
        out_specs=VMEM,
        name="assemble",
    )(packets)


def per_device(propagator, rising_op, energies, hyb_particle, hyb_hole, sector_sizes):
    states = propagator.shape[2]
    n = lax.axis_size("tx")
    step_size = 1.0 / (n * n)
    rows = states // n
    here_x = lax.axis_index("tx")
    operator = rising_op[0]

    masked, upward, own_g, *away_g = prepare(
        sector_sizes, propagator[0, 0], operator, n
    )
    below = shifted(upward, "sector", 1)
    above = shifted(masked, "sector", -1)
    crossed_g = {d: ring(away_g[d - 1], "ty", d) for d in (2, 1, 3)}
    columns = jnp.stack([own_g] + [crossed_g[d] for d in range(1, n)])

    own_e, *away_e = energy_blocks(
        sector_sizes, hyb_particle, hyb_hole, above, below, operator, n
    )
    crossed_e = {d: ring(away_e[d - 1], "tx", d) for d in (2, 1, 3)}
    before_g = turned_ring(columns, "tx", 1)
    after_g = turned_ring(columns, "tx", -1)
    far_g = turned_ring(before_g, "tx", 1)

    blocks = [own_e] + [crossed_e[d] for d in range(1, n)]
    halves = [jnp.stack(blocks[: n // 2]), jnp.stack(blocks[n // 2 :])]
    before_e = [turned_ring(half, "ty", 1) for half in halves]
    lines = jnp.stack(blocks)
    after_e = turned_ring(lines, "ty", -1)
    far_e = [turned_ring(half, "ty", 1) for half in before_e]
    entries = [("e", 0, 0, lines), ("e", 1, 0, after_e)]
    for k in range(2):
        entries += [("e", -1, k * n // 2, before_e[k]), ("e", 2, k * n // 2, far_e[k])]
    entries += [
        ("g", step, 0, part)
        for step, part in zip((0, -1, 1, 2), (columns, before_g, after_g, far_g))
    ]
    rates = lax.dynamic_slice_in_dim(energies[0], here_x * rows, rows, 0)[:, None]
    packets = convolve(entries, sector_sizes, rates, n, step_size)
    packets = lax.all_to_all(packets, ("tx", "ty"), 0, 0, tiled=True)
    return assemble(packets, n)[None, None]


def solution(mesh):
    n = round(mesh.shape["tm"] ** 0.5)
    split = Mesh(
        np.asarray(mesh.devices).reshape(n, n, mesh.shape["sector"]), ("tx", "ty", "sector")
    )
    times = ("tx", "ty")
    placed = (
        P("sector", times, None, None),
        P("sector", None, None),
        P("sector", None),
        P(times),
        P(times),
        P("sector"),
    )
    return jax.shard_map(
        per_device,
        mesh=split,
        in_specs=placed,
        out_specs=P("sector", times, None, None),
        check_vma=False,
    )
```

```python
import functools

import jax
import jax.numpy as jnp
import numpy as np
from jax import lax
from jax.experimental import pallas as pl
from jax.experimental.pallas import tpu as pltpu
from jax.sharding import Mesh
from jax.sharding import PartitionSpec as P

MIB = 1024 * 1024
VMEM = pl.BlockSpec(memory_space=pltpu.VMEM)
SMEM = pl.BlockSpec(memory_space=pltpu.SMEM)
ANY = pl.BlockSpec(memory_space=pl.ANY)
NT = (((1,), (1,)), ((), ()))


def shifted(block, axis, distance):
    devices = range(lax.axis_size(axis))
    route = [(i - distance, i) for i in devices if i - distance in devices]
    return lax.ppermute(block, axis, route)


def ring(block, axis, distance):
    n = lax.axis_size(axis)
    return lax.ppermute(block, axis, [(i, (i + distance) % n) for i in range(n)])


def turn_sign():
    return 1 - 2 * lax.rem(lax.axis_index("sector"), 2)


def turned_ring(block, axis, distance):
    n, sectors = lax.axis_size(axis), lax.axis_size("sector")
    route = []
    for i in range(n):
        for s in range(sectors):
            step = distance if s % 2 == 0 else -distance
            route.append((i * sectors + s, (i + step) % n * sectors + s))
    return lax.ppermute(block, (axis, "sector"), route)


def live(shape, size, first_row=0):
    row = lax.broadcasted_iota(jnp.int32, shape, 0) + first_row
    column = lax.broadcasted_iota(jnp.int32, shape, 1)
    return (row < size) & (column < size)


def dot(a, b):
    return jnp.dot(a, b, preferred_element_type=jnp.float32)


def prepare_kernel(sizes, prop, operator, masked, upward, *refs):
    *turned, staged = refs
    n = len(turned)
    rows = turned[0].shape[0]
    inner = prop[...].astype(jnp.float32)
    inner = jnp.where(live(inner.shape, sizes[0]), inner, 0.0).astype(jnp.bfloat16)
    masked[...] = inner
    r = operator[...]
    raised = dot(r, inner).astype(jnp.bfloat16)
    upward[...] = lax.dot_general(raised, r, NT, preferred_element_type=jnp.float32).astype(
        jnp.bfloat16
    )
    staged[...] = inner.T
    here_y = lax.axis_index("ty")
    for d in range(n):
        first = pl.multiple_of(lax.rem(here_y + d, n) * rows, 32)
        turned[d][...] = staged[pl.ds(first, rows), :]


def prepare(sizes, prop, operator, n):
    states = prop.shape[0]
    square = jax.ShapeDtypeStruct((states, states), jnp.bfloat16)
    block = jax.ShapeDtypeStruct((states // n, states), jnp.bfloat16)
    return pl.pallas_call(
        prepare_kernel,
        out_shape=(square,) * 2 + (block,) * n,
        in_specs=[SMEM, VMEM, VMEM],
        out_specs=(VMEM,) * (2 + n),
        scratch_shapes=[pltpu.VMEM((states, states), jnp.bfloat16)],
        cost_estimate=pl.CostEstimate(
            flops=4 * states**3, bytes_accessed=12 * states**2, transcendentals=0
        ),
        name="prepare",
    )(sizes, prop, operator)


def energy_kernel(sizes, particle, hole, *refs):
    sources, (*outs,), copies, lowered, sems = refs[:3], refs[3:-5], refs[-5:-2], refs[-2], refs[-1]
    moves = [
        pltpu.make_async_copy(src, dst, sems.at[i])
        for i, (src, dst) in enumerate(zip(sources, copies))
    ]
    for move in moves:
        move.start()
    n = len(outs)
    rows = outs[0].shape[0]
    here_x = lax.axis_index("tx")
    for move in moves:
        move.wait()
    above, operator, below = copies
    r = operator[...]
    lowered[...] = lax.dot_general(
        r, above[...], (((0,), (0,)), ((), ())), preferred_element_type=jnp.float32
    ).astype(jnp.bfloat16)
    for d in (2, 1, 3, 0):
        first = pl.multiple_of(lax.rem(here_x + d, n) * rows, 32)
        downward = dot(lowered[pl.ds(first, rows), :], r)
        raised = below[pl.ds(first, rows), :].astype(jnp.float32)
        both = particle[0] * raised + hole[0] * downward
        kept = live(both.shape, sizes[0], first)
        outs[d][...] = jnp.where(kept, both, 0.0).astype(jnp.bfloat16)


def energy_blocks(sizes, particle, hole, above, below, operator, n):
    states = above.shape[0]
    block = jax.ShapeDtypeStruct((states // n, states), jnp.bfloat16)
    return pl.pallas_call(
        energy_kernel,
        out_shape=(block,) * n,
        in_specs=[SMEM] * 3 + [ANY] * 3,
        out_specs=(VMEM,) * n,
        scratch_shapes=[pltpu.VMEM((states, states), jnp.bfloat16)] * 4
        + [pltpu.SemaphoreType.DMA((3,))],
        cost_estimate=pl.CostEstimate(
            flops=4 * states**3, bytes_accessed=8 * states**2, transcendentals=0
        ),
        compiler_params=pltpu.CompilerParams(vmem_limit_bytes=16 * MIB),
        name="energy_blocks",
    )(sizes, particle, hole, above, operator, below)


def around(here, offset, n):
    return lax.rem(here + offset + n, n)


def convolve_kernel(plan, n, step_size, sizes, rates, *refs):
    parts = refs[: len(plan)]
    out, e_all, g_all, total, sems = refs[len(plan) :]
    rows, states = g_all.shape[1], e_all.shape[1] // (n * n + 1)
    here_x, here_y, size = lax.axis_index("tx"), lax.axis_index("ty"), sizes[0]
    sign = turn_sign()
    copies_e, copies_g = [], []
    for part, (kind, step, crossed) in zip(parts, plan):
        for k in range(part.shape[0]):
            d = crossed + k
            if kind == "e":
                lag = n * around(here_x, -d, n) + around(here_y, sign * step, n)
                left = pl.multiple_of((n * n - 1 - lag) * states, 128)
                copies_e.append((part.at[k], e_all.at[:, pl.ds(left, states)]))
            else:
                u = n * around(here_x, sign * step, n) + around(here_y, -d, n)
                left = pl.multiple_of(lax.rem(u, 2) * states, 128)
                copies_g.append((part.at[k], g_all.at[u // 2, :, pl.ds(left, states)]))
    moves = [
        pltpu.make_async_copy(src, dst, sems.at[i])
        for i, (src, dst) in enumerate(copies_e + copies_g)
    ]
    for move in moves:
        move.start()
    e_all[:, n * n * states :] = jnp.zeros((rows, states), jnp.bfloat16)
    for move in moves:
        move.wait()

    for u in range(0, n * n, 2):
        right = g_all[u // 2]
        for first in range(0, n * n - u, n):
            lags = range(first, min(first + n, n * n - u))
            left = jnp.concatenate(
                [
                    e_all[:, (n * n - 1 - lag) * states : (n * n + 1 - lag) * states]
                    for lag in lags
                ],
                axis=0,
            )
            product = lax.dot_general(left, right, NT, preferred_element_type=jnp.float32)
            where = slice((u + lags[0]) * rows, (u + lags[-1] + 1) * rows)
            if u == 0:
                total[where] = product
            else:
                total[where] += product

    quarter = rows // n
    scale = step_size * step_size
    for b in range(n):
        row = lax.broadcasted_iota(jnp.int32, (quarter, rows), 0) + b * quarter
        column = lax.broadcasted_iota(jnp.int32, (quarter, rows), 1)
        starts = (row == column) & (here_x == here_y) & (row + here_x * rows < size)
        rate = rates[b * quarter : (b + 1) * quarter]
        decay = jnp.broadcast_to(jnp.exp(-step_size * rate), (quarter, rows))
        for t in range(n * n):
            term = scale * total[t * rows + b * quarter : t * rows + (b + 1) * quarter]
            fresh = (jnp.where(starts, 1.0, 0.0) if t == 0 else decay * fresh) - term
            out[t, :, b * rows : (b + 1) * rows] = fresh.astype(jnp.bfloat16)


def convolve(entries, sizes, rates, n, step_size):
    plan, parts = [e[:3] for e in entries], [e[3] for e in entries]
    _, rows, states = parts[0].shape
    copies = sum(part.shape[0] for part in parts)
    return pl.pallas_call(
        functools.partial(convolve_kernel, plan, n, step_size),
        out_shape=jax.ShapeDtypeStruct((n * n, rows // n, states), jnp.bfloat16),
        in_specs=[SMEM, VMEM] + [ANY] * len(parts),
        out_specs=VMEM,
        scratch_shapes=[
            pltpu.VMEM((rows, (n * n + 1) * states), jnp.bfloat16),
            pltpu.VMEM((n * n // 2, rows, 2 * states), jnp.bfloat16),
            pltpu.VMEM((n * n * rows, rows), jnp.float32),
            pltpu.SemaphoreType.DMA((copies,)),
        ],
        compiler_params=pltpu.CompilerParams(vmem_limit_bytes=20 * MIB),
        cost_estimate=pl.CostEstimate(
            flops=n * n * (n * n + 1) * rows * rows * states,
            bytes_accessed=4 * n * n * rows * states,
            transcendentals=0,
        ),
        name="convolve",
    )(sizes, rates, *parts)


def assemble_kernel(n, packets, out):
    quarter, states = packets.shape[1:]
    rows = states // n
    for x in range(n):
        for b in range(n):
            out[x * rows + b * quarter : x * rows + (b + 1) * quarter, :] = jnp.concatenate(
                [packets[x * n + y, :, b * rows : (b + 1) * rows] for y in range(n)], axis=1
            )


def assemble(packets, n):
    states = packets.shape[2]
    return pl.pallas_call(
        functools.partial(assemble_kernel, n),
        out_shape=jax.ShapeDtypeStruct((states, states), jnp.bfloat16),
        in_specs=[VMEM],
        out_specs=VMEM,
        name="assemble",
    )(packets)


def per_device(propagator, rising_op, energies, hyb_particle, hyb_hole, sector_sizes):
    states = propagator.shape[2]
    n = lax.axis_size("tx")
    step_size = 1.0 / (n * n)
    rows = states // n
    here_x = lax.axis_index("tx")
    operator = rising_op[0]

    masked, upward, own_g, *away_g = prepare(
        sector_sizes, propagator[0, 0], operator, n
    )
    below = shifted(upward, "sector", 1)
    above = shifted(masked, "sector", -1)
    crossed_g = {d: ring(away_g[d - 1], "ty", d) for d in (2, 1, 3)}
    own_e, *away_e = energy_blocks(
        sector_sizes, hyb_particle, hyb_hole, above, below, operator, n
    )
    crossed_e = {d: ring(away_e[d - 1], "tx", d) for d in (2, 1, 3)}
    entries = []
    for kind, axis, own, crossed in (("e", "ty", own_e, crossed_e), ("g", "tx", own_g, crossed_g)):
        blocks = [own] + [crossed[d] for d in range(1, n)]
        whole = jnp.stack(blocks)
        after = turned_ring(whole, axis, -1)
        entries += [(kind, 0, 0, whole), (kind, 1, 0, after)]
        for k in (0, n // 2):
            before = turned_ring(jnp.stack(blocks[k : k + n // 2]), axis, 1)
            far = turned_ring(before, axis, 1)
            entries += [(kind, -1, k, before), (kind, 2, k, far)]
    rates = lax.dynamic_slice_in_dim(energies[0], here_x * rows, rows, 0)[:, None]
    packets = convolve(entries, sector_sizes, rates, n, step_size)
    packets = lax.all_to_all(packets, ("tx", "ty"), 0, 0, tiled=True)
    return assemble(packets, n)[None, None]


def solution(mesh):
    n = round(mesh.shape["tm"] ** 0.5)
    split = Mesh(
        np.asarray(mesh.devices).reshape(n, n, mesh.shape["sector"]), ("tx", "ty", "sector")
    )
    times = ("tx", "ty")
    placed = (
        P("sector", times, None, None),
        P("sector", None, None),
        P("sector", None),
        P(times),
        P(times),
        P("sector"),
    )
    return jax.shard_map(
        per_device,
        mesh=split,
        in_specs=placed,
        out_specs=P("sector", times, None, None),
        check_vma=False,
    )
```

```python
import functools

import jax
import jax.numpy as jnp
import numpy as np
from jax import lax
from jax.experimental import pallas as pl
from jax.experimental.pallas import tpu as pltpu
from jax.sharding import Mesh
from jax.sharding import PartitionSpec as P

MIB = 1024 * 1024
VMEM = pl.BlockSpec(memory_space=pltpu.VMEM)
SMEM = pl.BlockSpec(memory_space=pltpu.SMEM)
ANY = pl.BlockSpec(memory_space=pl.ANY)
NT = (((1,), (1,)), ((), ()))


def shifted(block, axis, distance):
    devices = range(lax.axis_size(axis))
    route = [(i - distance, i) for i in devices if i - distance in devices]
    return lax.ppermute(block, axis, route)


def ring(block, axis, distance):
    n = lax.axis_size(axis)
    return lax.ppermute(block, axis, [(i, (i + distance) % n) for i in range(n)])


def turn_sign():
    return 1 - 2 * lax.rem(lax.axis_index("sector"), 2)


def turned_ring(block, axis, distance):
    n, sectors = lax.axis_size(axis), lax.axis_size("sector")
    route = []
    for i in range(n):
        for s in range(sectors):
            step = distance if s % 2 == 0 else -distance
            route.append((i * sectors + s, (i + step) % n * sectors + s))
    return lax.ppermute(block, (axis, "sector"), route)


def ring_gather(block, axis):
    before = turned_ring(block, axis, 1)
    after = turned_ring(block, axis, -1)
    return [(0, block), (-1, before), (1, after), (2, turned_ring(before, axis, 1))]


def live(shape, size, first_row=0):
    row = lax.broadcasted_iota(jnp.int32, shape, 0) + first_row
    column = lax.broadcasted_iota(jnp.int32, shape, 1)
    return (row < size) & (column < size)


def dot(a, b):
    return jnp.dot(a, b, preferred_element_type=jnp.float32)


def raise_kernel(sizes, prop, operator, masked, upward):
    inner = prop[...].astype(jnp.float32)
    inner = jnp.where(live(inner.shape, sizes[0]), inner, 0.0).astype(jnp.bfloat16)
    masked[...] = inner
    r = operator[...]
    raised = dot(r, inner).astype(jnp.bfloat16)
    upward[...] = lax.dot_general(raised, r, NT, preferred_element_type=jnp.float32).astype(
        jnp.bfloat16
    )


def raise_terms(sizes, prop, operator):
    states = prop.shape[0]
    square = jax.ShapeDtypeStruct((states, states), jnp.bfloat16)
    return pl.pallas_call(
        raise_kernel,
        out_shape=(square,) * 2,
        in_specs=[SMEM, VMEM, VMEM],
        out_specs=(VMEM,) * 2,
        cost_estimate=pl.CostEstimate(
            flops=4 * states**3, bytes_accessed=8 * states**2, transcendentals=0
        ),
        name="raise_terms",
    )(sizes, prop, operator)


def turn_kernel(masked, *refs):
    *turned, staged, copied, sem = refs
    move = pltpu.make_async_copy(masked, copied, sem.at[0])
    move.start()
    move.wait()
    n = len(turned)
    rows = turned[0].shape[0]
    staged[...] = copied[...].T
    here_y = lax.axis_index("ty")
    for d in range(n):
        first = pl.multiple_of(lax.rem(here_y + d, n) * rows, 32)
        turned[d][...] = staged[pl.ds(first, rows), :]


def turn_blocks(masked, n):
    states = masked.shape[0]
    block = jax.ShapeDtypeStruct((states // n, states), jnp.bfloat16)
    return pl.pallas_call(
        turn_kernel,
        out_shape=(block,) * n,
        in_specs=[ANY],
        out_specs=(VMEM,) * n,
        scratch_shapes=[pltpu.VMEM((states, states), jnp.bfloat16)] * 2
        + [pltpu.SemaphoreType.DMA((1,))],
        cost_estimate=pl.CostEstimate(flops=0, bytes_accessed=4 * states**2, transcendentals=0),
        compiler_params=pltpu.CompilerParams(vmem_limit_bytes=16 * MIB),
        name="turn_blocks",
    )(masked)


def energy_kernel(sizes, particle, hole, *refs):
    sources, (*outs,), copies, lowered, sems = refs[:3], refs[3:-5], refs[-5:-2], refs[-2], refs[-1]
    moves = [
        pltpu.make_async_copy(src, dst, sems.at[i])
        for i, (src, dst) in enumerate(zip(sources, copies))
    ]
    for move in moves:
        move.start()
    n = len(outs)
    rows = outs[0].shape[0]
    here_x = lax.axis_index("tx")
    for move in moves:
        move.wait()
    above, operator, below = copies
    r = operator[...]
    lowered[...] = lax.dot_general(
        r, above[...], (((0,), (0,)), ((), ())), preferred_element_type=jnp.float32
    ).astype(jnp.bfloat16)
    for d in (2, 1, 3, 0):
        first = pl.multiple_of(lax.rem(here_x + d, n) * rows, 32)
        downward = dot(lowered[pl.ds(first, rows), :], r)
        raised = below[pl.ds(first, rows), :].astype(jnp.float32)
        both = particle[0] * raised + hole[0] * downward
        kept = live(both.shape, sizes[0], first)
        outs[d][...] = jnp.where(kept, both, 0.0).astype(jnp.bfloat16)


def energy_blocks(sizes, particle, hole, above, below, operator, n):
    states = above.shape[0]
    block = jax.ShapeDtypeStruct((states // n, states), jnp.bfloat16)
    return pl.pallas_call(
        energy_kernel,
        out_shape=(block,) * n,
        in_specs=[SMEM] * 3 + [ANY] * 3,
        out_specs=(VMEM,) * n,
        scratch_shapes=[pltpu.VMEM((states, states), jnp.bfloat16)] * 4
        + [pltpu.SemaphoreType.DMA((3,))],
        cost_estimate=pl.CostEstimate(
            flops=4 * states**3, bytes_accessed=8 * states**2, transcendentals=0
        ),
        compiler_params=pltpu.CompilerParams(vmem_limit_bytes=16 * MIB),
        name="energy_blocks",
    )(sizes, particle, hole, above, operator, below)


def around(here, offset, n):
    return lax.rem(here + offset + n, n)


def convolve_kernel(plan, n, step_size, sizes, rates, *refs):
    parts = refs[: len(plan)]
    out, e_all, g_all, total, sems = refs[len(plan) :]
    rows, states = g_all.shape[1], e_all.shape[1] // (n * n + 1)
    here_x, here_y, size = lax.axis_index("tx"), lax.axis_index("ty"), sizes[0]
    sign = turn_sign()
    copies_e, copies_g = [], []
    for part, (kind, step) in zip(parts, plan):
        for d in range(n):
            if kind == "e":
                lag = n * around(here_x, -d, n) + around(here_y, sign * step, n)
                left = pl.multiple_of((n * n - 1 - lag) * states, 128)
                copies_e.append((part.at[d], e_all.at[:, pl.ds(left, states)]))
            else:
                u = n * around(here_x, sign * step, n) + around(here_y, -d, n)
                left = pl.multiple_of(lax.rem(u, 2) * states, 128)
                copies_g.append((part.at[d], g_all.at[u // 2, :, pl.ds(left, states)]))
    moves = [
        pltpu.make_async_copy(src, dst, sems.at[i])
        for i, (src, dst) in enumerate(copies_e + copies_g)
    ]
    for move in moves:
        move.start()
    e_all[:, n * n * states :] = jnp.zeros((rows, states), jnp.bfloat16)
    for move in moves:
        move.wait()

    for u in range(0, n * n, 2):
        right = g_all[u // 2]
        for first in range(0, n * n - u, n):
            lags = range(first, min(first + n, n * n - u))
            left = jnp.concatenate(
                [
                    e_all[:, (n * n - 1 - lag) * states : (n * n + 1 - lag) * states]
                    for lag in lags
                ],
                axis=0,
            )
            product = lax.dot_general(left, right, NT, preferred_element_type=jnp.float32)
            where = slice((u + lags[0]) * rows, (u + lags[-1] + 1) * rows)
            if u == 0:
                total[where] = product
            else:
                total[where] += product

    quarter = rows // n
    scale = step_size * step_size
    for b in range(n):
        row = lax.broadcasted_iota(jnp.int32, (quarter, rows), 0) + b * quarter
        column = lax.broadcasted_iota(jnp.int32, (quarter, rows), 1)
        starts = (row == column) & (here_x == here_y) & (row + here_x * rows < size)
        rate = rates[b * quarter : (b + 1) * quarter]
        decay = jnp.broadcast_to(jnp.exp(-step_size * rate), (quarter, rows))
        for t in range(n * n):
            term = scale * total[t * rows + b * quarter : t * rows + (b + 1) * quarter]
            fresh = (jnp.where(starts, 1.0, 0.0) if t == 0 else decay * fresh) - term
            out[t, :, b * rows : (b + 1) * rows] = fresh.astype(jnp.bfloat16)


def convolve(entries, sizes, rates, n, step_size):
    plan, parts = [e[:2] for e in entries], [e[2] for e in entries]
    _, rows, states = parts[0].shape
    copies = n * len(parts)
    return pl.pallas_call(
        functools.partial(convolve_kernel, plan, n, step_size),
        out_shape=jax.ShapeDtypeStruct((n * n, rows // n, states), jnp.bfloat16),
        in_specs=[SMEM, VMEM] + [ANY] * len(parts),
        out_specs=VMEM,
        scratch_shapes=[
            pltpu.VMEM((rows, (n * n + 1) * states), jnp.bfloat16),
            pltpu.VMEM((n * n // 2, rows, 2 * states), jnp.bfloat16),
            pltpu.VMEM((n * n * rows, rows), jnp.float32),
            pltpu.SemaphoreType.DMA((copies,)),
        ],
        compiler_params=pltpu.CompilerParams(vmem_limit_bytes=20 * MIB),
        cost_estimate=pl.CostEstimate(
            flops=n * n * (n * n + 1) * rows * rows * states,
            bytes_accessed=4 * n * n * rows * states,
            transcendentals=0,
        ),
        name="convolve",
    )(sizes, rates, *parts)


def assemble_kernel(n, packets, out):
    quarter, states = packets.shape[1:]
    rows = states // n
    for x in range(n):
        for b in range(n):
            out[x * rows + b * quarter : x * rows + (b + 1) * quarter, :] = jnp.concatenate(
                [packets[x * n + y, :, b * rows : (b + 1) * rows] for y in range(n)], axis=1
            )


def assemble(packets, n):
    states = packets.shape[2]
    return pl.pallas_call(
        functools.partial(assemble_kernel, n),
        out_shape=jax.ShapeDtypeStruct((states, states), jnp.bfloat16),
        in_specs=[VMEM],
        out_specs=VMEM,
        name="assemble",
    )(packets)


def per_device(propagator, rising_op, energies, hyb_particle, hyb_hole, sector_sizes):
    states = propagator.shape[2]
    n = lax.axis_size("tx")
    step_size = 1.0 / (n * n)
    rows = states // n
    here_x = lax.axis_index("tx")
    operator = rising_op[0]

    masked, upward = raise_terms(sector_sizes, propagator[0, 0], operator)
    below = shifted(upward, "sector", 1)
    above = shifted(masked, "sector", -1)
    own_g, *away_g = turn_blocks(masked, n)
    crossed_g = {d: ring(away_g[d - 1], "ty", d) for d in (2, 1, 3)}
    columns = jnp.stack([own_g] + [crossed_g[d] for d in range(1, n)])

    own_e, *away_e = energy_blocks(
        sector_sizes, hyb_particle, hyb_hole, above, below, operator, n
    )
    crossed_e = {d: ring(away_e[d - 1], "tx", d) for d in (2, 1, 3)}
    lines = jnp.stack([own_e] + [crossed_e[d] for d in range(1, n)])

    entries = [("g", step, part) for step, part in ring_gather(columns, "tx")]
    entries = [("e", step, part) for step, part in ring_gather(lines, "ty")] + entries
    rates = lax.dynamic_slice_in_dim(energies[0], here_x * rows, rows, 0)[:, None]
    packets = convolve(entries, sector_sizes, rates, n, step_size)
    packets = lax.all_to_all(packets, ("tx", "ty"), 0, 0, tiled=True)
    return assemble(packets, n)[None, None]


def solution(mesh):
    n = round(mesh.shape["tm"] ** 0.5)
    split = Mesh(
        np.asarray(mesh.devices).reshape(n, n, mesh.shape["sector"]), ("tx", "ty", "sector")
    )
    times = ("tx", "ty")
    placed = (
        P("sector", times, None, None),
        P("sector", None, None),
        P("sector", None),
        P(times),
        P(times),
        P("sector"),
    )
    return jax.shard_map(
        per_device,
        mesh=split,
        in_specs=placed,
        out_specs=P("sector", times, None, None),
        check_vma=False,
    )
```

```python
import functools

import jax
import jax.numpy as jnp
import numpy as np
from jax import lax
from jax.experimental import pallas as pl
from jax.experimental.pallas import tpu as pltpu
from jax.sharding import Mesh
from jax.sharding import PartitionSpec as P

MIB = 1024 * 1024
VMEM = pl.BlockSpec(memory_space=pltpu.VMEM)
SMEM = pl.BlockSpec(memory_space=pltpu.SMEM)
ANY = pl.BlockSpec(memory_space=pl.ANY)
NT = (((1,), (1,)), ((), ()))


def shifted(block, axis, distance):
    devices = range(lax.axis_size(axis))
    route = [(i - distance, i) for i in devices if i - distance in devices]
    return lax.ppermute(block, axis, route)


def ring(block, axis, distance):
    n = lax.axis_size(axis)
    return lax.ppermute(block, axis, [(i, (i + distance) % n) for i in range(n)])


def turn_sign():
    return 1 - 2 * lax.rem(lax.axis_index("sector"), 2)


def turned_ring(block, axis, distance):
    n, sectors = lax.axis_size(axis), lax.axis_size("sector")
    route = []
    for i in range(n):
        for s in range(sectors):
            step = distance if s % 2 == 0 else -distance
            route.append((i * sectors + s, (i + step) % n * sectors + s))
    return lax.ppermute(block, (axis, "sector"), route)


def ring_gather(block, axis):
    before = turned_ring(block, axis, 1)
    after = turned_ring(block, axis, -1)
    return [(0, block), (-1, before), (1, after), (2, turned_ring(before, axis, 1))]


def live(shape, size, first_row=0):
    row = lax.broadcasted_iota(jnp.int32, shape, 0) + first_row
    column = lax.broadcasted_iota(jnp.int32, shape, 1)
    return (row < size) & (column < size)


def dot(a, b):
    return jnp.dot(a, b, preferred_element_type=jnp.float32)


def prepare_kernel(sizes, prop, operator, masked, upward, *refs):
    *turned, staged = refs
    n = len(turned)
    rows = turned[0].shape[0]
    inner = prop[...].astype(jnp.float32)
    inner = jnp.where(live(inner.shape, sizes[0]), inner, 0.0).astype(jnp.bfloat16)
    masked[...] = inner
    r = operator[...]
    raised = dot(r, inner).astype(jnp.bfloat16)
    upward[...] = lax.dot_general(raised, r, NT, preferred_element_type=jnp.float32).astype(
        jnp.bfloat16
    )
    staged[...] = inner.T
    here_y = lax.axis_index("ty")
    for d in range(n):
        first = pl.multiple_of(lax.rem(here_y + d, n) * rows, 32)
        turned[d][...] = staged[pl.ds(first, rows), :]


def prepare(sizes, prop, operator, n):
    states = prop.shape[0]
    square = jax.ShapeDtypeStruct((states, states), jnp.bfloat16)
    block = jax.ShapeDtypeStruct((states // n, states), jnp.bfloat16)
    return pl.pallas_call(
        prepare_kernel,
        out_shape=(square,) * 2 + (block,) * n,
        in_specs=[SMEM, VMEM, VMEM],
        out_specs=(VMEM,) * (2 + n),
        scratch_shapes=[pltpu.VMEM((states, states), jnp.bfloat16)],
        cost_estimate=pl.CostEstimate(
            flops=4 * states**3, bytes_accessed=12 * states**2, transcendentals=0
        ),
        name="prepare",
    )(sizes, prop, operator)


def energy_kernel(sizes, particle, hole, *refs):
    sources, (*outs,), copies, lowered, sems = refs[:3], refs[3:-5], refs[-5:-2], refs[-2], refs[-1]
    moves = [
        pltpu.make_async_copy(src, dst, sems.at[i])
        for i, (src, dst) in enumerate(zip(sources, copies))
    ]
    for move in moves:
        move.start()
    n = len(outs)
    rows = outs[0].shape[0]
    here_x = lax.axis_index("tx")
    for move in moves:
        move.wait()
    above, operator, below = copies
    r = operator[...]
    lowered[...] = lax.dot_general(
        r, above[...], (((0,), (0,)), ((), ())), preferred_element_type=jnp.float32
    ).astype(jnp.bfloat16)
    for d in (2, 1, 3, 0):
        first = pl.multiple_of(lax.rem(here_x + d, n) * rows, 32)
        downward = dot(lowered[pl.ds(first, rows), :], r)
        raised = below[pl.ds(first, rows), :].astype(jnp.float32)
        both = particle[0] * raised + hole[0] * downward
        kept = live(both.shape, sizes[0], first)
        outs[d][...] = jnp.where(kept, both, 0.0).astype(jnp.bfloat16)


def energy_blocks(sizes, particle, hole, above, below, operator, n):
    states = above.shape[0]
    block = jax.ShapeDtypeStruct((states // n, states), jnp.bfloat16)
    return pl.pallas_call(
        energy_kernel,
        out_shape=(block,) * n,
        in_specs=[SMEM] * 3 + [ANY] * 3,
        out_specs=(VMEM,) * n,
        scratch_shapes=[pltpu.VMEM((states, states), jnp.bfloat16)] * 4
        + [pltpu.SemaphoreType.DMA((3,))],
        cost_estimate=pl.CostEstimate(
            flops=4 * states**3, bytes_accessed=8 * states**2, transcendentals=0
        ),
        compiler_params=pltpu.CompilerParams(vmem_limit_bytes=16 * MIB),
        name="energy_blocks",
    )(sizes, particle, hole, above, operator, below)


def around(here, offset, n):
    return lax.rem(here + offset + n, n)


def convolve_kernel(plan, n, step_size, sizes, rates, *refs):
    parts = refs[: len(plan)]
    out, e_all, g_all, total, sems = refs[len(plan) :]
    rows, states = g_all.shape[1], e_all.shape[1] // (n * n + 1)
    here_x, here_y, size = lax.axis_index("tx"), lax.axis_index("ty"), sizes[0]
    sign = turn_sign()
    copies_e, copies_g = [], []
    for part, (kind, step) in zip(parts, plan):
        for d in range(n):
            if kind == "e":
                lag = n * around(here_x, -d, n) + around(here_y, sign * step, n)
                left = pl.multiple_of((n * n - 1 - lag) * states, 128)
                copies_e.append((part.at[d], e_all.at[:, pl.ds(left, states)]))
            else:
                u = n * around(here_x, sign * step, n) + around(here_y, -d, n)
                left = pl.multiple_of(lax.rem(u, 2) * states, 128)
                copies_g.append((part.at[d], g_all.at[u // 2, :, pl.ds(left, states)]))
    moves = [
        pltpu.make_async_copy(src, dst, sems.at[i])
        for i, (src, dst) in enumerate(copies_e + copies_g)
    ]
    for move in moves:
        move.start()
    e_all[:, n * n * states :] = jnp.zeros((rows, states), jnp.bfloat16)
    for move in moves:
        move.wait()

    for u in range(0, n * n, 2):
        right = g_all[u // 2]
        for first in range(0, n * n - u, n):
            lags = range(first, min(first + n, n * n - u))
            left = jnp.concatenate(
                [
                    e_all[:, (n * n - 1 - lag) * states : (n * n + 1 - lag) * states]
                    for lag in lags
                ],
                axis=0,
            )
            product = lax.dot_general(left, right, NT, preferred_element_type=jnp.float32)
            where = slice((u + lags[0]) * rows, (u + lags[-1] + 1) * rows)
            if u == 0:
                total[where] = product
            else:
                total[where] += product

    quarter = rows // n
    scale = step_size * step_size
    for b in range(n):
        row = lax.broadcasted_iota(jnp.int32, (quarter, rows), 0) + b * quarter
        column = lax.broadcasted_iota(jnp.int32, (quarter, rows), 1)
        starts = (row == column) & (here_x == here_y) & (row + here_x * rows < size)
        rate = rates[b * quarter : (b + 1) * quarter]
        decay = jnp.broadcast_to(jnp.exp(-step_size * rate), (quarter, rows))
        for t in range(n * n):
            term = scale * total[t * rows + b * quarter : t * rows + (b + 1) * quarter]
            fresh = (jnp.where(starts, 1.0, 0.0) if t == 0 else decay * fresh) - term
            out[t, :, b * rows : (b + 1) * rows] = fresh.astype(jnp.bfloat16)


def convolve(entries, sizes, rates, n, step_size):
    plan, parts = [e[:2] for e in entries], [e[2] for e in entries]
    _, rows, states = parts[0].shape
    copies = n * len(parts)
    return pl.pallas_call(
        functools.partial(convolve_kernel, plan, n, step_size),
        out_shape=jax.ShapeDtypeStruct((n * n, rows // n, states), jnp.bfloat16),
        in_specs=[SMEM, VMEM] + [ANY] * len(parts),
        out_specs=VMEM,
        scratch_shapes=[
            pltpu.VMEM((rows, (n * n + 1) * states), jnp.bfloat16),
            pltpu.VMEM((n * n // 2, rows, 2 * states), jnp.bfloat16),
            pltpu.VMEM((n * n * rows, rows), jnp.float32),
            pltpu.SemaphoreType.DMA((copies,)),
        ],
        compiler_params=pltpu.CompilerParams(vmem_limit_bytes=20 * MIB),
        cost_estimate=pl.CostEstimate(
            flops=n * n * (n * n + 1) * rows * rows * states,
            bytes_accessed=4 * n * n * rows * states,
            transcendentals=0,
        ),
        name="convolve",
    )(sizes, rates, *parts)


def assemble_kernel(n, arrived, out, packets, sem):
    move = pltpu.make_async_copy(arrived, packets, sem.at[0])
    move.start()
    move.wait()
    quarter, states = packets.shape[1:]
    rows = states // n
    for x in range(n):
        for b in range(n):
            out[x * rows + b * quarter : x * rows + (b + 1) * quarter, :] = jnp.concatenate(
                [packets[x * n + y, :, b * rows : (b + 1) * rows] for y in range(n)], axis=1
            )


def assemble(packets, n):
    states = packets.shape[2]
    return pl.pallas_call(
        functools.partial(assemble_kernel, n),
        out_shape=jax.ShapeDtypeStruct((states, states), jnp.bfloat16),
        in_specs=[ANY],
        out_specs=VMEM,
        scratch_shapes=[
            pltpu.VMEM(packets.shape, jnp.bfloat16),
            pltpu.SemaphoreType.DMA((1,)),
        ],
        compiler_params=pltpu.CompilerParams(vmem_limit_bytes=16 * MIB),
        name="assemble",
    )(packets)


def per_device(propagator, rising_op, energies, hyb_particle, hyb_hole, sector_sizes):
    states = propagator.shape[2]
    n = lax.axis_size("tx")
    step_size = 1.0 / (n * n)
    rows = states // n
    here_x = lax.axis_index("tx")
    operator = rising_op[0]

    masked, upward, own_g, *away_g = prepare(
        sector_sizes, propagator[0, 0], operator, n
    )
    below = shifted(upward, "sector", 1)
    above = shifted(masked, "sector", -1)
    crossed_g = {d: ring(away_g[d - 1], "ty", d) for d in (2, 1, 3)}
    columns = jnp.stack([own_g] + [crossed_g[d] for d in range(1, n)])

    own_e, *away_e = energy_blocks(
        sector_sizes, hyb_particle, hyb_hole, above, below, operator, n
    )
    crossed_e = {d: ring(away_e[d - 1], "tx", d) for d in (2, 1, 3)}
    lines = jnp.stack([own_e] + [crossed_e[d] for d in range(1, n)])

    entries = [("g", step, part) for step, part in ring_gather(columns, "tx")]
    entries = [("e", step, part) for step, part in ring_gather(lines, "ty")] + entries
    rates = lax.dynamic_slice_in_dim(energies[0], here_x * rows, rows, 0)[:, None]
    packets = convolve(entries, sector_sizes, rates, n, step_size)
    packets = lax.all_to_all(packets, ("tx", "ty"), 0, 0, tiled=True)
    return assemble(packets, n)[None, None]


def solution(mesh):
    n = round(mesh.shape["tm"] ** 0.5)
    split = Mesh(
        np.asarray(mesh.devices).reshape(n, n, mesh.shape["sector"]), ("tx", "ty", "sector")
    )
    times = ("tx", "ty")
    placed = (
        P("sector", times, None, None),
        P("sector", None, None),
        P("sector", None),
        P(times),
        P(times),
        P("sector"),
    )
    return jax.shard_map(
        per_device,
        mesh=split,
        in_specs=placed,
        out_specs=P("sector", times, None, None),
        check_vma=False,
    )
```
